32 devices in a mesh: dp: 8 (over y, x, core), fsdp: 4 (over z).
Axes of the slice: x: 2, y: 2, z: 4, core: 2. Of those that a mesh axis runs over, the one named last changes fastest.
Arguments:
- inputs: bfloat16 [32, 8, 12, 6, 6, 256], P(('dp', 'fsdp')), may hold values from -6 to 6
- cotangent: bfloat16 [32, 8, 12, 6, 6, 256], P(('dp', 'fsdp')), may hold values from -6 to 6
- lengths: int32 [32], P(('dp', 'fsdp')), may hold values from 2 to 8
- face_table: int32 [12, 4], replicated, may hold values from 0 to 11
- w_first: float32 [2304, 256], P('fsdp'), may hold values from -0.125 to 0.125
- w_second: float32 [2304, 256], P('fsdp'), may hold values from -0.125 to 0.125
- w_skip: float32 [256, 256], P('fsdp'), may hold values from -0.375 to 0.375
- mom_first: float32 [2304, 256], P('fsdp'), may hold values from -64 to 64
- sq_first: float32 [2304, 256], P('fsdp'), may hold values from 12.16512 to 48.66048
- mom_second: float32 [2304, 256], P('fsdp'), may hold values from -64 to 64
- sq_second: float32 [2304, 256], P('fsdp'), may hold values from 12.16512 to 48.66048
- mom_skip: float32 [256, 256], P('fsdp'), may hold values from -160 to 160
- sq_skip: float32 [256, 256], P('fsdp'), may hold values from 68.56704 to 276.48
Outputs:
- output: bfloat16 [32, 8, 12, 6, 6, 256], P(('dp', 'fsdp'))
- grad_inputs: float32 [32, 8, 12, 6, 6, 256], P(('dp', 'fsdp'))
- new_first: float32 [2304, 256], P('fsdp')
- new_mom_first: float32 [2304, 256], P('fsdp')
- new_sq_first: float32 [2304, 256], P('fsdp')
- new_second: float32 [2304, 256], P('fsdp')
- new_mom_second: float32 [2304, 256], P('fsdp')
- new_sq_second: float32 [2304, 256], P('fsdp')
- new_skip: float32 [256, 256], P('fsdp')
- new_mom_skip: float32 [256, 256], P('fsdp')
- new_sq_skip: float32 [256, 256], P('fsdp')
The draws below stay inside these ranges and needn't reach their ends.
All inputs are finite; a program needn't handle non-finite values.
Results may differ from the reference program's by a relative error of at most 0.019.
Values may be sent and summed in bfloat16 or wider, within the bound.
No kernel may reach another device: no remote copies, remote signals or barrier semaphores. Data moves between devices by JAX's collectives and lax.ppermute only.
A program may use at most 256 MiB of HBM per device.

```python
import math
import jax
import jax.numpy as jnp
from jax import lax

C = 256
FACES = 12
FS = 6
ROLL = 8
STEP_COUNT = 10
SAMPLES = 32
PIXELS = 110592


def place_ends(array, own_key, smallest, top_value):
    longest = array.shape.index(max(array.shape))
    spots = []
    for shift in (0, 1):
        where = [jax.random.randint(jax.random.fold_in(own_key, axis), (), 0, length) for axis, length in enumerate(array.shape)]
        where[longest] = (where[longest] + shift) % array.shape[longest]
        spots.append(tuple(where))
    return array.at[spots[0]].set(smallest).at[spots[1]].set(top_value)


def levels(stream_key, shape, shards, low, high):
    loudness = 1.0
    for dim, parts in shards:
        heights = jax.random.uniform(jax.random.fold_in(jax.random.fold_in(stream_key, 6), dim), (parts,), jnp.float32, low / len(shards), high / len(shards))
        loudness = loudness * jnp.repeat(jnp.exp(heights), shape[dim] // parts).reshape((-1,) + (1,) * (len(shape) - 1 - dim))
    return loudness


def centred(rng, extent, deviation, limit, shards=(), held_as=jnp.bfloat16):
    array = deviation * jax.random.normal(rng, extent, jnp.float32)
    if shards:
        array = array * levels(rng, extent, shards, -0.22, 0.18)
    return jnp.clip(array, -limit, limit).astype(held_as)


def setup_inputs(seed: int = 0) -> dict:
    arg_keys = jax.random.split(jax.random.key(seed), 14)
    return {
        "inputs": centred(arg_keys[0], (SAMPLES, ROLL, FACES, FS, FS, C), 1.0, 6.0, ((0, 32),)),
        "cotangent": centred(arg_keys[1], (SAMPLES, ROLL, FACES, FS, FS, C), 1.0, 6.0, ((0, 32),)),
        "lengths": place_ends(jax.random.randint(arg_keys[2], (SAMPLES,), 2, ROLL + 1), jax.random.fold_in(arg_keys[2], 1), 2, ROLL).astype(jnp.int32),
        "face_table": place_ends(jax.random.randint(arg_keys[3], (FACES, 4), 0, FACES), jax.random.fold_in(arg_keys[3], 1), 0, FACES - 1).astype(jnp.int32),
        "w_first": centred(arg_keys[4], (9 * C, C), (9 * C) ** -0.5, 0.125, ((0, 4),), jnp.float32),
        "w_second": centred(arg_keys[5], (9 * C, C), (9 * C) ** -0.5, 0.125, ((0, 4),), jnp.float32),
        "w_skip": centred(arg_keys[6], (C, C), C ** -0.5, 0.375, ((0, 4),), jnp.float32),
        "mom_first": centred(arg_keys[7], (9 * C, C), (0.037 * PIXELS ** 0.5), 64.0, ((0, 4),), jnp.float32),
        "sq_first": jnp.clip(jnp.exp(math.log(48.66048) - 1.3862944 * jax.random.uniform(arg_keys[8], (9 * C, C), jnp.float32) ** levels(arg_keys[8], (9 * C, C), ((0, 4),), -0.2, 0.2)), 12.16512, 48.66048),
        "mom_second": centred(arg_keys[9], (9 * C, C), (0.037 * PIXELS ** 0.5), 64.0, ((0, 4),), jnp.float32),
        "sq_second": jnp.clip(jnp.exp(math.log(48.66048) - 1.3862944 * jax.random.uniform(arg_keys[10], (9 * C, C), jnp.float32) ** levels(arg_keys[10], (9 * C, C), ((0, 4),), -0.2, 0.2)), 12.16512, 48.66048),
        "mom_skip": centred(arg_keys[11], (C, C), (0.088 * PIXELS ** 0.5), 160.0, ((0, 4),), jnp.float32),
        "sq_skip": jnp.clip(jnp.exp(math.log(276.48) - 1.3943266 * jax.random.uniform(arg_keys[12], (C, C), jnp.float32) ** levels(arg_keys[12], (C, C), ((0, 4),), -0.2, 0.2)), 68.56704, 276.48),
    }


@jax.custom_vjp
def low(v):
    return lax.optimization_barrier(v.astype(jnp.bfloat16)).astype(jnp.float32)

@jax.custom_vjp
def low_back(v):
    return v

def low_keep(v):
    return (low(v), None)

def low_pass(kept, grad):
    return (grad,)

def back_keep(v):
    return (v, None)

def back_low(kept, grad):
    return (low(grad),)
low.defvjp(low_keep, low_pass)
low_back.defvjp(back_keep, back_low)
tap_offsets = [(row_off, col_off) for row_off in range(3) for col_off in range(3)]

def pad_faces(field, face_table):
    north = jnp.take(field[:, :, -1], face_table[:, 0], axis=1)
    east = jnp.take(field[:, :, :, 0], face_table[:, 1], axis=1)
    south = jnp.take(field[:, :, 0], face_table[:, 2], axis=1)
    west = jnp.take(field[:, :, :, -1], face_table[:, 3], axis=1)
    middle = jnp.concatenate([west[:, :, :, None], field, east[:, :, :, None]], axis=3)
    top_row = jnp.pad(north, ((0, 0), (0, 0), (1, 1), (0, 0)))
    bottom_row = jnp.pad(south, ((0, 0), (0, 0), (1, 1), (0, 0)))
    return jnp.concatenate([top_row[:, :, None], middle, bottom_row[:, :, None]], axis=2)

def conv_apply(padded, weight):
    edge_len = padded.shape[2] - 2
    channels = weight.shape[1]
    summed = None
    for tap_index, (row_off, col_off) in enumerate(tap_offsets):
        window = padded[:, :, row_off:row_off + edge_len, col_off:col_off + edge_len]
        product = jnp.einsum('rfijc,cd->rfijd', window, weight[tap_index * channels:(tap_index + 1) * channels], precision=lax.Precision.HIGHEST)
        summed = product if summed is None else summed + product
    return summed

def gelu_tanh(v):
    return jax.nn.gelu(v, approximate=True)

def forward_block(fields, w_one, w_two, w_three, face_table):
    low_one = low(w_one)
    low_two = low(w_two)
    low_three = low(w_three)
    pre_one = low_back(conv_apply(pad_faces(fields, face_table), low_one))
    hidden = low(gelu_tanh(pre_one))
    pre_two = low_back(conv_apply(pad_faces(hidden, face_table), low_two))
    skipped = jnp.einsum('rfijc,cd->rfijd', fields, low_three, precision=lax.Precision.HIGHEST)
    return gelu_tanh(pre_two) + skipped

def adamw(weight, moment, square, grad, rate):
    moment_new = 0.9 * moment + 0.1 * grad
    square_new = 0.999 * square + 0.001 * grad * grad
    fix_one = 1.0 - 0.9 ** STEP_COUNT
    fix_two = 1.0 - 0.999 ** STEP_COUNT
    weight_new = weight - rate * (moment_new / fix_one / (jnp.sqrt(square_new / fix_two) + 1e-08) + 0.01 * weight)
    return (weight_new, moment_new, square_new)

def reference(inputs, cotangent, lengths, face_table, w_first, w_second, w_skip, mom_first, sq_first, mom_second, sq_second, mom_skip, sq_skip):

    def per_sample(carry, items):
        fields, cot_one, length = items

        def block_fn(field_f, one, two, three):
            return forward_block(field_f, one, two, three, face_table)
        result, pullback = jax.vjp(block_fn, fields.astype(jnp.float32), w_first, w_second, w_skip)
        live = (jnp.arange(ROLL) < length).astype(jnp.float32)
        grad_out = cot_one.astype(jnp.float32) * live[:, None, None, None, None]
        grad_in, grad_one, grad_two, grad_three = pullback(grad_out)
        carry = (carry[0] + grad_one, carry[1] + grad_two, carry[2] + grad_three)
        return (carry, (result.astype(jnp.bfloat16), grad_in))
    start = (jnp.zeros_like(w_first), jnp.zeros_like(w_second), jnp.zeros_like(w_skip))
    totals, (output, grad_inputs) = lax.scan(per_sample, start, (inputs, cotangent, lengths))
    rate_conv = (9 * C) ** (-0.5)
    rate_skip = C ** (-0.5)
    new_first, new_mom_first, new_sq_first = adamw(w_first, mom_first, sq_first, totals[0], rate_conv)
    new_second, new_mom_second, new_sq_second = adamw(w_second, mom_second, sq_second, totals[1], rate_conv)
    new_skip, new_mom_skip, new_sq_skip = adamw(w_skip, mom_skip, sq_skip, totals[2], rate_skip)
    return (output, grad_inputs, new_first, new_mom_first, new_sq_first, new_second, new_mom_second, new_sq_second, new_skip, new_mom_skip, new_sq_skip)
```

```python
import functools

import jax
import jax.numpy as jnp
from jax import lax
from jax.experimental import pallas as pl
from jax.experimental.pallas import tpu as pltpu
from jax.sharding import PartitionSpec as P

STEP_COUNT = 10
BF = jnp.bfloat16
F32 = jnp.float32
FS = 6
ROLL = 8
PAIRS = 6
PAIR_ROWS = 2 * ROLL
GELU_K = 0.7978845608028654
GELU_C = 0.044715
VMEM_LIMIT = 56 * 2**20


def spec_any():
    return pl.BlockSpec(memory_space=pl.ANY)


def spec_vmem():
    return pl.BlockSpec(memory_space=pltpu.VMEM)


def spec_smem():
    return pl.BlockSpec(memory_space=pltpu.SMEM)


def gelu_both(v):
    sq = v * v
    t = jnp.tanh(v * (GELU_K + (GELU_K * GELU_C) * sq))
    half = 0.5 + 0.5 * t
    slope = half + (0.5 * v) * (1.0 - t * t) * (GELU_K + (3.0 * GELU_K * GELU_C) * sq)
    return v * half, slope


def window(p_ref, pair, row, rows, col, channels):
    return p_ref[pair, row : row + rows, col : col + FS].reshape(rows * FS * PAIR_ROWS, channels)


def conv_rows(p_ref, w_ref, pair, row, rows):
    c = w_ref.shape[1]
    acc = None
    for a in range(3):
        for b in range(3):
            t = 3 * a + b
            part = jnp.dot(
                window(p_ref, pair, row + a, rows, b, c),
                w_ref[t * c : (t + 1) * c],
                preferred_element_type=F32,
            )
            acc = part if acc is None else acc + part
    return acc


def conv_rows_back(g_ref, w_ref, pair, row, rows):
    c = w_ref.shape[1]
    acc = None
    for a in range(3):
        for b in range(3):
            t = 3 * a + b
            part = lax.dot_general(
                window(g_ref, pair, row + 2 - a, rows, 2 - b, c),
                w_ref[t * c : (t + 1) * c],
                (((1,), (1,)), ((), ())),
                preferred_element_type=F32,
            )
            acc = part if acc is None else acc + part
    return acc


def weight_grad(p_ref, g_ref, dw_ref):
    c = p_ref.shape[-1]
    g = g_ref[:, 1 : FS + 1, 1 : FS + 1].reshape(-1, c)
    for a in range(3):
        for b in range(3):
            t = 3 * a + b
            dw_ref[t * c : (t + 1) * c] = lax.dot_general(
                p_ref[:, a : a + FS, b : b + FS].reshape(-1, c),
                g,
                (((0,), (0,)), ((), ())),
                preferred_element_type=F32,
            ).astype(dw_ref.dtype)


def zero_corners(p_ref):
    zero = jnp.zeros((PAIRS, 1, 1, PAIR_ROWS, p_ref.shape[-1]), p_ref.dtype)
    for i in (0, FS + 1):
        for j in (0, FS + 1):
            p_ref[:, i : i + 1, j : j + 1] = zero


def stash_edges(e_ref, pair, row, rows, v):
    for par in range(2):
        face = 2 * pair + par
        half = v[:, :, par * ROLL : (par + 1) * ROLL]
        if row + rows == FS:
            e_ref[face, 0] = half[rows - 1]
        e_ref[face, 1, row : row + rows] = half[:, 0]
        if row == 0:
            e_ref[face, 2] = half[0]
        e_ref[face, 3, row : row + rows] = half[:, FS - 1]


def fill_halo(e_ref, table_ref, p_ref):
    for pair in range(PAIRS):
        for side in range(4):
            one = e_ref[table_ref[2 * pair, side], side]
            two = e_ref[table_ref[2 * pair + 1, side], side]
            v = jnp.concatenate([one, two], axis=1).astype(p_ref.dtype)
            if side == 0:
                p_ref[pair, 0, 1 : FS + 1] = v
            elif side == 1:
                p_ref[pair, 1 : FS + 1, FS + 1] = v
            elif side == 2:
                p_ref[pair, FS + 1, 1 : FS + 1] = v
            else:
                p_ref[pair, 1 : FS + 1, 0] = v
    zero_corners(p_ref)


def add_edges(e_ref, table_ref, pair, row, rows, v):
    for par in range(2):
        face = 2 * pair + par
        half = v[:, :, par * ROLL : (par + 1) * ROLL]
        if row == 0:
            to = table_ref[face, 0]
            e_ref[to, 0] = e_ref[to, 0] + half[0]
        to = table_ref[face, 1]
        e_ref[to, 1, row : row + rows] = e_ref[to, 1, row : row + rows] + half[:, FS - 1]
        if row + rows == FS:
            to = table_ref[face, 2]
            e_ref[to, 2] = e_ref[to, 2] + half[rows - 1]
        to = table_ref[face, 3]
        e_ref[to, 3, row : row + rows] = e_ref[to, 3, row : row + rows] + half[:, 0]


def fill_halo_back(e_ref, p_ref):
    for pair in range(PAIRS):
        for side in range(4):
            v = jnp.concatenate([e_ref[2 * pair, side], e_ref[2 * pair + 1, side]], axis=1)
            v = v.astype(p_ref.dtype)
            if side == 0:
                p_ref[pair, FS + 1, 1 : FS + 1] = v
            elif side == 1:
                p_ref[pair, 1 : FS + 1, 0] = v
            elif side == 2:
                p_ref[pair, 0, 1 : FS + 1] = v
            else:
                p_ref[pair, 1 : FS + 1, FS + 1] = v
    zero_corners(p_ref)


def to_pairs(ref, row):
    halves = []
    for par in range(2):
        v = ref[0, :, par, row].astype(F32)
        halves.append(jnp.transpose(v, (1, 0, 2)))
    return jnp.concatenate(halves, axis=1)


def from_pairs(ref, row, v):
    for par in range(2):
        half = v[:, par * ROLL : (par + 1) * ROLL]
        ref[0, :, par, row] = jnp.transpose(half, (1, 0, 2)).astype(ref.dtype)


def enter_kernel(lengths_ref, table_ref, x_ref, cot_ref, xp_ref, go_ref, dws_ref, e_ref, acc_ref):
    pair = pl.program_id(0)
    c = x_ref.shape[-1]
    live = (
        lax.broadcasted_iota(jnp.int32, (FS, PAIR_ROWS, c), 1) % ROLL < lengths_ref[0]
    )
    for i in range(FS):
        v = to_pairs(x_ref, i)
        xp_ref[pair, i + 1, 1 : FS + 1] = v.astype(BF)
        for par in range(2):
            face = 2 * pair + par
            half = v[:, par * ROLL : (par + 1) * ROLL]
            if i == FS - 1:
                e_ref[face, 0] = half
            e_ref[face, 1, i] = half[0]
            if i == 0:
                e_ref[face, 2] = half
            e_ref[face, 3, i] = half[FS - 1]
        go_ref[0, i] = jnp.where(live, to_pairs(cot_ref, i), 0.0).astype(BF)
    part = lax.dot_general(
        xp_ref[pair, 1 : FS + 1, 1 : FS + 1].reshape(-1, c),
        go_ref[0].reshape(-1, c),
        (((0,), (0,)), ((), ())),
        preferred_element_type=F32,
    )

    @pl.when(pair == 0)
    def _():
        acc_ref[...] = part

    @pl.when(pair > 0)
    def _():
        acc_ref[...] = acc_ref[...] + part

    @pl.when(pair == PAIRS - 1)
    def _():
        dws_ref[...] = acc_ref[...].astype(dws_ref.dtype)
        fill_halo(e_ref, table_ref, xp_ref)


def enter(lengths, table, x, cot):
    c = x.shape[-1]
    block = pl.BlockSpec((1, ROLL, 2, FS, FS, c), lambda p: (0, 0, p, 0, 0, 0))
    return pl.pallas_call(
        enter_kernel,
        grid=(PAIRS,),
        in_specs=[spec_smem(), spec_smem(), block, block],
        out_specs=[
            spec_vmem(),
            pl.BlockSpec((1, FS, FS, PAIR_ROWS, c), lambda p: (p, 0, 0, 0, 0)),
            spec_vmem(),
        ],
        out_shape=[
            jax.ShapeDtypeStruct((PAIRS, FS + 2, FS + 2, PAIR_ROWS, c), BF),
            jax.ShapeDtypeStruct((PAIRS, FS, FS, PAIR_ROWS, c), BF),
            jax.ShapeDtypeStruct((c, c), BF),
        ],
        scratch_shapes=[
            pltpu.VMEM((2 * PAIRS, 4, FS, ROLL, c), F32),
            pltpu.VMEM((c, c), F32),
        ],
        compiler_params=pltpu.CompilerParams(
            dimension_semantics=("arbitrary",), vmem_limit_bytes=VMEM_LIMIT
        ),
        name="enter",
    )(lengths, table, x, cot)


ROWS = 3


def first_kernel(table_ref, xp_ref, w_ref, hp_ref, slope_ref, e_ref):
    c = w_ref.shape[1]
    for pair in range(PAIRS):
        for row in range(0, FS, ROWS):
            hidden, slope = gelu_both(conv_rows(xp_ref, w_ref, pair, row, ROWS))
            shape = (ROWS, FS, PAIR_ROWS, c)
            low = hidden.astype(BF).reshape(shape)
            hp_ref[pair, row + 1 : row + 1 + ROWS, 1 : FS + 1] = low
            slope_ref[pair, row : row + ROWS] = slope.astype(BF).reshape(shape)
            stash_edges(e_ref, pair, row, ROWS, hidden.reshape(shape))
    fill_halo(e_ref, table_ref, hp_ref)


def first(table, xp, w):
    c = w.shape[1]
    return pl.pallas_call(
        first_kernel,
        in_specs=[spec_smem(), spec_vmem(), spec_vmem()],
        out_specs=[spec_vmem(), spec_vmem()],
        out_shape=[
            jax.ShapeDtypeStruct(xp.shape, BF),
            jax.ShapeDtypeStruct((PAIRS, FS, FS, PAIR_ROWS, c), BF),
        ],
        scratch_shapes=[pltpu.VMEM((2 * PAIRS, 4, FS, ROLL, c), F32)],
        compiler_params=pltpu.CompilerParams(vmem_limit_bytes=VMEM_LIMIT),
        name="first",
    )(table, xp, w)


def second_kernel(table_ref, hp_ref, w_ref, ws_ref, xp_ref, go_ref, out_ref, gp_ref, dw_ref, e_ref):
    c = w_ref.shape[1]
    e_ref[...] = jnp.zeros_like(e_ref)
    for pair in range(PAIRS):
        for row in range(0, FS, ROWS):
            value, slope = gelu_both(conv_rows(hp_ref, w_ref, pair, row, ROWS))
            value = value + jnp.dot(
                window(xp_ref, pair, row + 1, ROWS, 1, c), ws_ref[...], preferred_element_type=F32
            )
            shape = (ROWS, FS, PAIR_ROWS, c)
            value = value.reshape(shape)
            for i in range(ROWS):
                from_pairs(out_ref.at[:, :, 2 * pair : 2 * pair + 2], row + i, value[i])
            grad = go_ref[pair, row : row + ROWS].astype(F32) * slope.reshape(shape)
            low = grad.astype(BF)
            gp_ref[pair, row + 1 : row + 1 + ROWS, 1 : FS + 1] = low
            add_edges(e_ref, table_ref, pair, row, ROWS, low.astype(F32))
    fill_halo_back(e_ref, gp_ref)
    weight_grad(hp_ref, gp_ref, dw_ref)


def second(table, hp, w, ws, xp, go):
    c = w.shape[1]
    return pl.pallas_call(
        second_kernel,
        in_specs=[spec_smem()] + [spec_vmem()] * 5,
        out_specs=[spec_vmem()] * 3,
        out_shape=[
            jax.ShapeDtypeStruct((1, ROLL, 2 * PAIRS, FS, FS, c), BF),
            jax.ShapeDtypeStruct(hp.shape, BF),
            jax.ShapeDtypeStruct(w.shape, BF),
        ],
        scratch_shapes=[pltpu.VMEM((2 * PAIRS, 4, FS, ROLL, c), F32)],
        compiler_params=pltpu.CompilerParams(vmem_limit_bytes=VMEM_LIMIT),
        name="second",
    )(table, hp, w, ws, xp, go)


def hidden_back_kernel(table_ref, gp_ref, w_ref, slope_ref, xp_ref, op_ref, dw_ref, e_ref):
    c = w_ref.shape[1]
    e_ref[...] = jnp.zeros_like(e_ref)
    for pair in range(PAIRS):
        for row in range(0, FS, ROWS):
            shape = (ROWS, FS, PAIR_ROWS, c)
            grad = conv_rows_back(gp_ref, w_ref, pair, row, ROWS).reshape(shape)
            low = (grad * slope_ref[pair, row : row + ROWS].astype(F32)).astype(BF)
            op_ref[pair, row + 1 : row + 1 + ROWS, 1 : FS + 1] = low
            add_edges(e_ref, table_ref, pair, row, ROWS, low.astype(F32))
    fill_halo_back(e_ref, op_ref)
    weight_grad(xp_ref, op_ref, dw_ref)


def hidden_back(table, gp, w, slope, xp):
    c = w.shape[1]
    return pl.pallas_call(
        hidden_back_kernel,
        in_specs=[spec_smem()] + [spec_vmem()] * 4,
        out_specs=[spec_vmem()] * 2,
        out_shape=[
            jax.ShapeDtypeStruct(gp.shape, BF),
            jax.ShapeDtypeStruct(w.shape, BF),
        ],
        scratch_shapes=[pltpu.VMEM((2 * PAIRS, 4, FS, ROLL, c), F32)],
        compiler_params=pltpu.CompilerParams(vmem_limit_bytes=VMEM_LIMIT),
        name="hidden_back",
    )(table, gp, w, slope, xp)


def inputs_back_kernel(gp_ref, w_ref, ws_ref, go_ref, out_ref):
    c = w_ref.shape[1]
    for pair in range(PAIRS):
        for row in range(0, FS, ROWS):
            grad = conv_rows_back(gp_ref, w_ref, pair, row, ROWS)
            grad = grad + lax.dot_general(
                go_ref[pair, row : row + ROWS].reshape(-1, c),
                ws_ref[...],
                (((1,), (1,)), ((), ())),
                preferred_element_type=F32,
            )
            grad = grad.reshape(ROWS, FS, PAIR_ROWS, c)
            for i in range(ROWS):
                from_pairs(out_ref.at[:, :, 2 * pair : 2 * pair + 2], row + i, grad[i])


def inputs_back(gp, w, ws, go):
    c = w.shape[1]
    return pl.pallas_call(
        inputs_back_kernel,
        in_specs=[spec_vmem()] * 4,
        out_specs=spec_vmem(),
        out_shape=jax.ShapeDtypeStruct((1, ROLL, 2 * PAIRS, FS, FS, c), F32),
        compiler_params=pltpu.CompilerParams(vmem_limit_bytes=VMEM_LIMIT),
        name="inputs_back",
    )(gp, w, ws, go)


def adamw(weight, moment, square, grad, rate):
    moment_new = 0.9 * moment + 0.1 * grad
    square_new = 0.999 * square + 0.001 * grad * grad
    fix_one = 1.0 - 0.9**STEP_COUNT
    fix_two = 1.0 - 0.999**STEP_COUNT
    weight_new = weight - rate * (
        moment_new / fix_one / (jnp.sqrt(square_new / fix_two) + 1e-08) + 0.01 * weight
    )
    return (weight_new, moment_new, square_new)


def reduce_rows(grad):
    shard = lax.psum_scatter(grad, "fsdp", scatter_dimension=0, tiled=True)
    return lax.psum(shard, "dp").astype(F32)


def per_device(
    inputs,
    cotangent,
    lengths,
    face_table,
    w_first,
    w_second,
    w_skip,
    mom_first,
    sq_first,
    mom_second,
    sq_second,
    mom_skip,
    sq_skip,
):
    c = inputs.shape[-1]
    gather = functools.partial(lax.all_gather, axis_name="fsdp", axis=0, tiled=True)
    all_first = gather(w_first.astype(BF))
    all_second = gather(w_second.astype(BF))
    all_skip = gather(w_skip.astype(BF))
    xp, go, dw_skip = enter(lengths, face_table, inputs, cotangent)
    hp, slope = first(face_table, xp, all_first)
    output, gp, dw_second = second(face_table, hp, all_second, all_skip, xp, go)
    op, dw_first = hidden_back(face_table, gp, all_second, slope, xp)
    grad_inputs = inputs_back(op, all_first, all_skip, go)
    rate_conv = (9 * c) ** (-0.5)
    rate_skip = c ** (-0.5)
    skip_set = adamw(w_skip, mom_skip, sq_skip, reduce_rows(dw_skip), rate_skip)
    second_set = adamw(w_second, mom_second, sq_second, reduce_rows(dw_second), rate_conv)
    first_set = adamw(w_first, mom_first, sq_first, reduce_rows(dw_first), rate_conv)
    return (output, grad_inputs) + first_set + second_set + skip_set


def solution(mesh):
    fields = P(("dp", "fsdp"), None, None, None, None, None)
    rows = P("fsdp", None)
    return jax.shard_map(
        per_device,
        mesh=mesh,
        in_specs=(fields, fields, P(("dp", "fsdp")), P()) + (rows,) * 9,
        out_specs=(fields, fields) + (rows,) * 9,
        check_vma=False,
    )
```

```python
import jax
import jax.numpy as jnp
from jax import lax
from jax.experimental import pallas as pl
from jax.experimental.pallas import tpu as pltpu
from jax.sharding import Mesh
from jax.sharding import PartitionSpec as P

STEP_COUNT = 10
BF = jnp.bfloat16
F32 = jnp.float32
FS = 6
ROLL = 8
FACES = 12
GELU_K = 0.7978845608028654
GELU_C = 0.044715
VMEM_LIMIT = 40 * 2**20


ANY = pl.BlockSpec(memory_space=pl.ANY)
VMEM = pl.BlockSpec(memory_space=pltpu.VMEM)
SMEM = pl.BlockSpec(memory_space=pltpu.SMEM)


def field(c, dtype=BF):
    return jax.ShapeDtypeStruct((FACES, FS, FS, ROLL, c), dtype)


def padded(c):
    return (FACES, FS + 2, FS + 2, ROLL, c)


def inner(ref):
    return ref.at[:, 1 : FS + 1, 1 : FS + 1]


def params():
    return pltpu.CompilerParams(vmem_limit_bytes=VMEM_LIMIT)


def gelu_both(v):
    sq = v * v
    t = jnp.tanh(v * (GELU_K + (GELU_K * GELU_C) * sq))
    half = 0.5 + 0.5 * t
    slope = half + (0.5 * v) * (1.0 - t * t) * (GELU_K + (3.0 * GELU_K * GELU_C) * sq)
    return v * half, slope


def window(p_ref, face, a, b):
    return p_ref[face, a : a + FS, b : b + FS].reshape(FS * FS * ROLL, p_ref.shape[-1])


def conv(p_ref, w_ref, face):
    c = w_ref.shape[1]
    acc = None
    for a in range(3):
        for b in range(3):
            t = 3 * a + b
            part = jnp.dot(
                window(p_ref, face, a, b), w_ref[t * c : (t + 1) * c], preferred_element_type=F32
            )
            acc = part if acc is None else acc + part
    return acc


def dot_back(v, w):
    return lax.dot_general(v, w, (((1,), (1,)), ((), ())), preferred_element_type=F32)


def conv_back(g_ref, w_ref, face):
    c = w_ref.shape[1]
    acc = None
    for a in range(3):
        for b in range(3):
            t = 3 * a + b
            part = dot_back(window(g_ref, face, 2 - a, 2 - b), w_ref[t * c : (t + 1) * c])
            acc = part if acc is None else acc + part
    return acc


def outer(p, g):
    c = p.shape[-1]
    return lax.dot_general(
        p.reshape(-1, c), g.reshape(-1, c), (((0,), (0,)), ((), ())), preferred_element_type=F32
    )


def zero_corners(p_ref):
    zero = jnp.zeros((FACES, 1, 1, ROLL, p_ref.shape[-1]), p_ref.dtype)
    for i in (0, FS + 1):
        for j in (0, FS + 1):
            p_ref[:, i : i + 1, j : j + 1] = zero


def fill_halo(table_ref, p_ref):
    for face in range(FACES):
        p_ref[face, 0, 1 : FS + 1] = p_ref[table_ref[0, face], FS, 1 : FS + 1]
        p_ref[face, 1 : FS + 1, FS + 1] = p_ref[table_ref[1, face], 1 : FS + 1, 1]
        p_ref[face, FS + 1, 1 : FS + 1] = p_ref[table_ref[2, face], 1, 1 : FS + 1]
        p_ref[face, 1 : FS + 1, 0] = p_ref[table_ref[3, face], 1 : FS + 1, FS]
    zero_corners(p_ref)


def add_edges(e_ref, table_ref, face, v):
    for side, part in enumerate((v[0], v[:, FS - 1], v[FS - 1], v[:, 0])):
        to = table_ref[side, face]
        e_ref[to, side] = e_ref[to, side] + part


def fill_halo_back(e_ref, p_ref):
    for face in range(FACES):
        p_ref[face, FS + 1, 1 : FS + 1] = e_ref[face, 0].astype(p_ref.dtype)
        p_ref[face, 1 : FS + 1, 0] = e_ref[face, 1].astype(p_ref.dtype)
        p_ref[face, 0, 1 : FS + 1] = e_ref[face, 2].astype(p_ref.dtype)
        p_ref[face, 1 : FS + 1, FS + 1] = e_ref[face, 3].astype(p_ref.dtype)
    zero_corners(p_ref)


def edge_sums(c):
    return pltpu.VMEM((FACES, 4, FS, ROLL, c), F32)


class Plan:
    def __init__(self, sizes, channels):
        self.tiles, self.ranks = sizes["tile"], sizes["fsdp"]
        self.c = channels
        self.conv = 9 * channels
        self.piece = self.conv // (self.ranks * 2 * self.tiles)
        self.skip_piece = channels // (self.ranks * 2 * self.tiles)
        self.chunk = 2 * self.piece + self.skip_piece
        self.shard = self.conv // self.ranks
        self.skip_shard = channels // self.ranks


def place_rows(plan, ids_ref, dst_ref, value, first_row, piece, offset):
    core, tile, rank = ids_ref[0], ids_ref[1], ids_ref[2]
    end = first_row + value.shape[0]
    row = first_row
    while row < end:
        number = row // piece
        stop = min(end, (number + 1) * piece)
        to_tile = number % plan.tiles
        to_core = number // plan.tiles % 2
        to_rank = number // (2 * plan.tiles)
        at = offset + row - number * piece
        dst_ref[
            to_core ^ core,
            to_tile ^ tile,
            (to_rank + plan.ranks - rank) % plan.ranks,
            at : at + stop - row,
        ] = value[row - first_row : stop - first_row]
        row = stop


def weight_grad(plan, ids_ref, p_ref, g, dst_ref, offset):
    c = p_ref.shape[-1]
    for a in range(3):
        for b in range(3):
            part = outer(p_ref[:, a : a + FS, b : b + FS], g).astype(BF)
            place_rows(plan, ids_ref, dst_ref, part, (3 * a + b) * c, plan.piece, offset)


def pack_kernel(ids_ref, one_ref, two_ref, skip_ref, low1_ref, half1_ref, low2_ref, low3_ref, half2_ref):
    core = ids_ref[0]
    rows = one_ref.shape[0] // 2
    few = skip_ref.shape[0] // 2
    low1_ref[...] = one_ref[...].astype(BF)
    half1_ref[...] = one_ref[pl.ds(core * rows, rows)].astype(BF)
    low2_ref[...] = two_ref[...].astype(BF)
    low3_ref[...] = skip_ref[...].astype(BF)
    half2_ref[0:rows] = two_ref[pl.ds(core * rows, rows)].astype(BF)
    half2_ref[rows : rows + few] = skip_ref[pl.ds(core * few, few)].astype(BF)


def pack(plan, ids, one, two, skip):
    c, rows, few = plan.c, plan.shard, plan.skip_shard
    shapes = [(rows, c), (rows // 2, c), (rows, c), (few, c), ((rows + few) // 2, c)]
    return pl.pallas_call(
        pack_kernel,
        in_specs=[SMEM] + [VMEM] * 3,
        out_specs=[VMEM] * 5,
        out_shape=[jax.ShapeDtypeStruct(v, BF) for v in shapes],
        compiler_params=params(),
        name="pack",
    )(ids, one, two, skip)


def weight_copies(plan, ids_ref, low_ref, near_refs, far_refs, w_ref, rows, offset, sem):
    core, rank = ids_ref[0], ids_ref[2]
    half = rows // 2
    copies = [pltpu.make_async_copy(low_ref, w_ref.at[pl.ds(rank * rows, rows)], sem.at[0])]
    for d in range(1, plan.ranks):
        start = (rank + plan.ranks - d) % plan.ranks * rows
        for k, refs in enumerate((near_refs, far_refs)):
            side = core if k == 0 else 1 - core
            copies.append(
                pltpu.make_async_copy(
                    refs[d - 1].at[pl.ds(offset, half)],
                    w_ref.at[pl.ds(start + side * half, half)],
                    sem.at[2 * d - 1 + k],
                )
            )
    return copies


def enter_kernel(lengths_ref, table_ref, x_ref, cot_ref, xp_ref, go_ref, dw_ref, sem):
    c = x_ref.shape[-1]
    load = pltpu.make_async_copy(x_ref, inner(xp_ref), sem)
    load.start()
    live = lax.broadcasted_iota(jnp.int32, (FS, FS, ROLL, c), 2) < lengths_ref[0]
    for face in range(FACES):
        go_ref[face] = jnp.where(live, cot_ref[face].astype(F32), 0.0).astype(BF)
    load.wait()
    fill_halo(table_ref, xp_ref)
    dw_ref[...] = outer(xp_ref[:, 1 : FS + 1, 1 : FS + 1], go_ref[...]).astype(dw_ref.dtype)


def enter(lengths, table, x, cot):
    c = x.shape[-1]
    return pl.pallas_call(
        enter_kernel,
        in_specs=[SMEM, SMEM, ANY, VMEM],
        out_specs=[VMEM, VMEM, VMEM],
        out_shape=[
            jax.ShapeDtypeStruct(padded(c), BF),
            field(c),
            jax.ShapeDtypeStruct((c, c), BF),
        ],
        scratch_shapes=[pltpu.SemaphoreType.DMA],
        compiler_params=params(),
        name="enter",
    )(lengths, table, x, cot)


def first(plan, ids, table, xp, low, near, far):
    c = plan.c
    count = plan.ranks - 1

    def kernel(ids_ref, table_ref, xp_ref, low_ref, *refs):
        near_refs, far_refs = refs[:count], refs[count : 2 * count]
        hp_ref, slope_ref, w_out, w_ref, sem, out_sem = refs[2 * count :]
        copies = weight_copies(plan, ids_ref, low_ref, near_refs, far_refs, w_ref, plan.shard, 0, sem)
        for copy in copies:
            copy.start()
        for copy in copies:
            copy.wait()
        keep = pltpu.make_async_copy(w_ref, w_out, out_sem)
        keep.start()
        for face in range(FACES):
            hidden, slope = gelu_both(conv(xp_ref, w_ref, face))
            hp_ref[face, 1 : FS + 1, 1 : FS + 1] = hidden.astype(BF).reshape(FS, FS, ROLL, c)
            slope_ref[face] = slope.astype(BF).reshape(FS, FS, ROLL, c)
        fill_halo(table_ref, hp_ref)
        keep.wait()

    return pl.pallas_call(
        kernel,
        in_specs=[SMEM, SMEM, VMEM] + [ANY] * (1 + 2 * count),
        out_specs=[VMEM, VMEM, ANY],
        out_shape=[
            jax.ShapeDtypeStruct(padded(c), BF),
            field(c),
            jax.ShapeDtypeStruct((plan.conv, c), BF),
        ],
        scratch_shapes=[
            pltpu.VMEM((plan.conv, c), BF),
            pltpu.SemaphoreType.DMA((2 * count + 1,)),
            pltpu.SemaphoreType.DMA,
        ],
        compiler_params=params(),
        name="first",
    )(ids, table, xp, low, *near, *far)


def second(plan, ids, table, hp, slope, xp, go, dws, low, low_skip, near, far):
    c = plan.c
    count = plan.ranks - 1

    def kernel(ids_ref, table_ref, hp_ref, slope_hbm, xp_hbm, go_hbm, dws_ref, low_ref, lows_ref, *refs):
        near_refs, far_refs = refs[:count], refs[count : 2 * count]
        (out_hbm, op_hbm, ws_hbm, keep_hbm, send_hbm) = refs[2 * count : 2 * count + 5]
        (out_ref, op_ref, w_ref, ws_ref, dw_ref, gp_ref, xp_ref, go_ref, slope_ref, e_ref) = refs[
            2 * count + 5 : 2 * count + 15
        ]
        sem, sem_skip, sem_in, sem_out = refs[2 * count + 15 :]
        copies = weight_copies(plan, ids_ref, low_ref, near_refs, far_refs, w_ref, plan.shard, 0, sem)
        copies += weight_copies(
            plan, ids_ref, lows_ref, near_refs, far_refs, ws_ref, plan.skip_shard, plan.shard // 2, sem_skip
        )
        for copy in copies:
            copy.start()
        loads = [
            pltpu.make_async_copy(xp_hbm, xp_ref, sem_in.at[0]),
            pltpu.make_async_copy(go_hbm, go_ref, sem_in.at[1]),
            pltpu.make_async_copy(slope_hbm, slope_ref, sem_in.at[2]),
        ]
        for load in loads:
            load.start()
        e_ref[...] = jnp.zeros_like(e_ref)
        place_rows(plan, ids_ref, dw_ref, dws_ref[...], 0, plan.skip_piece, 2 * plan.piece)
        for copy in copies:
            copy.wait()
        for load in loads:
            load.wait()
        stores = [
            pltpu.make_async_copy(ws_ref, ws_hbm, sem_out.at[0]),
            pltpu.make_async_copy(out_ref, out_hbm, sem_out.at[1]),
            pltpu.make_async_copy(op_ref, op_hbm, sem_out.at[2]),
            pltpu.make_async_copy(dw_ref.at[0], keep_hbm, sem_out.at[3]),
            pltpu.make_async_copy(dw_ref.at[1], send_hbm, sem_out.at[4]),
        ]
        stores[0].start()
        for face in range(FACES):
            value, slope = gelu_both(conv(hp_ref, w_ref, face))
            value = value + jnp.dot(
                xp_ref[face, 1 : FS + 1, 1 : FS + 1].reshape(-1, c),
                ws_ref[...],
                preferred_element_type=F32,
            )
            out_ref[face] = value.astype(BF).reshape(FS, FS, ROLL, c)
            low_grad = (go_ref[face].astype(F32) * slope.reshape(FS, FS, ROLL, c)).astype(BF)
            gp_ref[face, 1 : FS + 1, 1 : FS + 1] = low_grad
            add_edges(e_ref, table_ref, face, low_grad.astype(F32))
        stores[1].start()
        weight_grad(plan, ids_ref, hp_ref, gp_ref[:, 1 : FS + 1, 1 : FS + 1], dw_ref, plan.piece)
        fill_halo_back(e_ref, gp_ref)
        e_ref[...] = jnp.zeros_like(e_ref)
        for face in range(FACES):
            grad = conv_back(gp_ref, w_ref, face).reshape(FS, FS, ROLL, c)
            low_grad = (grad * slope_ref[face].astype(F32)).astype(BF)
            op_ref[face, 1 : FS + 1, 1 : FS + 1] = low_grad
            add_edges(e_ref, table_ref, face, low_grad.astype(F32))
        fill_halo_back(e_ref, op_ref)
        stores[2].start()
        weight_grad(plan, ids_ref, xp_ref, op_ref[:, 1 : FS + 1, 1 : FS + 1], dw_ref, 0)
        stores[3].start()
        stores[4].start()
        for store in stores:
            store.wait()

    sums = (plan.tiles, plan.ranks, plan.chunk, c)
    return pl.pallas_call(
        kernel,
        in_specs=[SMEM, SMEM, VMEM, ANY, ANY, ANY, VMEM] + [ANY] * (2 + 2 * count),
        out_specs=[ANY] * 5,
        out_shape=[
            field(c),
            jax.ShapeDtypeStruct(padded(c), BF),
            jax.ShapeDtypeStruct((c, c), BF),
            jax.ShapeDtypeStruct(sums, BF),
            jax.ShapeDtypeStruct(sums, BF),
        ],
        scratch_shapes=[
            pltpu.VMEM(field(c).shape, BF),
            pltpu.VMEM(padded(c), BF),
            pltpu.VMEM((plan.conv, c), BF),
            pltpu.VMEM((c, c), BF),
            pltpu.VMEM((2,) + sums, BF),
            pltpu.VMEM(padded(c), BF),
            pltpu.VMEM(padded(c), BF),
            pltpu.VMEM(field(c).shape, BF),
            pltpu.VMEM(field(c).shape, BF),
            edge_sums(c),
            pltpu.SemaphoreType.DMA((2 * count + 1,)),
            pltpu.SemaphoreType.DMA((2 * count + 1,)),
            pltpu.SemaphoreType.DMA((3,)),
            pltpu.SemaphoreType.DMA((5,)),
        ],
        compiler_params=params(),
        name="second",
    )(ids, table, hp, slope, xp, go, dws, low, low_skip, *near, *far)


def inputs_back_kernel(gp_ref, w_ref, ws_ref, go_ref, out_hbm, out_ref, sem):
    c = w_ref.shape[1]
    stores = []
    for face in range(FACES):
        grad = conv_back(gp_ref, w_ref, face)
        grad = grad + dot_back(go_ref[face].reshape(-1, c), ws_ref[...])
        out_ref[face] = grad.reshape(FS, FS, ROLL, c)
        stores.append(pltpu.make_async_copy(out_ref.at[face], out_hbm.at[face], sem.at[face]))
        stores[-1].start()
    for store in stores:
        store.wait()


def inputs_back(gp, w, ws, go):
    c = w.shape[1]
    return pl.pallas_call(
        inputs_back_kernel,
        in_specs=[VMEM] * 4,
        out_specs=ANY,
        out_shape=field(c, F32),
        scratch_shapes=[pltpu.VMEM(field(c).shape, F32), pltpu.SemaphoreType.DMA((FACES,))],
        compiler_params=params(),
        name="inputs_back",
    )(gp, w, ws, go)


def adamw(weight, moment, square, grad, rate):
    moment_new = 0.9 * moment + 0.1 * grad
    square_new = 0.999 * square + 0.001 * grad * grad
    fix_one = 1.0 - 0.9**STEP_COUNT
    fix_two = 1.0 - 0.999**STEP_COUNT
    weight_new = weight - rate * (
        moment_new / fix_one / (jnp.sqrt(square_new / fix_two) + 1e-08) + 0.01 * weight
    )
    return (weight_new, moment_new, square_new)


def update(plan, ids, near, far, sets):
    c, tiles = plan.c, plan.tiles

    def kernel(ids_ref, *refs):
        near_refs, far_refs = refs[:tiles], refs[tiles : 2 * tiles]
        state = refs[2 * tiles : 2 * tiles + 9]
        new = refs[2 * tiles + 9 : 2 * tiles + 18]
        g_ref, sum_ref, sem = refs[2 * tiles + 18 :]
        core, tile = ids_ref[0], ids_ref[1]
        copies = []
        for k, group in enumerate((near_refs, far_refs)):
            side = core if k == 0 else 1 - core
            for d in range(tiles):
                copies.append(
                    pltpu.make_async_copy(group[d], g_ref.at[side, tile ^ d], sem.at[k * tiles + d])
                )
        for copy in copies:
            copy.start()
        for copy in copies:
            copy.wait()
        at = 0
        for n in range(3):
            piece = plan.skip_piece if n == 2 else plan.piece
            rows = 2 * tiles * piece
            for side in range(2):
                for t in range(tiles):
                    row = (side * tiles + t) * piece
                    sum_ref[row : row + piece] = g_ref[side, t, at : at + piece].astype(F32)
            at += piece
            rate = (rows * plan.ranks) ** (-0.5)
            done = adamw(*(state[3 * n + k][...] for k in range(3)), sum_ref[0:rows], rate)
            for k in range(3):
                new[3 * n + k][...] = done[k]

    return pl.pallas_call(
        kernel,
        in_specs=[SMEM] + [ANY] * (2 * tiles) + [VMEM] * 9,
        out_specs=[VMEM] * 9,
        out_shape=[jax.ShapeDtypeStruct(v.shape, F32) for v in sets],
        scratch_shapes=[
            pltpu.VMEM((2, tiles, plan.chunk, c), BF),
            pltpu.VMEM((plan.shard, c), F32),
            pltpu.SemaphoreType.DMA((2 * tiles,)),
        ],
        compiler_params=params(),
        name="update",
    )(ids, *near, *far, *sets)


def send(v, axis, size, step):
    if axis == "fsdp":
        pairs = [(i, (i + step) % size) for i in range(size)]
    else:
        pairs = [(i, i ^ step) for i in range(size)]
    return lax.ppermute(v, axis, pairs)


def total(*parts):
    acc = parts[0].astype(F32)
    for part in parts[1:]:
        acc = acc + part.astype(F32)
    return acc.astype(BF)


def make_body(sizes):
    tiles, ranks = sizes["tile"], sizes["fsdp"]

    def to_core(v):
        return send(v, "core", 2, 1)

    def to_tile(v, d):
        return send(v, "tile", tiles, d)

    def to_rank(v, d):
        return send(v, "fsdp", ranks, d)

    def per_device(
        inputs,
        cotangent,
        lengths,
        face_table,
        w_first,
        w_second,
        w_skip,
        mom_first,
        sq_first,
        mom_second,
        sq_second,
        mom_skip,
        sq_skip,
    ):
        plan = Plan(sizes, inputs.shape[-1])
        x = jnp.transpose(inputs[0], (1, 2, 3, 0, 4))
        cot = jnp.transpose(cotangent[0], (1, 2, 3, 0, 4))
        table = face_table.T
        ids = jnp.stack([lax.axis_index(n) for n in ("core", "tile", "fsdp")]).astype(jnp.int32)
        low1, half1, low2, low3, half2 = pack(plan, ids, w_first, w_second, w_skip)
        near1 = [to_rank(half1, d) for d in range(1, ranks)]
        near2 = [to_rank(half2, d) for d in range(1, ranks)]
        x, cot, _ = lax.optimization_barrier((x, cot, half1))
        xp, go, dws = enter(lengths, table, x, cot)
        far1 = [to_core(v) for v in near1]
        hp, slope, w1 = first(plan, ids, table, xp, low1, near1, far1)
        hp, near2 = lax.optimization_barrier((hp, near2))
        far2 = [to_core(v) for v in near2]
        output, op, ws, keep, away = second(
            plan, ids, table, hp, slope, xp, go, dws, low2, low3, near2, far2
        )
        came = to_core(away)
        parts = [total(keep[d], came[d]) for d in range(tiles)]
        op, parts = lax.optimization_barrier((op, parts))
        came = [to_tile(parts[d], d) for d in range(1, tiles)]
        grad_inputs = inputs_back(op, w1, ws, go)
        came, grad_inputs = lax.optimization_barrier((came, grad_inputs))
        parts = [total(parts[0][r], *(v[r] for v in came)) for r in range(ranks)]
        came = [to_rank(parts[d], d) for d in range(1, ranks)]
        mine = total(parts[0], *came)
        near = [mine] + [to_tile(mine, d) for d in range(1, tiles)]
        far = [to_core(v) for v in near]
        news = update(
            plan,
            ids,
            near,
            far,
            (
                w_first,
                mom_first,
                sq_first,
                w_second,
                mom_second,
                sq_second,
                w_skip,
                mom_skip,
                sq_skip,
            ),
        )
        output = jnp.transpose(output, (3, 0, 1, 2, 4))[None]
        grad_inputs = jnp.transpose(grad_inputs, (3, 0, 1, 2, 4))[None]
        return (output, grad_inputs, *news)

    return per_device


def solution(mesh):
    pairs = mesh.shape["dp"] // 2
    ranks = mesh.shape["fsdp"]
    fine = Mesh(mesh.devices.reshape(pairs, 2, ranks), ("tile", "core", "fsdp"))
    sizes = {"tile": pairs, "core": 2, "fsdp": ranks}
    every = ("tile", "core", "fsdp")
    fields = P(every, None, None, None, None, None)
    rows = P("fsdp", None)
    return jax.shard_map(
        make_body(sizes),
        mesh=fine,
        in_specs=(fields, fields, P(every), P()) + (rows,) * 9,
        out_specs=(fields, fields) + (rows,) * 9,
        check_vma=False,
    )
```

```python
import functools

import jax
import jax.numpy as jnp
from jax import lax
from jax.experimental import pallas as pl
from jax.experimental.pallas import tpu as pltpu
from jax.sharding import Mesh
from jax.sharding import PartitionSpec as P

STEP_COUNT = 10
BF = jnp.bfloat16
F32 = jnp.float32
FS = 6
ROLL = 8
FACES = 12
GELU_K = 0.7978845608028654
GELU_C = 0.044715
VMEM_LIMIT = 26 * 2**20


ANY = pl.BlockSpec(memory_space=pl.ANY)
HBM = pl.BlockSpec(memory_space=pltpu.HBM)
VMEM = pl.BlockSpec(memory_space=pltpu.VMEM)
SMEM = pl.BlockSpec(memory_space=pltpu.SMEM)


def field(c, dtype=BF):
    return jax.ShapeDtypeStruct((FACES, FS, FS, ROLL, c), dtype)


def padded(c):
    return (FACES, FS + 2, FS + 2, ROLL, c)


def inner(ref):
    return ref.at[:, 1 : FS + 1, 1 : FS + 1]


def in_hbm(v):
    return pltpu.with_memory_space_constraint(v, pltpu.HBM)


def params():
    return pltpu.CompilerParams(vmem_limit_bytes=VMEM_LIMIT)


def cost(gflop, mbyte):
    return pl.CostEstimate(flops=int(gflop * 1e9), bytes_accessed=int(mbyte * 1e6), transcendentals=0)


def gelu_both(v):
    a = (GELU_K * GELU_C) * (v * v) + GELU_K
    half = 0.5 * jnp.tanh(v * a) + 0.5
    value = v * half
    return value, half + (value * (1.0 - half)) * (6.0 * a - 4.0 * GELU_K)


def window(p_ref, face, a, b):
    return p_ref[face, a : a + FS, b : b + FS].reshape(FS * FS * ROLL, p_ref.shape[-1])


def conv(p_ref, w_ref, face):
    c = w_ref.shape[1]
    acc = None
    for a in range(3):
        for b in range(3):
            t = 3 * a + b
            part = jnp.dot(
                window(p_ref, face, a, b), w_ref[t * c : (t + 1) * c], preferred_element_type=F32
            )
            acc = part if acc is None else acc + part
    return acc


def dot_back(v, w):
    return lax.dot_general(v, w, (((1,), (1,)), ((), ())), preferred_element_type=F32)


def conv_back(g_ref, w_ref, face):
    c = w_ref.shape[1]
    acc = None
    for a in range(3):
        for b in range(3):
            t = 3 * a + b
            part = dot_back(window(g_ref, face, 2 - a, 2 - b), w_ref[t * c : (t + 1) * c])
            acc = part if acc is None else acc + part
    return acc


def outer(p, g):
    c = p.shape[-1]
    return lax.dot_general(
        p.reshape(-1, c), g.reshape(-1, c), (((0,), (0,)), ((), ())), preferred_element_type=F32
    )


def zero_corners(p_ref):
    zero = jnp.zeros((FACES, 1, 1, ROLL, p_ref.shape[-1]), p_ref.dtype)
    for i in (0, FS + 1):
        for j in (0, FS + 1):
            p_ref[:, i : i + 1, j : j + 1] = zero


def neighbour(ids_ref, side, face):
    return ids_ref[4 + side * FACES + face]


def fill_halo(ids_ref, p_ref):
    for face in range(FACES):
        p_ref[face, 0, 1 : FS + 1] = p_ref[neighbour(ids_ref, 0, face), FS, 1 : FS + 1]
        p_ref[face, 1 : FS + 1, FS + 1] = p_ref[neighbour(ids_ref, 1, face), 1 : FS + 1, 1]
        p_ref[face, FS + 1, 1 : FS + 1] = p_ref[neighbour(ids_ref, 2, face), 1, 1 : FS + 1]
        p_ref[face, 1 : FS + 1, 0] = p_ref[neighbour(ids_ref, 3, face), 1 : FS + 1, FS]
    zero_corners(p_ref)


def add_edges(e_ref, ids_ref, face, v):
    for side, part in enumerate((v[0], v[:, FS - 1], v[FS - 1], v[:, 0])):
        to = neighbour(ids_ref, side, face)
        e_ref[to, side] = e_ref[to, side] + part


def fill_halo_back(e_ref, p_ref):
    for face in range(FACES):
        p_ref[face, FS + 1, 1 : FS + 1] = e_ref[face, 0].astype(p_ref.dtype)
        p_ref[face, 1 : FS + 1, 0] = e_ref[face, 1].astype(p_ref.dtype)
        p_ref[face, 0, 1 : FS + 1] = e_ref[face, 2].astype(p_ref.dtype)
        p_ref[face, 1 : FS + 1, FS + 1] = e_ref[face, 3].astype(p_ref.dtype)
    zero_corners(p_ref)


def edge_sums(c):
    return pltpu.VMEM((FACES, 4, FS, ROLL, c), F32)


class Plan:
    def __init__(self, sizes, channels):
        self.tiles, self.ranks = sizes["tile"], sizes["fsdp"]
        self.c = channels
        self.conv = 9 * channels
        self.shard = self.conv // self.ranks
        self.skip_shard = channels // self.ranks
        self.piece = self.shard // (2 * self.tiles)
        self.skip_piece = self.skip_shard // (2 * self.tiles)
        self.late = self.piece + self.skip_piece
        self.chunk = self.piece + self.late
        self.split = self.piece % 8 == 0 and self.skip_piece % 8 == 0
        if self.split:
            self.sent = self.piece, self.piece, self.skip_piece
        else:
            self.sent = self.shard // 2, self.shard // 2, self.skip_shard // 2


def place_rows(plan, ids_ref, dst_ref, value, first_row, piece, offset):
    core, tile, rank = ids_ref[0], ids_ref[1], ids_ref[2]
    end = first_row + value.shape[0]
    row = first_row
    while row < end:
        number = row // piece
        stop = min(end, (number + 1) * piece)
        to_tile = number % plan.tiles
        to_core = number // plan.tiles % 2
        to_rank = number // (2 * plan.tiles)
        at = offset + row - number * piece
        dst_ref[
            to_core ^ core,
            to_tile ^ tile,
            (to_rank + plan.ranks - rank) % plan.ranks,
            at : at + stop - row,
        ] = value[row - first_row : stop - first_row]
        row = stop


def weight_grad(plan, ids_ref, p_ref, g, dst_ref):
    c = p_ref.shape[-1]
    for a in range(3):
        for b in range(3):
            part = outer(p_ref[:, a : a + FS, b : b + FS], g).astype(BF)
            place_rows(plan, ids_ref, dst_ref, part, (3 * a + b) * c, plan.piece, 0)


def pack(plan, ids, one, two, skip):
    c = plan.c
    sizes = plan.sent

    def kernel(ids_ref, one_hbm, two_hbm, skip_hbm, one_ref, two_ref, rows_ref, sem):
        loads = []
        at = 0
        for k, (hbm, rows) in enumerate(zip((one_hbm, two_hbm, skip_hbm), sizes)):
            start = ids_ref[0] * (hbm.shape[0] // 2)
            if plan.split:
                start = start + ids_ref[1] * rows
            source = hbm.at[pl.ds(pl.multiple_of(start, 8), rows)]
            loads.append(pltpu.make_async_copy(source, rows_ref.at[pl.ds(at, rows)], sem.at[k]))
            at += rows
        for load in loads:
            load.start()
        for load in loads:
            load.wait()
        one_ref[...] = rows_ref[: sizes[0]].astype(BF)
        two_ref[...] = rows_ref[sizes[0] :].astype(BF)

    return pl.pallas_call(
        kernel,
        in_specs=[SMEM, HBM, HBM, HBM],
        out_specs=[VMEM] * 2,
        out_shape=[jax.ShapeDtypeStruct((v, c), BF) for v in (sizes[0], sizes[1] + sizes[2])],
        scratch_shapes=[pltpu.VMEM((sum(sizes), c), F32), pltpu.SemaphoreType.DMA((3,))],
        compiler_params=params(),
        cost_estimate=cost(0, 0.3),
        name="pack",
    )(ids, in_hbm(one), in_hbm(two), in_hbm(skip))


def join_rows(plan, ids_ref, low_ref, pieces, w_ref, rows):
    rank = ids_ref[2]
    w_ref[pl.ds(pl.multiple_of(rank * rows, 8), rows)] = low_ref[...]
    for ref, index, d, row in pieces:
        start = (rank + plan.ranks - d) % plan.ranks * rows + row
        part = ref[index]
        w_ref[pl.ds(pl.multiple_of(start, 8), part.shape[0])] = part


def received(plan, ids_ref, near_refs, far_refs, at, rows, shard):
    core, tile = ids_ref[0], ids_ref[1]
    pieces = []
    for side, group in ((core, near_refs), (1 - core, far_refs)):
        for e, ref in enumerate(group):
            row = side * (shard // 2)
            if plan.split:
                row = row + (tile ^ e) * rows
            pieces += [(ref, (d - 1, pl.ds(at, rows)), d, row) for d in range(1, plan.ranks)]
    return pieces


def enter(plan, ids, x, cot, weights, after):
    c = plan.c

    def kernel(ids_ref, x_hbm, cot_hbm, *refs):
        refs = refs[:3] + refs[3 + len(after) :]
        weights_hbm, xp_ref, go_ref, dw_ref = refs[:3], *refs[3:6]
        low_refs, cot_ref, weight_refs, sem = refs[6:9], refs[9], refs[10:13], refs[13]
        load_x = pltpu.make_async_copy(x_hbm, inner(xp_ref), sem.at[FACES])
        load_x.start()
        loads = []
        for face in range(FACES):
            loads.append(pltpu.make_async_copy(cot_hbm.at[face], cot_ref.at[face], sem.at[face]))
            loads[-1].start()
        low_loads = []
        for k in range(3):
            low_loads.append(
                pltpu.make_async_copy(weights_hbm[k], weight_refs[k], sem.at[FACES + 1 + k])
            )
            low_loads[-1].start()
        live = lax.broadcasted_iota(jnp.int32, (FS, FS, ROLL, c), 2) < ids_ref[3]
        for face in range(FACES):
            loads[face].wait()
            go_ref[face] = jnp.where(live, cot_ref[face].astype(F32), 0.0).astype(BF)
        load_x.wait()
        fill_halo(ids_ref, xp_ref)
        dw_ref[...] = outer(xp_ref[:, 1 : FS + 1, 1 : FS + 1], go_ref[...]).astype(dw_ref.dtype)
        for k in range(3):
            low_loads[k].wait()
            low_refs[k][...] = weight_refs[k][...].astype(BF)

    return pl.pallas_call(
        kernel,
        in_specs=[SMEM] + [HBM] * 5 + [VMEM] * len(after),
        out_specs=[VMEM] * 6,
        out_shape=[
            jax.ShapeDtypeStruct(padded(c), BF),
            field(c),
            jax.ShapeDtypeStruct((c, c), BF),
            *(jax.ShapeDtypeStruct(v.shape, BF) for v in weights),
        ],
        scratch_shapes=[
            pltpu.VMEM(field(c).shape, BF),
            *(pltpu.VMEM(v.shape, F32) for v in weights),
            pltpu.SemaphoreType.DMA((FACES + 4,)),
        ],
        compiler_params=params(),
        cost_estimate=cost(0.6, 9),
        name="enter",
    )(ids, in_hbm(x), in_hbm(cot), *(in_hbm(v) for v in weights), *after)


def first(plan, ids, xp, low, near, far):
    c = plan.c
    count = len(near)

    def kernel(ids_ref, xp_ref, low_ref, *refs):
        near_refs, far_refs = refs[:count], refs[count : 2 * count]
        hp_ref, slope_ref, w_ref = refs[2 * count :]
        pieces = received(plan, ids_ref, near_refs, far_refs, 0, plan.sent[0], plan.shard)
        join_rows(plan, ids_ref, low_ref, pieces, w_ref, plan.shard)
        for face in range(FACES):
            hidden, slope = gelu_both(conv(xp_ref, w_ref, face))
            hp_ref[face, 1 : FS + 1, 1 : FS + 1] = hidden.astype(BF).reshape(FS, FS, ROLL, c)
            slope_ref[face] = slope.astype(BF).reshape(FS, FS, ROLL, c)
        fill_halo(ids_ref, hp_ref)

    return pl.pallas_call(
        kernel,
        in_specs=[SMEM] + [VMEM] * (2 + 2 * count),
        out_specs=[VMEM] * 3,
        out_shape=[
            jax.ShapeDtypeStruct(padded(c), BF),
            field(c),
            jax.ShapeDtypeStruct((plan.conv, c), BF),
        ],
        compiler_params=params(),
        cost_estimate=cost(4.1, 12),
        name="first",
    )(ids, xp, low, *near, *far)


def second(plan, ids, hp, xp, go, dws, low, low_skip, near, far):
    c = plan.c
    count = len(near)

    def kernel(ids_ref, hp_ref, xp_ref, go_ref, dws_ref, low_ref, lows_ref, *refs):
        near_refs, far_refs = refs[:count], refs[count : 2 * count]
        out_hbm, gp_ref, w_ref, ws_ref, keep_ref, send_ref = refs[2 * count : 2 * count + 6]
        out_ref, e_ref, dw_ref, sem_out = refs[2 * count + 6 :]
        pieces = received(plan, ids_ref, near_refs, far_refs, 0, plan.sent[1], plan.shard)
        join_rows(plan, ids_ref, low_ref, pieces, w_ref, plan.shard)
        pieces = received(plan, ids_ref, near_refs, far_refs, *plan.sent[1:], plan.skip_shard)
        join_rows(plan, ids_ref, lows_ref, pieces, ws_ref, plan.skip_shard)
        e_ref[...] = jnp.zeros_like(e_ref)
        place_rows(plan, ids_ref, dw_ref, dws_ref[...], 0, plan.skip_piece, plan.piece)
        for face in range(FACES):
            value, slope = gelu_both(conv(hp_ref, w_ref, face))
            value = value + jnp.dot(
                xp_ref[face, 1 : FS + 1, 1 : FS + 1].reshape(-1, c),
                ws_ref[...],
                preferred_element_type=F32,
            )
            out_ref[face] = value.astype(BF).reshape(FS, FS, ROLL, c)
            low_grad = (go_ref[face].astype(F32) * slope.reshape(FS, FS, ROLL, c)).astype(BF)
            gp_ref[face, 1 : FS + 1, 1 : FS + 1] = low_grad
            add_edges(e_ref, ids_ref, face, low_grad.astype(F32))
        store = pltpu.make_async_copy(out_ref, out_hbm, sem_out)
        store.start()
        weight_grad(plan, ids_ref, hp_ref, gp_ref[:, 1 : FS + 1, 1 : FS + 1], dw_ref)
        keep_ref[...] = dw_ref[0]
        send_ref[...] = dw_ref[1]
        fill_halo_back(e_ref, gp_ref)
        store.wait()

    sums = jax.ShapeDtypeStruct((plan.tiles, plan.ranks, plan.late, c), BF)
    return pl.pallas_call(
        kernel,
        in_specs=[SMEM] + [VMEM] * (6 + 2 * count),
        out_specs=[HBM] + [VMEM] * 5,
        out_shape=[
            field(c),
            jax.ShapeDtypeStruct(padded(c), BF),
            jax.ShapeDtypeStruct((plan.conv, c), BF),
            jax.ShapeDtypeStruct((c, c), BF),
            sums,
            sums,
        ],
        scratch_shapes=[
            pltpu.VMEM(field(c).shape, BF),
            edge_sums(c),
            pltpu.VMEM((2,) + sums.shape, BF),
            pltpu.SemaphoreType.DMA,
        ],
        compiler_params=params(),
        cost_estimate=cost(9, 16),
        name="second",
    )(ids, hp, xp, go, dws, low, low_skip, *near, *far)


def hidden_back_kernel(ids_ref, gp_ref, w_ref, slope_ref, op_ref, e_ref):
    c = w_ref.shape[1]
    e_ref[...] = jnp.zeros_like(e_ref)
    for face in range(FACES):
        grad = conv_back(gp_ref, w_ref, face).reshape(FS, FS, ROLL, c)
        low_grad = (grad * slope_ref[face].astype(F32)).astype(BF)
        op_ref[face, 1 : FS + 1, 1 : FS + 1] = low_grad
        add_edges(e_ref, ids_ref, face, low_grad.astype(F32))
    fill_halo_back(e_ref, op_ref)


def hidden_back(ids, gp, w, slope):
    c = w.shape[1]
    return pl.pallas_call(
        hidden_back_kernel,
        in_specs=[SMEM] + [VMEM] * 3,
        out_specs=VMEM,
        out_shape=jax.ShapeDtypeStruct(padded(c), BF),
        scratch_shapes=[edge_sums(c)],
        compiler_params=params(),
        cost_estimate=cost(4.1, 9),
        name="hidden_back",
    )(ids, gp, w, slope)


def first_grad(plan, ids, xp, op):
    def kernel(ids_ref, xp_ref, op_ref, keep_ref, send_ref, dw_ref):
        weight_grad(plan, ids_ref, xp_ref, op_ref[:, 1 : FS + 1, 1 : FS + 1], dw_ref)
        keep_ref[...] = dw_ref[0]
        send_ref[...] = dw_ref[1]

    sums = jax.ShapeDtypeStruct((plan.tiles, plan.ranks, plan.piece, plan.c), BF)
    return pl.pallas_call(
        kernel,
        in_specs=[SMEM, VMEM, VMEM],
        out_specs=[VMEM] * 2,
        out_shape=[sums, sums],
        scratch_shapes=[pltpu.VMEM((2,) + sums.shape, BF)],
        compiler_params=params(),
        cost_estimate=cost(4.1, 9),
        name="first_grad",
    )(ids, xp, op)


def tile_sums(plan, early, late):
    tiles, ranks, piece = plan.tiles, plan.ranks, plan.piece

    def kernel(*refs):
        for r in range(ranks):
            to = refs[2 * tiles + r]
            for at, group in ((0, refs[:tiles]), (piece, refs[tiles : 2 * tiles])):
                acc = group[0][r].astype(F32)
                for ref in group[1:]:
                    acc = acc + ref[r].astype(F32)
                to[at : at + acc.shape[0]] = acc.astype(BF)

    return pl.pallas_call(
        kernel,
        in_specs=[VMEM] * (2 * tiles),
        out_specs=[VMEM] * ranks,
        out_shape=[jax.ShapeDtypeStruct((plan.chunk, plan.c), BF)] * ranks,
        compiler_params=params(),
        cost_estimate=cost(0, 6),
        name="tile_sums",
    )(*early, *late)


def inputs_back_kernel(gp_ref, w_ref, ws_ref, go_ref, out_hbm, out_ref, sem):
    c = w_ref.shape[1]
    stores = []
    for face in range(FACES):
        grad = conv_back(gp_ref, w_ref, face)
        grad = grad + dot_back(go_ref[face].reshape(-1, c), ws_ref[...])
        out_ref[face] = grad.reshape(FS, FS, ROLL, c)
        stores.append(pltpu.make_async_copy(out_ref.at[face], out_hbm.at[face], sem.at[face]))
        stores[-1].start()
    for store in stores:
        store.wait()


def inputs_back(gp, w, ws, go):
    c = w.shape[1]
    return pl.pallas_call(
        inputs_back_kernel,
        in_specs=[VMEM] * 4,
        out_specs=ANY,
        out_shape=field(c, F32),
        scratch_shapes=[pltpu.VMEM(field(c).shape, F32), pltpu.SemaphoreType.DMA((FACES,))],
        compiler_params=params(),
        cost_estimate=cost(4.6, 10),
        name="inputs_back",
    )(gp, w, ws, go)


def adamw(weight, moment, square, grad, rate):
    moment_new = 0.9 * moment + 0.1 * grad
    square_new = 0.999 * square + 0.001 * grad * grad
    fix_one = 1.0 - 0.9**STEP_COUNT
    fix_two = 1.0 - 0.999**STEP_COUNT
    weight_new = weight - rate * (
        moment_new / fix_one / (jnp.sqrt(square_new / fix_two) + 1e-08) + 0.01 * weight
    )
    return (weight_new, moment_new, square_new)


UPDATE_STEPS = 4


def update(plan, ids, near, far, sets):
    c, tiles = plan.c, plan.tiles

    def kernel(ids_ref, *refs):
        groups, state, new, sum_ref = refs[:2], refs[2:11], refs[11:20], refs[20]
        done_refs, sem = refs[21:30], refs[30]
        core, tile = ids_ref[0], ids_ref[1]
        at = 0
        stores = []
        for n in range(3):
            piece = plan.skip_piece if n == 2 else plan.piece
            rows = 2 * tiles * piece
            for k, group in enumerate(groups):
                side = core if k == 0 else 1 - core
                for d in range(tiles):
                    part = group[d, at : at + piece].astype(F32)
                    if piece % 8:
                        for t in range(2 * tiles):

                            def put(part=part, t=t, piece=piece):
                                sum_ref[t * piece : (t + 1) * piece] = part

                            pl.when(side * tiles + (tile ^ d) == t)(put)
                    else:
                        start = pl.multiple_of((side * tiles + (tile ^ d)) * piece, 8)
                        sum_ref[pl.ds(start, piece)] = part
            at += piece
            rate = (rows * plan.ranks) ** (-0.5)
            step = rows // UPDATE_STEPS if rows % (8 * UPDATE_STEPS) == 0 else rows
            for row in range(0, rows, step):
                old = (state[3 * n + k][row : row + step] for k in range(3))
                done = adamw(*old, sum_ref[row : row + step], rate)
                for k in range(3 * n, 3 * n + 3):
                    done_refs[k][row : row + step] = done[k - 3 * n]
                    source = done_refs[k].at[pl.ds(row, step)]
                    target = new[k].at[pl.ds(row, step)]
                    number = UPDATE_STEPS * k + row // step
                    stores.append(pltpu.make_async_copy(source, target, sem.at[number]))
                    stores[-1].start()
        for store in stores:
            store.wait()

    shapes = [v.shape for v in sets]
    return pl.pallas_call(
        kernel,
        in_specs=[SMEM] + [VMEM] * 11,
        out_specs=[HBM] * 9,
        out_shape=[jax.ShapeDtypeStruct(v, F32) for v in shapes],
        scratch_shapes=[
            pltpu.VMEM((plan.shard, c), F32),
            *(pltpu.VMEM(v, F32) for v in shapes),
            pltpu.SemaphoreType.DMA((9 * UPDATE_STEPS,)),
        ],
        compiler_params=params(),
        cost_estimate=cost(0, 9),
        name="update",
    )(ids, near, far, *sets)


def send(v, axis, size, step):
    if axis == "fsdp":
        pairs = [(i, (i + step) % size) for i in range(size)]
    else:
        pairs = [(i, i ^ step) for i in range(size)]
    return lax.ppermute(v, axis, pairs)


def total(*parts):
    acc = parts[0].astype(F32)
    for part in parts[1:]:
        acc = acc + part.astype(F32)
    return acc.astype(BF)


def make_body(sizes):
    tiles, ranks = sizes["tile"], sizes["fsdp"]

    def to_core(v):
        return send(v, "core", 2, 1)

    def to_tile(v, d):
        return send(v, "tile", tiles, d)

    def to_rank(v, d):
        return send(v, "fsdp", ranks, d)

    def per_device(
        inputs,
        cotangent,
        lengths,
        face_table,
        w_first,
        w_second,
        w_skip,
        mom_first,
        sq_first,
        mom_second,
        sq_second,
        mom_skip,
        sq_skip,
    ):
        plan = Plan(sizes, inputs.shape[-1])
        x = jnp.transpose(inputs[0], (1, 2, 3, 0, 4))
        cot = jnp.transpose(cotangent[0], (1, 2, 3, 0, 4))
        places = jnp.stack([lax.axis_index(n) for n in ("core", "tile", "fsdp")]).astype(jnp.int32)
        weights = w_first, w_second, w_skip
        groups = []
        for sent in pack(plan, places, *weights):
            own = jnp.stack([to_rank(sent, d) for d in range(1, ranks)])
            groups.append([own])
            if plan.split:
                groups[-1] += [to_tile(own, e) for e in range(1, tiles)]
        near1, near2 = groups
        ids = jnp.concatenate([places, lengths, face_table.T.reshape(-1)])
        xp, go, dws, low1, low2, low3 = enter(plan, ids, x, cot, weights, (near1[0], near2[0]))
        xp, near1 = lax.optimization_barrier((xp, near1))
        far1 = [to_core(v) for v in near1]
        hp, slope, w1 = first(plan, ids, xp, low1, near1, far1)
        hp, near2 = lax.optimization_barrier((hp, near2))
        far2 = [to_core(v) for v in near2]
        hp, far2 = lax.optimization_barrier((hp, far2))
        output, gp, w2, ws, keep2, away2 = second(
            plan, ids, hp, xp, go, dws, low2, low3, near2, far2
        )
        came2 = to_core(away2)
        op = hidden_back(ids, gp, w2, slope)
        came2, op = lax.optimization_barrier((came2, op))
        parts2 = [total(keep2[d], came2[d]) for d in range(tiles)]
        op, parts2 = lax.optimization_barrier((op, parts2))
        late = [parts2[0]] + [to_tile(parts2[d], d) for d in range(1, tiles)]
        keep1, away1 = first_grad(plan, ids, xp, op)
        late, away1 = lax.optimization_barrier((late, away1))
        came1 = to_core(away1)
        parts1 = [total(keep1[d], came1[d]) for d in range(tiles)]
        op, parts1 = lax.optimization_barrier((op, parts1))
        early = [parts1[0]] + [to_tile(parts1[d], d) for d in range(1, tiles)]
        grad_inputs = inputs_back(op, w1, ws, go)
        early, late, grad_inputs = lax.optimization_barrier((early, late, grad_inputs))
        parts = tile_sums(plan, early, late)
        came = [to_rank(parts[d], d) for d in range(1, ranks)]
        mine = total(parts[0], *came)
        near = jnp.stack([mine] + [to_tile(mine, d) for d in range(1, tiles)])
        far = to_core(near)
        news = update(
            plan,
            ids,
            near,
            far,
            (
                w_first,
                mom_first,
                sq_first,
                w_second,
                mom_second,
                sq_second,
                w_skip,
                mom_skip,
                sq_skip,
            ),
        )
        output = jnp.transpose(output, (3, 0, 1, 2, 4))[None]
        grad_inputs = jnp.transpose(grad_inputs, (3, 0, 1, 2, 4))[None]
        return (output, grad_inputs, *news)

    return per_device


def solution(mesh):
    pairs = mesh.shape["dp"] // 2
    ranks = mesh.shape["fsdp"]
    fine = Mesh(mesh.devices.reshape(pairs, 2, ranks), ("tile", "core", "fsdp"))
    sizes = {"tile": pairs, "core": 2, "fsdp": ranks}
    every = ("tile", "core", "fsdp")
    fields = P(every, None, None, None, None, None)
    rows = P("fsdp", None)
    return jax.shard_map(
        make_body(sizes),
        mesh=fine,
        in_specs=(fields, fields, P(every), P()) + (rows,) * 9,
        out_specs=(fields, fields) + (rows,) * 9,
        check_vma=False,
    )
```

```python
import functools

import jax
import jax.numpy as jnp
from jax import lax
from jax.experimental import pallas as pl
from jax.experimental.pallas import tpu as pltpu
from jax.sharding import Mesh
from jax.sharding import PartitionSpec as P

STEP_COUNT = 10
BF = jnp.bfloat16
F32 = jnp.float32
FS = 6
ROLL = 8
FACES = 12
GELU_K = 0.7978845608028654
GELU_C = 0.044715
VMEM_LIMIT = 30 * 2**20
GROUP = 2


ANY = pl.BlockSpec(memory_space=pl.ANY)
HBM = pl.BlockSpec(memory_space=pltpu.HBM)
VMEM = pl.BlockSpec(memory_space=pltpu.VMEM)
SMEM = pl.BlockSpec(memory_space=pltpu.SMEM)


def field(c, dtype=BF):
    return jax.ShapeDtypeStruct((FACES, FS, FS, ROLL, c), dtype)


def padded(c):
    return (FACES, FS + 2, FS + 2, ROLL, c)


def inner(ref):
    return ref.at[:, 1 : FS + 1, 1 : FS + 1]


def in_hbm(v):
    return pltpu.with_memory_space_constraint(v, pltpu.HBM)


def params():
    return pltpu.CompilerParams(vmem_limit_bytes=VMEM_LIMIT)


def cost(gflop, mbyte):
    return pl.CostEstimate(flops=int(gflop * 1e9), bytes_accessed=int(mbyte * 1e6), transcendentals=0)


def gelu_both(v):
    a = (GELU_K * GELU_C) * (v * v) + GELU_K
    half = 0.5 * jnp.tanh(v * a) + 0.5
    value = v * half
    return value, half + (value * (1.0 - half)) * (6.0 * a - 4.0 * GELU_K)


def pair_shape(c):
    return (4, FS // 2, FACES, FS + 2, ROLL, c)


def grad_pairs(c):
    return (4, FS // 2, FACES, FS, ROLL, c)


def pair_rows(p_ref, v_ref, face, count):
    for t in range(FS // 2):
        d0, d1, d2, d3 = (p_ref[face : face + count, 2 * t + q] for q in range(4))
        v_ref[0, t, face : face + count] = d0 - d2
        v_ref[1, t, face : face + count] = d1 + d2
        v_ref[2, t, face : face + count] = d2 - d1
        v_ref[3, t, face : face + count] = d1 - d3


def pair_weights(w_ref, u_ref):
    c = w_ref.shape[1]
    for b in range(3):
        g0, g1, g2 = (w_ref[(3 * a + b) * c : (3 * a + b + 1) * c].astype(F32) for a in range(3))
        outside, middle = 0.5 * (g0 + g2), 0.5 * g1
        u_ref[0, b] = (outside + middle).astype(BF)
        u_ref[1, b] = (outside - middle).astype(BF)


def dot_back(v, w):
    return lax.dot_general(v, w, (((1,), (1,)), ((), ())), preferred_element_type=F32)


def conv(v_ref, w_ref, u_ref, face, count, back=False):
    c = w_ref.shape[1]
    products = []
    for k in range(4):
        acc = None
        for b in range(3):
            v = v_ref[k, :, face : face + count, b : b + FS].reshape(-1, c)
            col = 2 - b if back else b
            if k in (0, 3):
                t = 3 * (2 if (k == 3) != back else 0) + col
                g = w_ref[t * c : (t + 1) * c]
            else:
                g = u_ref[k - 1, col]
            part = dot_back(v, g) if back else jnp.dot(v, g, preferred_element_type=F32)
            acc = part if acc is None else acc + part
        products.append(acc.reshape(FS // 2, count, FS, ROLL, c))
    m0, m1, m2, m3 = products
    even, odd = m0 + m1 + m2, m1 - m2 - m3
    return [(odd if i % 2 else even)[i // 2] for i in range(FS)]


def by_rows(ref, face, count, first_row, first_col):
    cols = slice(first_col, first_col + FS)
    rows = [ref[face : face + count, first_row + i, cols] for i in range(FS)]
    return jnp.stack(rows).reshape(-1, ref.shape[-1])


def outer(p, g):
    c = p.shape[-1]
    return lax.dot_general(
        p.reshape(-1, c), g.reshape(-1, c), (((0,), (0,)), ((), ())), preferred_element_type=F32
    )


def zero_corners(p_ref):
    zero = jnp.zeros((FACES, 1, 1, ROLL, p_ref.shape[-1]), p_ref.dtype)
    for i in (0, FS + 1):
        for j in (0, FS + 1):
            p_ref[:, i : i + 1, j : j + 1] = zero


def neighbour(ids_ref, side, face):
    return ids_ref[4 + side * FACES + face]


def fill_halo(ids_ref, p_ref):
    for face in range(FACES):
        p_ref[face, 0, 1 : FS + 1] = p_ref[neighbour(ids_ref, 0, face), FS, 1 : FS + 1]
        p_ref[face, 1 : FS + 1, FS + 1] = p_ref[neighbour(ids_ref, 1, face), 1 : FS + 1, 1]
        p_ref[face, FS + 1, 1 : FS + 1] = p_ref[neighbour(ids_ref, 2, face), 1, 1 : FS + 1]
        p_ref[face, 1 : FS + 1, 0] = p_ref[neighbour(ids_ref, 3, face), 1 : FS + 1, FS]
    zero_corners(p_ref)


def add_edges(e_ref, ids_ref, face, p_ref):
    rows = cols = slice(1, FS + 1)
    edges = (p_ref[face, 1, cols], p_ref[face, rows, FS], p_ref[face, FS, cols], p_ref[face, rows, 1])
    for side, part in enumerate(edges):
        to = neighbour(ids_ref, side, face)
        e_ref[to, side] = e_ref[to, side] + part.astype(F32)


def fill_halo_back(e_ref, p_ref):
    for face in range(FACES):
        p_ref[face, FS + 1, 1 : FS + 1] = e_ref[face, 0].astype(p_ref.dtype)
        p_ref[face, 1 : FS + 1, 0] = e_ref[face, 1].astype(p_ref.dtype)
        p_ref[face, 0, 1 : FS + 1] = e_ref[face, 2].astype(p_ref.dtype)
        p_ref[face, 1 : FS + 1, FS + 1] = e_ref[face, 3].astype(p_ref.dtype)
    zero_corners(p_ref)


def edge_sums(c):
    return pltpu.VMEM((FACES, 4, FS, ROLL, c), F32)


class Plan:
    def __init__(self, sizes, channels):
        self.tiles, self.ranks = sizes["tile"], sizes["fsdp"]
        self.c = channels
        self.conv = 9 * channels
        self.shard = self.conv // self.ranks
        self.skip_shard = channels // self.ranks
        self.piece = self.shard // (2 * self.tiles)
        self.skip_piece = self.skip_shard // (2 * self.tiles)
        self.late = self.piece + self.skip_piece
        self.chunk = self.piece + self.late
        self.split = self.piece % 8 == 0 and self.skip_piece % 8 == 0
        if self.split:
            self.sent = self.piece, self.piece, self.skip_piece
        else:
            self.sent = self.shard // 2, self.shard // 2, self.skip_shard // 2


def place_rows(plan, ids_ref, dst_ref, value, first_row, piece, offset):
    core, tile, rank = ids_ref[0], ids_ref[1], ids_ref[2]
    end = first_row + value.shape[0]
    row = first_row
    while row < end:
        number = row // piece
        stop = min(end, (number + 1) * piece)
        to_tile = number % plan.tiles
        to_core = number // plan.tiles % 2
        to_rank = number // (2 * plan.tiles)
        at = offset + row - number * piece
        dst_ref[
            to_core ^ core,
            to_tile ^ tile,
            (to_rank + plan.ranks - rank) % plan.ranks,
            at : at + stop - row,
        ] = value[row - first_row : stop - first_row]
        row = stop


def weight_grad(plan, ids_ref, v_ref, g_ref, z_ref, dst_ref):
    c = plan.c
    halves = range(FS // 2)
    cols = slice(1, FS + 1)
    for t in halves:
        y0, y1 = g_ref[:, 2 * t + 1, cols], g_ref[:, 2 * t + 2, cols]
        z_ref[0, t] = y0
        z_ref[1, t] = (y0 + y1) * 0.5
        z_ref[2, t] = (y0 - y1) * 0.5
        z_ref[3, t] = y1
    for b in range(3):
        m0, m1, m2, m3 = (outer(v_ref[k, :, :, b : b + FS], z_ref[k]) for k in range(4))
        both = m1 + m2
        for a, part in enumerate((m0 + both, m1 - m2, both - m3)):
            place_rows(plan, ids_ref, dst_ref, part.astype(BF), (3 * a + b) * c, plan.piece, 0)


def pack(plan, ids, one, two, skip):
    c = plan.c
    sizes = plan.sent

    def kernel(ids_ref, one_hbm, two_hbm, skip_hbm, sent_ref, rows_ref, sem):
        loads = []
        at = 0
        for k, (hbm, rows) in enumerate(zip((one_hbm, two_hbm, skip_hbm), sizes)):
            start = ids_ref[0] * (hbm.shape[0] // 2)
            if plan.split:
                start = start + ids_ref[1] * rows
            source = hbm.at[pl.ds(pl.multiple_of(start, 8), rows)]
            loads.append(pltpu.make_async_copy(source, rows_ref.at[pl.ds(at, rows)], sem.at[k]))
            at += rows
        for load in loads:
            load.start()
        for load in loads:
            load.wait()
        sent_ref[...] = rows_ref[...].astype(BF)

    return pl.pallas_call(
        kernel,
        in_specs=[SMEM, HBM, HBM, HBM],
        out_specs=VMEM,
        out_shape=jax.ShapeDtypeStruct((sum(sizes), c), BF),
        scratch_shapes=[pltpu.VMEM((sum(sizes), c), F32), pltpu.SemaphoreType.DMA((3,))],
        compiler_params=params(),
        cost_estimate=cost(0, 0.3),
        name="pack",
    )(ids, in_hbm(one), in_hbm(two), in_hbm(skip))


def join_rows(plan, ids_ref, low_ref, pieces, w_ref, rows):
    rank = ids_ref[2]
    w_ref[pl.ds(pl.multiple_of(rank * rows, 8), rows)] = low_ref[...]
    for ref, index, d, row in pieces:
        start = (rank + plan.ranks - d) % plan.ranks * rows + row
        part = ref[index]
        w_ref[pl.ds(pl.multiple_of(start, 8), part.shape[0])] = part


def received(plan, ids_ref, near_refs, far_refs, at, rows, shard):
    core, tile = ids_ref[0], ids_ref[1]
    pieces = []
    for side, group in ((core, near_refs), (1 - core, far_refs)):
        for e, ref in enumerate(group):
            row = side * (shard // 2)
            if plan.split:
                row = row + (tile ^ e) * rows
            pieces += [(ref, (d - 1, pl.ds(at, rows)), d, row) for d in range(1, plan.ranks)]
    return pieces


def enter(plan, ids, x, cot, weights, after):
    c = plan.c

    def kernel(ids_ref, x_hbm, cot_hbm, *refs):
        refs = refs[:3] + refs[3 + len(after) :]
        weights_hbm, xp_ref, go_ref, dw_ref = refs[:3], *refs[3:6]
        low_refs, cot_ref, weight_refs, sem = refs[6:9], refs[9], refs[10:13], refs[13]
        load_x = pltpu.make_async_copy(x_hbm, inner(xp_ref), sem.at[FACES])
        load_x.start()
        loads = []
        for face in range(FACES):
            loads.append(pltpu.make_async_copy(cot_hbm.at[face], cot_ref.at[face], sem.at[face]))
            loads[-1].start()
        low_loads = []
        for k in range(3):
            low_loads.append(
                pltpu.make_async_copy(weights_hbm[k], weight_refs[k], sem.at[FACES + 1 + k])
            )
            low_loads[-1].start()
        live = lax.broadcasted_iota(jnp.int32, (FS, FS, ROLL, c), 2) < ids_ref[3]
        for face in range(FACES):
            loads[face].wait()
            go_ref[face] = jnp.where(live, cot_ref[face].astype(F32), 0.0).astype(BF)
        load_x.wait()
        fill_halo(ids_ref, xp_ref)
        dw_ref[...] = outer(xp_ref[:, 1 : FS + 1, 1 : FS + 1], go_ref[...]).astype(dw_ref.dtype)
        for k in range(3):
            low_loads[k].wait()
            low_refs[k][...] = weight_refs[k][...].astype(BF)

    return pl.pallas_call(
        kernel,
        in_specs=[SMEM] + [HBM] * 5 + [VMEM] * len(after),
        out_specs=[VMEM] * 6,
        out_shape=[
            jax.ShapeDtypeStruct(padded(c), BF),
            field(c),
            jax.ShapeDtypeStruct((c, c), BF),
            *(jax.ShapeDtypeStruct(v.shape, BF) for v in weights),
        ],
        scratch_shapes=[
            pltpu.VMEM(field(c).shape, BF),
            *(pltpu.VMEM(v.shape, F32) for v in weights),
            pltpu.SemaphoreType.DMA((FACES + 4,)),
        ],
        compiler_params=params(),
        cost_estimate=cost(0, 0),
        name="enter",
    )(ids, in_hbm(x), in_hbm(cot), *(in_hbm(v) for v in weights), *after)


def first(plan, ids, xp, low, near, far):
    c = plan.c
    count = len(near)

    def kernel(ids_ref, xp_ref, low_ref, *refs):
        near_refs, far_refs = refs[:count], refs[count : 2 * count]
        hp_ref, slope_ref, w_ref, u_ref, v_ref = refs[2 * count :]
        pieces = received(plan, ids_ref, near_refs, far_refs, 0, plan.sent[0], plan.shard)
        join_rows(plan, ids_ref, low_ref, pieces, w_ref, plan.shard)
        pair_weights(w_ref, u_ref)
        for face in range(0, FACES, GROUP):
            faces = slice(face, face + GROUP)
            pair_rows(xp_ref, v_ref, face, GROUP)
            for i, pre in enumerate(conv(v_ref, w_ref, u_ref, face, GROUP)):
                hidden, slope = gelu_both(pre)
                hp_ref[faces, i + 1, 1 : FS + 1] = hidden.astype(BF)
                slope_ref[faces, i] = slope.astype(BF)
        fill_halo(ids_ref, hp_ref)

    return pl.pallas_call(
        kernel,
        in_specs=[SMEM] + [VMEM] * (2 + 2 * count),
        out_specs=[VMEM] * 4,
        out_shape=[
            jax.ShapeDtypeStruct(padded(c), BF),
            field(c),
            jax.ShapeDtypeStruct((plan.conv, c), BF),
            jax.ShapeDtypeStruct((2, 3, c, c), BF),
        ],
        scratch_shapes=[pltpu.VMEM(pair_shape(c), BF)],
        compiler_params=params(),
        cost_estimate=cost(4.1, 12),
        name="first",
    )(ids, xp, low, *near, *far)


def second(plan, ids, hp, xp, go, dws, low, low_skip, near, far):
    c = plan.c
    count = len(near)

    def kernel(ids_ref, hp_ref, xp_ref, go_ref, dws_ref, low_ref, lows_ref, *refs):
        near_refs, far_refs = refs[:count], refs[count : 2 * count]
        out_hbm, gp_ref, w_ref, u_ref, ws_ref, keep_ref, send_ref = refs[2 * count : 2 * count + 7]
        out_ref, e_ref, dw_ref, v_ref, z_ref, sem_out = refs[2 * count + 7 :]
        pieces = received(plan, ids_ref, near_refs, far_refs, plan.sent[0], plan.sent[1], plan.shard)
        join_rows(plan, ids_ref, low_ref, pieces, w_ref, plan.shard)
        at = plan.sent[0] + plan.sent[1]
        pieces = received(plan, ids_ref, near_refs, far_refs, at, plan.sent[2], plan.skip_shard)
        join_rows(plan, ids_ref, lows_ref, pieces, ws_ref, plan.skip_shard)
        e_ref[...] = jnp.zeros_like(e_ref)
        place_rows(plan, ids_ref, dw_ref, dws_ref[...], 0, plan.skip_piece, plan.piece)
        pair_weights(w_ref, u_ref)
        for face in range(0, FACES, GROUP):
            faces = slice(face, face + GROUP)
            pair_rows(hp_ref, v_ref, face, GROUP)
            skip = jnp.dot(
                by_rows(xp_ref, face, GROUP, 1, 1), ws_ref[...], preferred_element_type=F32
            ).reshape(FS, GROUP, FS, ROLL, c)
            for i, pre in enumerate(conv(v_ref, w_ref, u_ref, face, GROUP)):
                value, slope = gelu_both(pre)
                out_ref[faces, i] = (value + skip[i]).astype(BF)
                low_grad = (go_ref[faces, i].astype(F32) * slope).astype(BF)
                gp_ref[faces, i + 1, 1 : FS + 1] = low_grad
            for one in range(face, face + GROUP):
                add_edges(e_ref, ids_ref, one, gp_ref)
        store = pltpu.make_async_copy(out_ref, out_hbm, sem_out)
        store.start()
        weight_grad(plan, ids_ref, v_ref, gp_ref, z_ref, dw_ref)
        keep_ref[...] = dw_ref[0]
        send_ref[...] = dw_ref[1]
        fill_halo_back(e_ref, gp_ref)
        store.wait()

    sums = jax.ShapeDtypeStruct((plan.tiles, plan.ranks, plan.late, c), BF)
    return pl.pallas_call(
        kernel,
        in_specs=[SMEM] + [VMEM] * (6 + 2 * count),
        out_specs=[HBM] + [VMEM] * 6,
        out_shape=[
            field(c),
            jax.ShapeDtypeStruct(padded(c), BF),
            jax.ShapeDtypeStruct((plan.conv, c), BF),
            jax.ShapeDtypeStruct((2, 3, c, c), BF),
            jax.ShapeDtypeStruct((c, c), BF),
            sums,
            sums,
        ],
        scratch_shapes=[
            pltpu.VMEM(field(c).shape, BF),
            edge_sums(c),
            pltpu.VMEM((2,) + sums.shape, BF),
            pltpu.VMEM(pair_shape(c), BF),
            pltpu.VMEM(grad_pairs(c), BF),
            pltpu.SemaphoreType.DMA,
        ],
        compiler_params=params(),
        cost_estimate=cost(9, 16),
        name="second",
    )(ids, hp, xp, go, dws, low, low_skip, *near, *far)


def hidden_back(plan, ids, gp, w, u, slope, xp, after):
    c = plan.c

    def kernel(ids_ref, gp_ref, w_ref, u_ref, slope_ref, xp_ref, _, op_ref, keep_ref, send_ref, *refs):
        e_ref, v_ref, z_ref, dw_ref = refs
        e_ref[...] = jnp.zeros_like(e_ref)
        for face in range(0, FACES, GROUP):
            faces = slice(face, face + GROUP)
            pair_rows(gp_ref, v_ref, face, GROUP)
            for i, grad in enumerate(conv(v_ref, w_ref, u_ref, face, GROUP, back=True)):
                low_grad = (grad * slope_ref[faces, i].astype(F32)).astype(BF)
                op_ref[faces, i + 1, 1 : FS + 1] = low_grad
            for one in range(face, face + GROUP):
                add_edges(e_ref, ids_ref, one, op_ref)
        pair_rows(xp_ref, v_ref, 0, FACES)
        weight_grad(plan, ids_ref, v_ref, op_ref, z_ref, dw_ref)
        fill_halo_back(e_ref, op_ref)
        keep_ref[...] = dw_ref[0]
        send_ref[...] = dw_ref[1]

    sums = (plan.tiles, plan.ranks, plan.piece, c)
    return pl.pallas_call(
        kernel,
        in_specs=[SMEM] + [VMEM] * 6,
        out_specs=[VMEM] * 3,
        out_shape=[jax.ShapeDtypeStruct(v, BF) for v in (padded(c), sums, sums)],
        scratch_shapes=[
            edge_sums(c),
            pltpu.VMEM(pair_shape(c), BF),
            pltpu.VMEM(grad_pairs(c), BF),
            pltpu.VMEM((2,) + sums, BF),
        ],
        compiler_params=params(),
        cost_estimate=cost(0, 0),
        name="hidden_back",
    )(ids, gp, w, u, slope, xp, after)


def tile_sums(plan, early, late):
    tiles, ranks, piece = plan.tiles, plan.ranks, plan.piece

    def kernel(*refs):
        for r in range(ranks):
            to = refs[2 * tiles + r]
            for at, group in ((0, refs[:tiles]), (piece, refs[tiles : 2 * tiles])):
                acc = group[0][r].astype(F32)
                for ref in group[1:]:
                    acc = acc + ref[r].astype(F32)
                to[at : at + acc.shape[0]] = acc.astype(BF)

    return pl.pallas_call(
        kernel,
        in_specs=[VMEM] * (2 * tiles),
        out_specs=[VMEM] * ranks,
        out_shape=[jax.ShapeDtypeStruct((plan.chunk, plan.c), BF)] * ranks,
        compiler_params=params(),
        cost_estimate=cost(0, 6),
        name="tile_sums",
    )(*early, *late)


def inputs_back_kernel(gp_ref, w_ref, u_ref, ws_ref, go_ref, out_hbm, out_ref, v_ref, sem):
    c = w_ref.shape[1]
    stores = []
    for face in range(0, FACES, GROUP):
        faces = slice(face, face + GROUP)
        pair_rows(gp_ref, v_ref, face, GROUP)
        skip = dot_back(by_rows(go_ref, face, GROUP, 0, 0), ws_ref[...])
        skip = skip.reshape(FS, GROUP, FS, ROLL, c)
        for i, grad in enumerate(conv(v_ref, w_ref, u_ref, face, GROUP, back=True)):
            out_ref[faces, i] = grad + skip[i]
        part = pl.ds(face, GROUP)
        copy = pltpu.make_async_copy(out_ref.at[part], out_hbm.at[part], sem.at[face // GROUP])
        copy.start()
        stores.append(copy)
    for store in stores:
        store.wait()


def inputs_back(gp, w, u, ws, go):
    c = w.shape[1]
    return pl.pallas_call(
        inputs_back_kernel,
        in_specs=[VMEM] * 5,
        out_specs=HBM,
        out_shape=field(c, F32),
        scratch_shapes=[
            pltpu.VMEM(field(c).shape, F32),
            pltpu.VMEM(pair_shape(c), BF),
            pltpu.SemaphoreType.DMA((FACES // GROUP,)),
        ],
        compiler_params=params(),
        cost_estimate=cost(0, 0),
        name="inputs_back",
    )(gp, w, u, ws, go)


def adamw(weight, moment, square, grad, rate):
    moment_new = 0.9 * moment + 0.1 * grad
    square_new = 0.999 * square + 0.001 * grad * grad
    fix_one = 1.0 - 0.9**STEP_COUNT
    fix_two = 1.0 - 0.999**STEP_COUNT
    weight_new = weight - rate * (
        moment_new / fix_one / (jnp.sqrt(square_new / fix_two) + 1e-08) + 0.01 * weight
    )
    return (weight_new, moment_new, square_new)


UPDATE_STEPS = 4


def update(plan, ids, near, far, sets):
    c, tiles = plan.c, plan.tiles

    def kernel(ids_ref, *refs):
        groups, state, new, sum_ref = refs[:2], refs[2:11], refs[11:20], refs[20]
        done_refs, sem = refs[21:30], refs[30]
        core, tile = ids_ref[0], ids_ref[1]
        at = 0
        stores = []
        for n in range(3):
            piece = plan.skip_piece if n == 2 else plan.piece
            rows = 2 * tiles * piece
            for k, group in enumerate(groups):
                side = core if k == 0 else 1 - core
                for d in range(tiles):
                    part = group[d, at : at + piece].astype(F32)
                    if piece % 8:
                        for t in range(2 * tiles):

                            def put(part=part, t=t, piece=piece):
                                sum_ref[t * piece : (t + 1) * piece] = part

                            pl.when(side * tiles + (tile ^ d) == t)(put)
                    else:
                        start = pl.multiple_of((side * tiles + (tile ^ d)) * piece, 8)
                        sum_ref[pl.ds(start, piece)] = part
            at += piece
            rate = (rows * plan.ranks) ** (-0.5)
            step = rows // UPDATE_STEPS if rows % (8 * UPDATE_STEPS) == 0 else rows
            for row in range(0, rows, step):
                old = (state[3 * n + k][row : row + step] for k in range(3))
                done = adamw(*old, sum_ref[row : row + step], rate)
                for k in range(3 * n, 3 * n + 3):
                    done_refs[k][row : row + step] = done[k - 3 * n]
                    source = done_refs[k].at[pl.ds(row, step)]
                    target = new[k].at[pl.ds(row, step)]
                    number = UPDATE_STEPS * k + row // step
                    stores.append(pltpu.make_async_copy(source, target, sem.at[number]))
                    stores[-1].start()
        for store in stores:
            store.wait()

    shapes = [v.shape for v in sets]
    return pl.pallas_call(
        kernel,
        in_specs=[SMEM] + [VMEM] * 11,
        out_specs=[HBM] * 9,
        out_shape=[jax.ShapeDtypeStruct(v, F32) for v in shapes],
        scratch_shapes=[
            pltpu.VMEM((plan.shard, c), F32),
            *(pltpu.VMEM(v, F32) for v in shapes),
            pltpu.SemaphoreType.DMA((9 * UPDATE_STEPS,)),
        ],
        compiler_params=params(),
        cost_estimate=cost(0, 9),
        name="update",
    )(ids, near, far, *sets)


def send(v, axis, size, step):
    if axis == "fsdp":
        pairs = [(i, (i + step) % size) for i in range(size)]
    else:
        pairs = [(i, i ^ step) for i in range(size)]
    return lax.ppermute(v, axis, pairs)


def total(*parts):
    acc = parts[0].astype(F32)
    for part in parts[1:]:
        acc = acc + part.astype(F32)
    return acc.astype(BF)


def make_body(sizes):
    tiles, ranks = sizes["tile"], sizes["fsdp"]

    def to_core(v):
        return send(v, "core", 2, 1)

    def to_tile(v, d):
        return send(v, "tile", tiles, d)

    def to_rank(v, d):
        return send(v, "fsdp", ranks, d)

    def per_device(
        inputs,
        cotangent,
        lengths,
        face_table,
        w_first,
        w_second,
        w_skip,
        mom_first,
        sq_first,
        mom_second,
        sq_second,
        mom_skip,
        sq_skip,
    ):
        plan = Plan(sizes, inputs.shape[-1])
        x = jnp.transpose(inputs[0], (1, 2, 3, 0, 4))
        cot = jnp.transpose(cotangent[0], (1, 2, 3, 0, 4))
        places = jnp.stack([lax.axis_index(n) for n in ("core", "tile", "fsdp")]).astype(jnp.int32)
        weights = w_first, w_second, w_skip
        sent = pack(plan, places, *weights)
        near = [jnp.stack([to_rank(sent, d) for d in range(1, ranks)])]
        if plan.split:
            near += [to_tile(near[0], e) for e in range(1, tiles)]
        ids = jnp.concatenate([places, lengths, face_table.T.reshape(-1)])
        xp, go, dws, low1, low2, low3 = enter(plan, ids, x, cot, weights, near[:1])
        xp, near = lax.optimization_barrier((xp, near))
        far = [to_core(v) for v in near]
        hp, slope, w1, u1 = first(plan, ids, xp, low1, near, far)
        output, gp, w2, u2, ws, keep2, away2 = second(
            plan, ids, hp, xp, go, dws, low2, low3, near, far
        )
        came2 = to_core(away2)
        parts2 = [total(keep2[d], came2[d]) for d in range(tiles)]
        op, keep1, away1 = hidden_back(plan, ids, gp, w2, u2, slope, xp, parts2[0])
        late = [parts2[0]] + [to_tile(parts2[d], d) for d in range(1, tiles)]
        late, away1 = lax.optimization_barrier((late, away1))
        came1 = to_core(away1)
        parts1 = [total(keep1[d], came1[d]) for d in range(tiles)]
        op, parts1 = lax.optimization_barrier((op, parts1))
        early = [parts1[0]] + [to_tile(parts1[d], d) for d in range(1, tiles)]
        grad_inputs = inputs_back(op, w1, u1, ws, go)
        early, late, grad_inputs = lax.optimization_barrier((early, late, grad_inputs))
        parts = tile_sums(plan, early, late)
        came = [to_rank(parts[d], d) for d in range(1, ranks)]
        mine = total(parts[0], *came)
        near = jnp.stack([mine] + [to_tile(mine, d) for d in range(1, tiles)])
        far = to_core(near)
        news = update(
            plan,
            ids,
            near,
            far,
            (
                w_first,
                mom_first,
                sq_first,
                w_second,
                mom_second,
                sq_second,
                w_skip,
                mom_skip,
                sq_skip,
            ),
        )
        output = jnp.transpose(output, (3, 0, 1, 2, 4))[None]
        grad_inputs = jnp.transpose(grad_inputs, (3, 0, 1, 2, 4))[None]
        return (output, grad_inputs, *news)

    return per_device


def solution(mesh):
    pairs = mesh.shape["dp"] // 2
    ranks = mesh.shape["fsdp"]
    fine = Mesh(mesh.devices.reshape(pairs, 2, ranks), ("tile", "core", "fsdp"))
    sizes = {"tile": pairs, "core": 2, "fsdp": ranks}
    every = ("tile", "core", "fsdp")
    fields = P(every, None, None, None, None, None)
    rows = P("fsdp", None)
    return jax.shard_map(
        make_body(sizes),
        mesh=fine,
        in_specs=(fields, fields, P(every), P()) + (rows,) * 9,
        out_specs=(fields, fields) + (rows,) * 9,
        check_vma=False,
    )
```

```python
import functools

import jax
import jax.numpy as jnp
from jax import lax
from jax.experimental import pallas as pl
from jax.experimental.pallas import tpu as pltpu
from jax.sharding import Mesh
from jax.sharding import PartitionSpec as P

STEP_COUNT = 10
BF = jnp.bfloat16
F32 = jnp.float32
FS = 6
ROLL = 8
FACES = 12
GELU_K = 0.7978845608028654
GELU_C = 0.044715
VMEM_LIMIT = 30 * 2**20
GROUP = 2


ANY = pl.BlockSpec(memory_space=pl.ANY)
HBM = pl.BlockSpec(memory_space=pltpu.HBM)
VMEM = pl.BlockSpec(memory_space=pltpu.VMEM)
SMEM = pl.BlockSpec(memory_space=pltpu.SMEM)


def field(c, dtype=BF):
    return jax.ShapeDtypeStruct((FACES, FS, FS, ROLL, c), dtype)


def padded(c):
    return (FACES, FS + 2, FS + 2, ROLL, c)


def inner(ref):
    return ref.at[:, 1 : FS + 1, 1 : FS + 1]


def in_hbm(v):
    return pltpu.with_memory_space_constraint(v, pltpu.HBM)


def params():
    return pltpu.CompilerParams(vmem_limit_bytes=VMEM_LIMIT)


def cost(gflop, mbyte):
    return pl.CostEstimate(flops=int(gflop * 1e9), bytes_accessed=int(mbyte * 1e6), transcendentals=0)


def gelu_both(v):
    a = (GELU_K * GELU_C) * (v * v) + GELU_K
    half = 0.5 * jnp.tanh(v * a) + 0.5
    value = v * half
    return value, half + (value * (1.0 - half)) * (6.0 * a - 4.0 * GELU_K)


def pair_shape(c):
    return (4, FS // 2, FACES, FS + 2, ROLL, c)


def grad_pairs(c):
    return (4, FS // 2, FACES, FS, ROLL, c)


def pair_rows(p_ref, v_ref, face, count):
    for t in range(FS // 2):
        d0, d1, d2, d3 = (p_ref[face : face + count, 2 * t + q] for q in range(4))
        v_ref[0, t, face : face + count] = d0 - d2
        v_ref[1, t, face : face + count] = d1 + d2
        v_ref[2, t, face : face + count] = d2 - d1
        v_ref[3, t, face : face + count] = d1 - d3


def pair_weights(w_ref, u_ref):
    c = w_ref.shape[1]
    for b in range(3):
        g0, g1, g2 = (w_ref[(3 * a + b) * c : (3 * a + b + 1) * c].astype(F32) for a in range(3))
        outside, middle = 0.5 * (g0 + g2), 0.5 * g1
        u_ref[0, b] = (outside + middle).astype(BF)
        u_ref[1, b] = (outside - middle).astype(BF)


def dot_back(v, w):
    return lax.dot_general(v, w, (((1,), (1,)), ((), ())), preferred_element_type=F32)


def conv(v_ref, w_ref, u_ref, face, count, back=False):
    c = w_ref.shape[1]
    products = []
    for k in range(4):
        acc = None
        for b in range(3):
            v = v_ref[k, :, face : face + count, b : b + FS].reshape(-1, c)
            col = 2 - b if back else b
            if k in (0, 3):
                t = 3 * (2 if (k == 3) != back else 0) + col
                g = w_ref[t * c : (t + 1) * c]
            else:
                g = u_ref[k - 1, col]
            part = dot_back(v, g) if back else jnp.dot(v, g, preferred_element_type=F32)
            acc = part if acc is None else acc + part
        products.append(acc.reshape(FS // 2, count, FS, ROLL, c))
    m0, m1, m2, m3 = products
    even, odd = m0 + m1 + m2, m1 - m2 - m3
    return [(odd if i % 2 else even)[i // 2] for i in range(FS)]


def by_rows(ref, face, count, first_row, first_col):
    cols = slice(first_col, first_col + FS)
    rows = [ref[face : face + count, first_row + i, cols] for i in range(FS)]
    return jnp.stack(rows).reshape(-1, ref.shape[-1])


def outer(p, g):
    c = p.shape[-1]
    return lax.dot_general(
        p.reshape(-1, c), g.reshape(-1, c), (((0,), (0,)), ((), ())), preferred_element_type=F32
    )


def zero_corners(p_ref):
    zero = jnp.zeros((FACES, 1, 1, ROLL, p_ref.shape[-1]), p_ref.dtype)
    for i in (0, FS + 1):
        for j in (0, FS + 1):
            p_ref[:, i : i + 1, j : j + 1] = zero


def neighbour(ids_ref, side, face):
    return ids_ref[4 + side * FACES + face]


def fill_halo(ids_ref, p_ref):
    for face in range(FACES):
        p_ref[face, 0, 1 : FS + 1] = p_ref[neighbour(ids_ref, 0, face), FS, 1 : FS + 1]
        p_ref[face, 1 : FS + 1, FS + 1] = p_ref[neighbour(ids_ref, 1, face), 1 : FS + 1, 1]
        p_ref[face, FS + 1, 1 : FS + 1] = p_ref[neighbour(ids_ref, 2, face), 1, 1 : FS + 1]
        p_ref[face, 1 : FS + 1, 0] = p_ref[neighbour(ids_ref, 3, face), 1 : FS + 1, FS]
    zero_corners(p_ref)


def add_edges(e_ref, ids_ref, face, p_ref):
    rows = cols = slice(1, FS + 1)
    edges = (p_ref[face, 1, cols], p_ref[face, rows, FS], p_ref[face, FS, cols], p_ref[face, rows, 1])
    for side, part in enumerate(edges):
        to = neighbour(ids_ref, side, face)
        e_ref[to, side] = e_ref[to, side] + part.astype(F32)


def fill_halo_back(e_ref, p_ref):
    for face in range(FACES):
        p_ref[face, FS + 1, 1 : FS + 1] = e_ref[face, 0].astype(p_ref.dtype)
        p_ref[face, 1 : FS + 1, 0] = e_ref[face, 1].astype(p_ref.dtype)
        p_ref[face, 0, 1 : FS + 1] = e_ref[face, 2].astype(p_ref.dtype)
        p_ref[face, 1 : FS + 1, FS + 1] = e_ref[face, 3].astype(p_ref.dtype)
    zero_corners(p_ref)


def edge_sums(c):
    return pltpu.VMEM((FACES, 4, FS, ROLL, c), F32)


class Plan:
    def __init__(self, sizes, channels):
        self.tiles, self.ranks = sizes["tile"], sizes["fsdp"]
        self.c = channels
        self.conv = 9 * channels
        self.shard = self.conv // self.ranks
        self.skip_shard = channels // self.ranks
        self.piece = self.shard // (2 * self.tiles)
        self.skip_piece = self.skip_shard // (2 * self.tiles)
        self.late = self.piece + self.skip_piece
        self.chunk = self.piece + self.late
        self.split = self.piece % 8 == 0 and self.skip_piece % 8 == 0
        self.halves = self.shard // 2, self.shard // 2, self.skip_shard // 2
        self.sent = self.halves
        self.direct = ()
        if self.split:
            self.sent = self.piece, self.piece, self.skip_piece
            self.direct = tuple(d for d in (1, 2) if d < self.ranks - 1)
        self.start = {}
        rows = 0
        for d in range(1, self.ranks):
            self.start[d] = rows
            rows += self.sent[0] if d in self.direct else sum(self.sent)


def place_rows(plan, ids_ref, dst_ref, value, first_row, piece, offset):
    core, tile, rank = ids_ref[0], ids_ref[1], ids_ref[2]
    end = first_row + value.shape[0]
    row = first_row
    while row < end:
        number = row // piece
        stop = min(end, (number + 1) * piece)
        to_tile = number % plan.tiles
        to_core = number // plan.tiles % 2
        to_rank = number // (2 * plan.tiles)
        at = offset + row - number * piece
        dst_ref[
            to_core ^ core,
            to_tile ^ tile,
            to_rank ^ rank,
            at : at + stop - row,
        ] = value[row - first_row : stop - first_row]
        row = stop


def weight_grad(plan, ids_ref, v_ref, g_ref, z_ref, dst_ref):
    c = plan.c
    halves = range(FS // 2)
    cols = slice(1, FS + 1)
    for t in halves:
        y0, y1 = g_ref[:, 2 * t + 1, cols], g_ref[:, 2 * t + 2, cols]
        z_ref[0, t] = y0
        z_ref[1, t] = (y0 + y1) * 0.5
        z_ref[2, t] = (y0 - y1) * 0.5
        z_ref[3, t] = y1
    for b in range(3):
        m0, m1, m2, m3 = (outer(v_ref[k, :, :, b : b + FS], z_ref[k]) for k in range(4))
        both = m1 + m2
        for a, part in enumerate((m0 + both, m1 - m2, both - m3)):
            place_rows(plan, ids_ref, dst_ref, part.astype(BF), (3 * a + b) * c, plan.piece, 0)


def pack(plan, ids, weights, rows, shared, parts):
    c = plan.c
    count = len(weights)

    def kernel(ids_ref, *refs):
        rows_ref, sem = refs[count + len(parts) :]
        loads = []
        at = 0
        for k in range(count):
            hbm = refs[k]
            start = ids_ref[0] * (hbm.shape[0] // 2)
            if shared:
                start = start + ids_ref[1] * rows[k]
            source = hbm.at[pl.ds(pl.multiple_of(start, 8), rows[k])]
            loads.append(pltpu.make_async_copy(source, rows_ref.at[pl.ds(at, rows[k])], sem.at[k]))
            at += rows[k]
        for load in loads:
            load.start()
        for load in loads:
            load.wait()
        for k, part in enumerate(parts):
            refs[count + k][...] = rows_ref[0:part].astype(BF)

    return pl.pallas_call(
        kernel,
        in_specs=[SMEM] + [HBM] * count,
        out_specs=[VMEM] * len(parts),
        out_shape=[jax.ShapeDtypeStruct((v, c), BF) for v in parts],
        scratch_shapes=[pltpu.VMEM((sum(rows), c), F32), pltpu.SemaphoreType.DMA((count,))],
        compiler_params=params(),
        cost_estimate=cost(0, 0),
        name="pack",
    )(ids, *(in_hbm(v) for v in weights))


def below(arrays):
    rows = [v.shape[0] for v in arrays]

    def kernel(*refs):
        at = 0
        for ref, count in zip(refs, rows):
            refs[-1][at : at + count] = ref[...]
            at += count

    return pl.pallas_call(
        kernel,
        in_specs=[VMEM] * len(rows),
        out_specs=VMEM,
        out_shape=jax.ShapeDtypeStruct((sum(rows), arrays[0].shape[1]), BF),
        compiler_params=params(),
        cost_estimate=cost(0, 0),
        name="below",
    )(*arrays)


def join_rows(plan, ids_ref, low_ref, pieces, w_ref, rows):
    rank = ids_ref[2]
    w_ref[pl.ds(pl.multiple_of(rank * rows, 8), rows)] = low_ref[...]
    for ref, index, d, row in pieces:
        start = (rank ^ d) * rows + row
        part = ref[index]
        w_ref[pl.ds(pl.multiple_of(start, 8), part.shape[0])] = part


def received(plan, ids_ref, near_refs, far_refs, weight):
    core, tile = ids_ref[0], ids_ref[1]
    rows = plan.sent[weight]
    pieces = []
    for side, group in ((core, near_refs), (1 - core, far_refs)):
        for e, ref in enumerate(group):
            row = side * plan.halves[weight]
            if plan.split:
                row = row + (tile ^ e) * rows
            for d in range(1, plan.ranks):
                if weight == 0 or d not in plan.direct:
                    at = plan.start[d] + sum(plan.sent[:weight])
                    pieces.append((ref, pl.ds(at, rows), d, row))
    return pieces


def received_directly(plan, ids_ref, near_refs, far_refs, at, weight):
    core = ids_ref[0]
    rows = plan.halves[weight]
    pieces = []
    for side, group in ((core, near_refs), (1 - core, far_refs)):
        for ref, d in zip(group, plan.direct):
            pieces.append((ref, pl.ds(at, rows), d, side * rows))
    return pieces


def enter(plan, ids, x, cot, weights, after):
    c = plan.c

    def kernel(ids_ref, x_hbm, cot_hbm, *refs):
        refs = refs[:3] + refs[3 + len(after) :]
        weights_hbm, xp_ref, go_ref, dw_ref = refs[:3], *refs[3:6]
        low_refs, cot_ref, weight_refs, sem = refs[6:9], refs[9], refs[10:13], refs[13]
        load_x = pltpu.make_async_copy(x_hbm, inner(xp_ref), sem.at[FACES])
        load_x.start()
        loads = []
        for face in range(FACES):
            loads.append(pltpu.make_async_copy(cot_hbm.at[face], cot_ref.at[face], sem.at[face]))
            loads[-1].start()
        low_loads = []
        for k in range(3):
            low_loads.append(
                pltpu.make_async_copy(weights_hbm[k], weight_refs[k], sem.at[FACES + 1 + k])
            )
            low_loads[-1].start()
        live = lax.broadcasted_iota(jnp.int32, (FS, FS, ROLL, c), 2) < ids_ref[3]
        for face in range(FACES):
            loads[face].wait()
            go_ref[face] = jnp.where(live, cot_ref[face].astype(F32), 0.0).astype(BF)
        load_x.wait()
        fill_halo(ids_ref, xp_ref)
        dw_ref[...] = outer(xp_ref[:, 1 : FS + 1, 1 : FS + 1], go_ref[...]).astype(dw_ref.dtype)
        for k in range(3):
            low_loads[k].wait()
            low_refs[k][...] = weight_refs[k][...].astype(BF)

    return pl.pallas_call(
        kernel,
        in_specs=[SMEM] + [HBM] * 5 + [VMEM] * len(after),
        out_specs=[VMEM] * 6,
        out_shape=[
            jax.ShapeDtypeStruct(padded(c), BF),
            field(c),
            jax.ShapeDtypeStruct((c, c), BF),
            *(jax.ShapeDtypeStruct(v.shape, BF) for v in weights),
        ],
        scratch_shapes=[
            pltpu.VMEM(field(c).shape, BF),
            *(pltpu.VMEM(v.shape, F32) for v in weights),
            pltpu.SemaphoreType.DMA((FACES + 4,)),
        ],
        compiler_params=params(),
        cost_estimate=cost(0, 0),
        name="enter",
    )(ids, in_hbm(x), in_hbm(cot), *(in_hbm(v) for v in weights), *after)


def first(plan, ids, xp, low, near, far):
    c = plan.c
    count = len(near)

    def kernel(ids_ref, xp_ref, low_ref, *refs):
        near_refs, far_refs = refs[:count], refs[count : 2 * count]
        hp_ref, slope_ref, w_ref, u_ref, v_ref = refs[2 * count :]
        pieces = received(plan, ids_ref, near_refs, far_refs, 0)
        join_rows(plan, ids_ref, low_ref, pieces, w_ref, plan.shard)
        pair_weights(w_ref, u_ref)
        for face in range(0, FACES, GROUP):
            faces = slice(face, face + GROUP)
            pair_rows(xp_ref, v_ref, face, GROUP)
            for i, pre in enumerate(conv(v_ref, w_ref, u_ref, face, GROUP)):
                hidden, slope = gelu_both(pre)
                hp_ref[faces, i + 1, 1 : FS + 1] = hidden.astype(BF)
                slope_ref[faces, i] = slope.astype(BF)
        fill_halo(ids_ref, hp_ref)

    return pl.pallas_call(
        kernel,
        in_specs=[SMEM] + [VMEM] * (2 + 2 * count),
        out_specs=[VMEM] * 4,
        out_shape=[
            jax.ShapeDtypeStruct(padded(c), BF),
            field(c),
            jax.ShapeDtypeStruct((plan.conv, c), BF),
            jax.ShapeDtypeStruct((2, 3, c, c), BF),
        ],
        scratch_shapes=[pltpu.VMEM(pair_shape(c), BF)],
        compiler_params=params(),
        cost_estimate=cost(0, 0),
        name="first",
    )(ids, xp, low, *near, *far)


def second(plan, ids, hp, xp, go, dws, low, low_skip, near, far, near_half, far_half):
    c = plan.c
    count = len(near)
    halves = len(near_half)

    def kernel(ids_ref, hp_ref, xp_ref, go_ref, dws_ref, low_ref, lows_ref, *refs):
        groups = refs[:count], refs[count : 2 * count]
        refs = refs[2 * count :]
        direct = refs[:halves], refs[halves : 2 * halves]
        refs = refs[2 * halves :]
        out_hbm, gp_ref, w_ref, u_ref, ws_ref, keep_ref, send_ref = refs[:7]
        out_ref, e_ref, dw_ref, v_ref, z_ref, sem_out = refs[7:]
        pieces = received(plan, ids_ref, *groups, 1)
        pieces += received_directly(plan, ids_ref, *direct, 0, 1)
        join_rows(plan, ids_ref, low_ref, pieces, w_ref, plan.shard)
        pieces = received(plan, ids_ref, *groups, 2)
        pieces += received_directly(plan, ids_ref, *direct, plan.halves[1], 2)
        join_rows(plan, ids_ref, lows_ref, pieces, ws_ref, plan.skip_shard)
        e_ref[...] = jnp.zeros_like(e_ref)
        place_rows(plan, ids_ref, dw_ref, dws_ref[...], 0, plan.skip_piece, plan.piece)
        pair_weights(w_ref, u_ref)
        for face in range(0, FACES, GROUP):
            faces = slice(face, face + GROUP)
            pair_rows(hp_ref, v_ref, face, GROUP)
            skip = jnp.dot(
                by_rows(xp_ref, face, GROUP, 1, 1), ws_ref[...], preferred_element_type=F32
            ).reshape(FS, GROUP, FS, ROLL, c)
            for i, pre in enumerate(conv(v_ref, w_ref, u_ref, face, GROUP)):
                value, slope = gelu_both(pre)
                out_ref[faces, i] = (value + skip[i]).astype(BF)
                low_grad = (go_ref[faces, i].astype(F32) * slope).astype(BF)
                gp_ref[faces, i + 1, 1 : FS + 1] = low_grad
            for one in range(face, face + GROUP):
                add_edges(e_ref, ids_ref, one, gp_ref)
        store = pltpu.make_async_copy(out_ref, out_hbm, sem_out)
        store.start()
        weight_grad(plan, ids_ref, v_ref, gp_ref, z_ref, dw_ref)
        keep_ref[...] = dw_ref[0]
        send_ref[...] = dw_ref[1]
        fill_halo_back(e_ref, gp_ref)
        store.wait()

    sums = jax.ShapeDtypeStruct((plan.tiles, plan.ranks, plan.late, c), BF)
    return pl.pallas_call(
        kernel,
        in_specs=[SMEM] + [VMEM] * (6 + 2 * count + 2 * halves),
        out_specs=[HBM] + [VMEM] * 6,
        out_shape=[
            field(c),
            jax.ShapeDtypeStruct(padded(c), BF),
            jax.ShapeDtypeStruct((plan.conv, c), BF),
            jax.ShapeDtypeStruct((2, 3, c, c), BF),
            jax.ShapeDtypeStruct((c, c), BF),
            sums,
            sums,
        ],
        scratch_shapes=[
            pltpu.VMEM(field(c).shape, BF),
            edge_sums(c),
            pltpu.VMEM((2,) + sums.shape, BF),
            pltpu.VMEM(pair_shape(c), BF),
            pltpu.VMEM(grad_pairs(c), BF),
            pltpu.SemaphoreType.DMA,
        ],
        compiler_params=params(),
        cost_estimate=cost(9, 16),
        name="second",
    )(ids, hp, xp, go, dws, low, low_skip, *near, *far, *near_half, *far_half)


def hidden_back(plan, ids, gp, w, u, slope, xp, after):
    c = plan.c

    def kernel(ids_ref, gp_ref, w_ref, u_ref, slope_ref, xp_ref, _, op_ref, keep_ref, send_ref, *refs):
        e_ref, v_ref, z_ref, dw_ref = refs
        e_ref[...] = jnp.zeros_like(e_ref)
        for face in range(0, FACES, GROUP):
            faces = slice(face, face + GROUP)
            pair_rows(gp_ref, v_ref, face, GROUP)
            for i, grad in enumerate(conv(v_ref, w_ref, u_ref, face, GROUP, back=True)):
                low_grad = (grad * slope_ref[faces, i].astype(F32)).astype(BF)
                op_ref[faces, i + 1, 1 : FS + 1] = low_grad
            for one in range(face, face + GROUP):
                add_edges(e_ref, ids_ref, one, op_ref)
        pair_rows(xp_ref, v_ref, 0, FACES)
        weight_grad(plan, ids_ref, v_ref, op_ref, z_ref, dw_ref)
        fill_halo_back(e_ref, op_ref)
        keep_ref[...] = dw_ref[0]
        send_ref[...] = dw_ref[1]

    sums = (plan.tiles, plan.ranks, plan.piece, c)
    return pl.pallas_call(
        kernel,
        in_specs=[SMEM] + [VMEM] * 6,
        out_specs=[VMEM] * 3,
        out_shape=[jax.ShapeDtypeStruct(v, BF) for v in (padded(c), sums, sums)],
        scratch_shapes=[
            edge_sums(c),
            pltpu.VMEM(pair_shape(c), BF),
            pltpu.VMEM(grad_pairs(c), BF),
            pltpu.VMEM((2,) + sums, BF),
        ],
        compiler_params=params(),
        cost_estimate=cost(0, 0),
        name="hidden_back",
    )(ids, gp, w, u, slope, xp, after)


def tile_sums(plan, early, late):
    tiles, ranks, piece = plan.tiles, plan.ranks, plan.piece

    def kernel(*refs):
        for r in range(ranks):
            to = refs[2 * tiles + r]
            for at, group in ((0, refs[:tiles]), (piece, refs[tiles : 2 * tiles])):
                acc = group[0][r].astype(F32)
                for ref in group[1:]:
                    acc = acc + ref[r].astype(F32)
                to[at : at + acc.shape[0]] = acc.astype(BF)

    return pl.pallas_call(
        kernel,
        in_specs=[VMEM] * (2 * tiles),
        out_specs=[VMEM] * ranks,
        out_shape=[jax.ShapeDtypeStruct((plan.chunk, plan.c), BF)] * ranks,
        compiler_params=params(),
        cost_estimate=cost(0, 6),
        name="tile_sums",
    )(*early, *late)


def inputs_back_kernel(gp_ref, w_ref, u_ref, ws_ref, go_ref, out_hbm, out_ref, v_ref, sem):
    c = w_ref.shape[1]
    stores = []
    for face in range(0, FACES, GROUP):
        faces = slice(face, face + GROUP)
        pair_rows(gp_ref, v_ref, face, GROUP)
        skip = dot_back(by_rows(go_ref, face, GROUP, 0, 0), ws_ref[...])
        skip = skip.reshape(FS, GROUP, FS, ROLL, c)
        for i, grad in enumerate(conv(v_ref, w_ref, u_ref, face, GROUP, back=True)):
            out_ref[faces, i] = grad + skip[i]
        part = pl.ds(face, GROUP)
        copy = pltpu.make_async_copy(out_ref.at[part], out_hbm.at[part], sem.at[face // GROUP])
        copy.start()
        stores.append(copy)
    for store in stores:
        store.wait()


def inputs_back(gp, w, u, ws, go):
    c = w.shape[1]
    return pl.pallas_call(
        inputs_back_kernel,
        in_specs=[VMEM] * 5,
        out_specs=HBM,
        out_shape=field(c, F32),
        scratch_shapes=[
            pltpu.VMEM(field(c).shape, F32),
            pltpu.VMEM(pair_shape(c), BF),
            pltpu.SemaphoreType.DMA((FACES // GROUP,)),
        ],
        compiler_params=params(),
        cost_estimate=cost(0, 0),
        name="inputs_back",
    )(gp, w, u, ws, go)


def adamw(weight, moment, square, grad, rate):
    moment_new = 0.9 * moment + 0.1 * grad
    square_new = 0.999 * square + 0.001 * grad * grad
    fix_one = 1.0 - 0.9**STEP_COUNT
    fix_two = 1.0 - 0.999**STEP_COUNT
    weight_new = weight - rate * (
        moment_new / fix_one / (jnp.sqrt(square_new / fix_two) + 1e-08) + 0.01 * weight
    )
    return (weight_new, moment_new, square_new)


UPDATE_STEPS = 4


def update(plan, ids, near, far, sets):
    c, tiles = plan.c, plan.tiles

    def kernel(ids_ref, *refs):
        groups, state, new, sum_ref = refs[:2], refs[2:11], refs[11:20], refs[20]
        done_refs, sem = refs[21:30], refs[30]
        core, tile = ids_ref[0], ids_ref[1]
        at = 0
        stores = []
        for n in range(3):
            piece = plan.skip_piece if n == 2 else plan.piece
            rows = 2 * tiles * piece
            for k, group in enumerate(groups):
                side = core if k == 0 else 1 - core
                for d in range(tiles):
                    part = group[d, at : at + piece].astype(F32)
                    if piece % 8:
                        for t in range(2 * tiles):

                            def put(part=part, t=t, piece=piece):
                                sum_ref[t * piece : (t + 1) * piece] = part

                            pl.when(side * tiles + (tile ^ d) == t)(put)
                    else:
                        start = pl.multiple_of((side * tiles + (tile ^ d)) * piece, 8)
                        sum_ref[pl.ds(start, piece)] = part
            at += piece
            rate = (rows * plan.ranks) ** (-0.5)
            step = rows // UPDATE_STEPS if rows % (8 * UPDATE_STEPS) == 0 else rows
            for row in range(0, rows, step):
                old = (state[3 * n + k][row : row + step] for k in range(3))
                done = adamw(*old, sum_ref[row : row + step], rate)
                for k in range(3 * n, 3 * n + 3):
                    done_refs[k][row : row + step] = done[k - 3 * n]
                    source = done_refs[k].at[pl.ds(row, step)]
                    target = new[k].at[pl.ds(row, step)]
                    number = UPDATE_STEPS * k + row // step
                    stores.append(pltpu.make_async_copy(source, target, sem.at[number]))
                    stores[-1].start()
        for store in stores:
            store.wait()

    shapes = [v.shape for v in sets]
    return pl.pallas_call(
        kernel,
        in_specs=[SMEM] + [VMEM] * 11,
        out_specs=[HBM] * 9,
        out_shape=[jax.ShapeDtypeStruct(v, F32) for v in shapes],
        scratch_shapes=[
            pltpu.VMEM((plan.shard, c), F32),
            *(pltpu.VMEM(v, F32) for v in shapes),
            pltpu.SemaphoreType.DMA((9 * UPDATE_STEPS,)),
        ],
        compiler_params=params(),
        cost_estimate=cost(0, 9),
        name="update",
    )(ids, near, far, *sets)


def send(v, axis, size, step):
    return lax.ppermute(v, axis, [(i, i ^ step) for i in range(size)])


def total(*parts):
    acc = parts[0].astype(F32)
    for part in parts[1:]:
        acc = acc + part.astype(F32)
    return acc.astype(BF)


def make_body(sizes):
    tiles, ranks = sizes["tile"], sizes["fsdp"]

    def to_core(v):
        return send(v, "core", 2, 1)

    def to_tile(v, d):
        return send(v, "tile", tiles, d)

    def to_rank(v, d):
        return send(v, "fsdp", ranks, d)

    def per_device(
        inputs,
        cotangent,
        lengths,
        face_table,
        w_first,
        w_second,
        w_skip,
        mom_first,
        sq_first,
        mom_second,
        sq_second,
        mom_skip,
        sq_skip,
    ):
        plan = Plan(sizes, inputs.shape[-1])
        x = jnp.transpose(inputs[0], (1, 2, 3, 0, 4))
        cot = jnp.transpose(cotangent[0], (1, 2, 3, 0, 4))
        places = jnp.stack([lax.axis_index(n) for n in ("core", "tile", "fsdp")]).astype(jnp.int32)
        weights = w_first, w_second, w_skip
        parts = (plan.sent[0], sum(plan.sent))
        some, sent = pack(plan, places, weights, plan.sent, plan.split, parts)
        near = [to_rank(some if d in plan.direct else sent, d) for d in range(1, ranks)]
        near = [below(near)]
        near_half, after = [], near[:]
        if plan.split:
            near += [to_tile(near[0], e) for e in range(1, tiles)]
            (half,) = pack(plan, places, weights[1:], plan.halves[1:], False, (sum(plan.halves[1:]),))
            near_half = [to_rank(half, d) for d in plan.direct]
            after.append(half)
        ids = jnp.concatenate([places, lengths, face_table.T.reshape(-1)])
        xp, go, dws, low1, low2, low3 = enter(plan, ids, x, cot, weights, after)
        xp, near, near_half = lax.optimization_barrier((xp, near, near_half))
        far = [to_core(v) for v in near]
        far_half = [to_core(v) for v in near_half]
        hp, slope, w1, u1 = first(plan, ids, xp, low1, near, far)
        hp, far_half = lax.optimization_barrier((hp, far_half))
        output, gp, w2, u2, ws, keep2, away2 = second(
            plan, ids, hp, xp, go, dws, low2, low3, near, far, near_half, far_half
        )
        came2 = to_core(away2)
        parts2 = [total(keep2[d], came2[d]) for d in range(tiles)]
        op, keep1, away1 = hidden_back(plan, ids, gp, w2, u2, slope, xp, parts2[0])
        late = [parts2[0]] + [to_tile(parts2[d], d) for d in range(1, tiles)]
        late, away1 = lax.optimization_barrier((late, away1))
        came1 = to_core(away1)
        parts1 = [total(keep1[d], came1[d]) for d in range(tiles)]
        op, parts1 = lax.optimization_barrier((op, parts1))
        early = [parts1[0]] + [to_tile(parts1[d], d) for d in range(1, tiles)]
        grad_inputs = inputs_back(op, w1, u1, ws, go)
        early, late, grad_inputs = lax.optimization_barrier((early, late, grad_inputs))
        parts = tile_sums(plan, early, late)
        came = [to_rank(parts[d], d) for d in range(1, ranks)]
        mine = total(parts[0], *came)
        near = jnp.stack([mine] + [to_tile(mine, d) for d in range(1, tiles)])
        far = to_core(near)
        news = update(
            plan,
            ids,
            near,
            far,
            (
                w_first,
                mom_first,
                sq_first,
                w_second,
                mom_second,
                sq_second,
                w_skip,
                mom_skip,
                sq_skip,
            ),
        )
        output = jnp.transpose(output, (3, 0, 1, 2, 4))[None]
        grad_inputs = jnp.transpose(grad_inputs, (3, 0, 1, 2, 4))[None]
        return (output, grad_inputs, *news)

    return per_device


def solution(mesh):
    pairs = mesh.shape["dp"] // 2
    ranks = mesh.shape["fsdp"]
    fine = Mesh(mesh.devices.reshape(pairs, 2, ranks), ("tile", "core", "fsdp"))
    sizes = {"tile": pairs, "core": 2, "fsdp": ranks}
    every = ("tile", "core", "fsdp")
    fields = P(every, None, None, None, None, None)
    rows = P("fsdp", None)
    return jax.shard_map(
        make_body(sizes),
        mesh=fine,
        in_specs=(fields, fields, P(every), P()) + (rows,) * 9,
        out_specs=(fields, fields) + (rows,) * 9,
        check_vma=False,
    )
```

```python
import functools

import jax
import jax.numpy as jnp
from jax import lax
from jax.experimental import pallas as pl
from jax.experimental.pallas import tpu as pltpu
from jax.sharding import Mesh
from jax.sharding import PartitionSpec as P

STEP_COUNT = 10
BF = jnp.bfloat16
F32 = jnp.float32
FS = 6
ROLL = 8
FACES = 12
GELU_K = 0.7978845608028654
GELU_C = 0.044715
VMEM_LIMIT = 30 * 2**20
GROUP = 2


ANY = pl.BlockSpec(memory_space=pl.ANY)
HBM = pl.BlockSpec(memory_space=pltpu.HBM)
VMEM = pl.BlockSpec(memory_space=pltpu.VMEM)
SMEM = pl.BlockSpec(memory_space=pltpu.SMEM)


def field(c, dtype=BF):
    return jax.ShapeDtypeStruct((FACES, FS, FS, ROLL, c), dtype)


def padded(c):
    return (FACES, FS + 2, FS + 2, ROLL, c)


def inner(ref):
    return ref.at[:, 1 : FS + 1, 1 : FS + 1]


def in_hbm(v):
    return pltpu.with_memory_space_constraint(v, pltpu.HBM)


def params():
    return pltpu.CompilerParams(vmem_limit_bytes=VMEM_LIMIT)


def cost(gflop, mbyte):
    return pl.CostEstimate(flops=int(gflop * 1e9), bytes_accessed=int(mbyte * 1e6), transcendentals=0)


def gelu_both(v):
    a = (GELU_K * GELU_C) * (v * v) + GELU_K
    half = 0.5 * jnp.tanh(v * a) + 0.5
    value = v * half
    return value, half + (value * (1.0 - half)) * (6.0 * a - 4.0 * GELU_K)


def pair_shape(c):
    return (4, FS // 2, FACES, FS + 2, ROLL, c)


def grad_pairs(c):
    return (4, FS // 2, FACES, FS, ROLL, c)


def pair_rows(p_ref, v_ref, face, count):
    for t in range(FS // 2):
        d0, d1, d2, d3 = (p_ref[face : face + count, 2 * t + q] for q in range(4))
        v_ref[0, t, face : face + count] = d0 - d2
        v_ref[1, t, face : face + count] = d1 + d2
        v_ref[2, t, face : face + count] = d2 - d1
        v_ref[3, t, face : face + count] = d1 - d3


def pair_weights(w_ref, u_ref):
    c = w_ref.shape[1]
    for b in range(3):
        g0, g1, g2 = (w_ref[(3 * a + b) * c : (3 * a + b + 1) * c].astype(F32) for a in range(3))
        outside, middle = 0.5 * (g0 + g2), 0.5 * g1
        u_ref[0, b] = (outside + middle).astype(BF)
        u_ref[1, b] = (outside - middle).astype(BF)


def dot_back(v, w):
    return lax.dot_general(v, w, (((1,), (1,)), ((), ())), preferred_element_type=F32)


def conv(v_ref, w_ref, u_ref, face, count, back=False):
    c = w_ref.shape[1]
    products = []
    for k in range(4):
        acc = None
        for b in range(3):
            v = v_ref[k, :, face : face + count, b : b + FS].reshape(-1, c)
            col = 2 - b if back else b
            if k in (0, 3):
                t = 3 * (2 if (k == 3) != back else 0) + col
                g = w_ref[t * c : (t + 1) * c]
            else:
                g = u_ref[k - 1, col]
            part = dot_back(v, g) if back else jnp.dot(v, g, preferred_element_type=F32)
            acc = part if acc is None else acc + part
        products.append(acc.reshape(FS // 2, count, FS, ROLL, c))
    m0, m1, m2, m3 = products
    even, odd = m0 + m1 + m2, m1 - m2 - m3
    return [(odd if i % 2 else even)[i // 2] for i in range(FS)]


def by_rows(ref, face, count, first_row, first_col):
    cols = slice(first_col, first_col + FS)
    rows = [ref[face : face + count, first_row + i, cols] for i in range(FS)]
    return jnp.stack(rows).reshape(-1, ref.shape[-1])


def outer(p, g):
    c = p.shape[-1]
    return lax.dot_general(
        p.reshape(-1, c), g.reshape(-1, c), (((0,), (0,)), ((), ())), preferred_element_type=F32
    )


def zero_corners(p_ref):
    zero = jnp.zeros((FACES, 1, 1, ROLL, p_ref.shape[-1]), p_ref.dtype)
    for i in (0, FS + 1):
        for j in (0, FS + 1):
            p_ref[:, i : i + 1, j : j + 1] = zero


def neighbour(ids_ref, side, face):
    return ids_ref[4 + side * FACES + face]


def fill_halo(ids_ref, p_ref):
    for face in range(FACES):
        p_ref[face, 0, 1 : FS + 1] = p_ref[neighbour(ids_ref, 0, face), FS, 1 : FS + 1]
        p_ref[face, 1 : FS + 1, FS + 1] = p_ref[neighbour(ids_ref, 1, face), 1 : FS + 1, 1]
        p_ref[face, FS + 1, 1 : FS + 1] = p_ref[neighbour(ids_ref, 2, face), 1, 1 : FS + 1]
        p_ref[face, 1 : FS + 1, 0] = p_ref[neighbour(ids_ref, 3, face), 1 : FS + 1, FS]
    zero_corners(p_ref)


def add_edges(e_ref, ids_ref, face, p_ref):
    rows = cols = slice(1, FS + 1)
    edges = (p_ref[face, 1, cols], p_ref[face, rows, FS], p_ref[face, FS, cols], p_ref[face, rows, 1])
    for side, part in enumerate(edges):
        to = neighbour(ids_ref, side, face)
        e_ref[to, side] = e_ref[to, side] + part.astype(F32)


def fill_halo_back(e_ref, p_ref):
    for face in range(FACES):
        p_ref[face, FS + 1, 1 : FS + 1] = e_ref[face, 0].astype(p_ref.dtype)
        p_ref[face, 1 : FS + 1, 0] = e_ref[face, 1].astype(p_ref.dtype)
        p_ref[face, 0, 1 : FS + 1] = e_ref[face, 2].astype(p_ref.dtype)
        p_ref[face, 1 : FS + 1, FS + 1] = e_ref[face, 3].astype(p_ref.dtype)
    zero_corners(p_ref)


def edge_sums(c):
    return pltpu.VMEM((FACES, 4, FS, ROLL, c), F32)


class Plan:
    def __init__(self, sizes, channels):
        self.tiles, self.ranks = sizes["tile"], sizes["fsdp"]
        self.c = channels
        self.conv = 9 * channels
        self.shard = self.conv // self.ranks
        self.skip_shard = channels // self.ranks
        self.piece = self.shard // (2 * self.tiles)
        self.skip_piece = self.skip_shard // (2 * self.tiles)
        self.late = self.piece + self.skip_piece
        self.chunk = self.piece + self.late
        self.split = self.piece % 8 == 0 and self.skip_piece % 8 == 0
        self.halves = self.shard // 2, self.shard // 2, self.skip_shard // 2
        self.sent = self.halves
        self.direct = ()
        if self.split:
            self.sent = self.piece, self.piece, self.skip_piece
            self.direct = tuple(d for d in (1, 2) if d < self.ranks - 1)
        self.start = {}
        rows = 0
        for d in range(1, self.ranks):
            self.start[d] = rows
            rows += self.sent[0] if d in self.direct else sum(self.sent)


def place_rows(plan, ids_ref, dst_ref, value, first_row, piece, offset):
    core, tile, rank = ids_ref[0], ids_ref[1], ids_ref[2]
    end = first_row + value.shape[0]
    row = first_row
    while row < end:
        number = row // piece
        stop = min(end, (number + 1) * piece)
        to_tile = number % plan.tiles
        to_core = number // plan.tiles % 2
        to_rank = number // (2 * plan.tiles)
        at = offset + row - number * piece
        dst_ref[
            to_core ^ core,
            to_tile ^ tile,
            to_rank ^ rank,
            at : at + stop - row,
        ] = value[row - first_row : stop - first_row]
        row = stop


def weight_grad(plan, ids_ref, v_ref, g_ref, z_ref, dst_ref):
    c = plan.c
    halves = range(FS // 2)
    cols = slice(1, FS + 1)
    for t in halves:
        y0, y1 = g_ref[:, 2 * t + 1, cols], g_ref[:, 2 * t + 2, cols]
        z_ref[0, t] = y0
        z_ref[1, t] = (y0 + y1) * 0.5
        z_ref[2, t] = (y0 - y1) * 0.5
        z_ref[3, t] = y1
    for b in range(3):
        m0, m1, m2, m3 = (outer(v_ref[k, :, :, b : b + FS], z_ref[k]) for k in range(4))
        both = m1 + m2
        for a, part in enumerate((m0 + both, m1 - m2, both - m3)):
            place_rows(plan, ids_ref, dst_ref, part.astype(BF), (3 * a + b) * c, plan.piece, 0)


def pack(plan, ids, weights, rows, shared, parts):
    c = plan.c
    count = len(weights)

    def kernel(ids_ref, *refs):
        rows_ref, sem = refs[count + len(parts) :]
        loads = []
        at = 0
        for k in range(count):
            hbm = refs[k]
            start = ids_ref[0] * (hbm.shape[0] // 2)
            if shared:
                start = start + ids_ref[1] * rows[k]
            source = hbm.at[pl.ds(pl.multiple_of(start, 8), rows[k])]
            loads.append(pltpu.make_async_copy(source, rows_ref.at[pl.ds(at, rows[k])], sem.at[k]))
            at += rows[k]
        for load in loads:
            load.start()
        for load in loads:
            load.wait()
        for k, part in enumerate(parts):
            refs[count + k][...] = rows_ref[0:part].astype(BF)

    return pl.pallas_call(
        kernel,
        in_specs=[SMEM] + [HBM] * count,
        out_specs=[VMEM] * len(parts),
        out_shape=[jax.ShapeDtypeStruct((v, c), BF) for v in parts],
        scratch_shapes=[pltpu.VMEM((sum(rows), c), F32), pltpu.SemaphoreType.DMA((count,))],
        compiler_params=params(),
        cost_estimate=cost(0, 0),
        name="pack",
    )(ids, *(in_hbm(v) for v in weights))


def below(arrays):
    rows = [v.shape[0] for v in arrays]

    def kernel(*refs):
        at = 0
        for ref, count in zip(refs, rows):
            refs[-1][at : at + count] = ref[...]
            at += count

    return pl.pallas_call(
        kernel,
        in_specs=[VMEM] * len(rows),
        out_specs=VMEM,
        out_shape=jax.ShapeDtypeStruct((sum(rows), arrays[0].shape[1]), BF),
        compiler_params=params(),
        cost_estimate=cost(0, 0),
        name="below",
    )(*arrays)


def join_rows(plan, ids_ref, low_ref, pieces, w_ref, rows):
    rank = ids_ref[2]
    w_ref[pl.ds(pl.multiple_of(rank * rows, 8), rows)] = low_ref[...]
    for ref, index, d, row in pieces:
        start = (rank ^ d) * rows + row
        part = ref[index]
        w_ref[pl.ds(pl.multiple_of(start, 8), part.shape[0])] = part


def received(plan, ids_ref, near_refs, far_refs, weight):
    core, tile = ids_ref[0], ids_ref[1]
    rows = plan.sent[weight]
    pieces = []
    for side, group in ((core, near_refs), (1 - core, far_refs)):
        for e, ref in enumerate(group):
            row = side * plan.halves[weight]
            if plan.split:
                row = row + (tile ^ e) * rows
            for d in range(1, plan.ranks):
                if weight == 0 or d not in plan.direct:
                    at = plan.start[d] + sum(plan.sent[:weight])
                    pieces.append((ref, pl.ds(at, rows), d, row))
    return pieces


def received_directly(plan, ids_ref, near_refs, far_refs, at, weight):
    core = ids_ref[0]
    rows = plan.halves[weight]
    pieces = []
    for side, group in ((core, near_refs), (1 - core, far_refs)):
        for ref, d in zip(group, plan.direct):
            pieces.append((ref, pl.ds(at, rows), d, side * rows))
    return pieces


def enter(plan, ids, x, cot, weights, after):
    c = plan.c

    def kernel(ids_ref, x_hbm, cot_hbm, *refs):
        refs = refs[:3] + refs[3 + len(after) :]
        weights_hbm, xp_ref, go_ref, dw_ref = refs[:3], *refs[3:6]
        low_refs, cot_ref, weight_refs, sem = refs[6:9], refs[9], refs[10:13], refs[13]
        load_x = pltpu.make_async_copy(x_hbm, inner(xp_ref), sem.at[FACES])
        load_x.start()
        loads = []
        for face in range(FACES):
            loads.append(pltpu.make_async_copy(cot_hbm.at[face], cot_ref.at[face], sem.at[face]))
            loads[-1].start()
        low_loads = []
        for k in range(3):
            low_loads.append(
                pltpu.make_async_copy(weights_hbm[k], weight_refs[k], sem.at[FACES + 1 + k])
            )
            low_loads[-1].start()
        live = lax.broadcasted_iota(jnp.int32, (FS, FS, ROLL, c), 2) < ids_ref[3]
        for face in range(FACES):
            loads[face].wait()
            go_ref[face] = jnp.where(live, cot_ref[face].astype(F32), 0.0).astype(BF)
        load_x.wait()
        fill_halo(ids_ref, xp_ref)
        dw_ref[...] = outer(xp_ref[:, 1 : FS + 1, 1 : FS + 1], go_ref[...]).astype(dw_ref.dtype)
        for k in range(3):
            low_loads[k].wait()
            low_refs[k][...] = weight_refs[k][...].astype(BF)

    return pl.pallas_call(
        kernel,
        in_specs=[SMEM] + [HBM] * 5 + [VMEM] * len(after),
        out_specs=[VMEM] * 6,
        out_shape=[
            jax.ShapeDtypeStruct(padded(c), BF),
            field(c),
            jax.ShapeDtypeStruct((c, c), BF),
            *(jax.ShapeDtypeStruct(v.shape, BF) for v in weights),
        ],
        scratch_shapes=[
            pltpu.VMEM(field(c).shape, BF),
            *(pltpu.VMEM(v.shape, F32) for v in weights),
            pltpu.SemaphoreType.DMA((FACES + 4,)),
        ],
        compiler_params=params(),
        cost_estimate=cost(0, 0),
        name="enter",
    )(ids, in_hbm(x), in_hbm(cot), *(in_hbm(v) for v in weights), *after)


def first(plan, ids, xp, low, near, far):
    c = plan.c
    count = len(near)

    def kernel(ids_ref, xp_ref, low_ref, *refs):
        near_refs, far_refs = refs[:count], refs[count : 2 * count]
        hp_ref, slope_ref, w_ref, u_ref, v_ref = refs[2 * count :]
        pieces = received(plan, ids_ref, near_refs, far_refs, 0)
        join_rows(plan, ids_ref, low_ref, pieces, w_ref, plan.shard)
        pair_weights(w_ref, u_ref)
        for face in range(0, FACES, GROUP):
            faces = slice(face, face + GROUP)
            pair_rows(xp_ref, v_ref, face, GROUP)
            for i, pre in enumerate(conv(v_ref, w_ref, u_ref, face, GROUP)):
                hidden, slope = gelu_both(pre)
                hp_ref[faces, i + 1, 1 : FS + 1] = hidden.astype(BF)
                slope_ref[faces, i] = slope.astype(BF)
        fill_halo(ids_ref, hp_ref)

    return pl.pallas_call(
        kernel,
        in_specs=[SMEM] + [VMEM] * (2 + 2 * count),
        out_specs=[VMEM] * 4,
        out_shape=[
            jax.ShapeDtypeStruct(padded(c), BF),
            field(c),
            jax.ShapeDtypeStruct((plan.conv, c), BF),
            jax.ShapeDtypeStruct((2, 3, c, c), BF),
        ],
        scratch_shapes=[pltpu.VMEM(pair_shape(c), BF)],
        compiler_params=params(),
        cost_estimate=cost(0, 0),
        name="first",
    )(ids, xp, low, *near, *far)


def second(plan, ids, hp, xp, go, dws, low, low_skip, near, far, near_half, far_half):
    c = plan.c
    count = len(near)
    halves = len(near_half)

    def kernel(ids_ref, hp_ref, xp_ref, go_ref, dws_ref, low_ref, lows_ref, *refs):
        groups = refs[:count], refs[count : 2 * count]
        refs = refs[2 * count :]
        direct = refs[:halves], refs[halves : 2 * halves]
        refs = refs[2 * halves :]
        out_hbm, gp_ref, w_ref, u_ref, ws_ref, keep_ref, send_ref = refs[:7]
        out_ref, e_ref, dw_ref, v_ref, z_ref, sem_out = refs[7:]
        pieces = received(plan, ids_ref, *groups, 1)
        pieces += received_directly(plan, ids_ref, *direct, 0, 1)
        join_rows(plan, ids_ref, low_ref, pieces, w_ref, plan.shard)
        pieces = received(plan, ids_ref, *groups, 2)
        pieces += received_directly(plan, ids_ref, *direct, plan.halves[1], 2)
        join_rows(plan, ids_ref, lows_ref, pieces, ws_ref, plan.skip_shard)
        e_ref[...] = jnp.zeros_like(e_ref)
        place_rows(plan, ids_ref, dw_ref, dws_ref[...], 0, plan.skip_piece, plan.piece)
        pair_weights(w_ref, u_ref)
        for face in range(0, FACES, GROUP):
            faces = slice(face, face + GROUP)
            pair_rows(hp_ref, v_ref, face, GROUP)
            skip = jnp.dot(
                by_rows(xp_ref, face, GROUP, 1, 1), ws_ref[...], preferred_element_type=F32
            ).reshape(FS, GROUP, FS, ROLL, c)
            for i, pre in enumerate(conv(v_ref, w_ref, u_ref, face, GROUP)):
                value, slope = gelu_both(pre)
                out_ref[faces, i] = (value + skip[i]).astype(BF)
                low_grad = (go_ref[faces, i].astype(F32) * slope).astype(BF)
                gp_ref[faces, i + 1, 1 : FS + 1] = low_grad
            for one in range(face, face + GROUP):
                add_edges(e_ref, ids_ref, one, gp_ref)
        store = pltpu.make_async_copy(out_ref, out_hbm, sem_out)
        store.start()
        weight_grad(plan, ids_ref, v_ref, gp_ref, z_ref, dw_ref)
        keep_ref[...] = dw_ref[0]
        send_ref[...] = dw_ref[1]
        fill_halo_back(e_ref, gp_ref)
        store.wait()

    sums = jax.ShapeDtypeStruct((plan.tiles, plan.ranks, plan.late, c), BF)
    return pl.pallas_call(
        kernel,
        in_specs=[SMEM] + [VMEM] * (6 + 2 * count + 2 * halves),
        out_specs=[HBM] + [VMEM] * 6,
        out_shape=[
            field(c),
            jax.ShapeDtypeStruct(padded(c), BF),
            jax.ShapeDtypeStruct((plan.conv, c), BF),
            jax.ShapeDtypeStruct((2, 3, c, c), BF),
            jax.ShapeDtypeStruct((c, c), BF),
            sums,
            sums,
        ],
        scratch_shapes=[
            pltpu.VMEM(field(c).shape, BF),
            edge_sums(c),
            pltpu.VMEM((2,) + sums.shape, BF),
            pltpu.VMEM(pair_shape(c), BF),
            pltpu.VMEM(grad_pairs(c), BF),
            pltpu.SemaphoreType.DMA,
        ],
        compiler_params=params(),
        cost_estimate=cost(9, 16),
        name="second",
    )(ids, hp, xp, go, dws, low, low_skip, *near, *far, *near_half, *far_half)


def hidden_back(plan, ids, gp, w, u, slope, xp, after):
    c = plan.c

    def kernel(ids_ref, gp_ref, w_ref, u_ref, slope_ref, xp_ref, _, op_ref, keep_ref, send_ref, *refs):
        e_ref, v_ref, z_ref, dw_ref = refs
        e_ref[...] = jnp.zeros_like(e_ref)
        for face in range(0, FACES, GROUP):
            faces = slice(face, face + GROUP)
            pair_rows(gp_ref, v_ref, face, GROUP)
            for i, grad in enumerate(conv(v_ref, w_ref, u_ref, face, GROUP, back=True)):
                low_grad = (grad * slope_ref[faces, i].astype(F32)).astype(BF)
                op_ref[faces, i + 1, 1 : FS + 1] = low_grad
            for one in range(face, face + GROUP):
                add_edges(e_ref, ids_ref, one, op_ref)
        pair_rows(xp_ref, v_ref, 0, FACES)
        weight_grad(plan, ids_ref, v_ref, op_ref, z_ref, dw_ref)
        fill_halo_back(e_ref, op_ref)
        keep_ref[...] = dw_ref[0]
        send_ref[...] = dw_ref[1]

    sums = (plan.tiles, plan.ranks, plan.piece, c)
    return pl.pallas_call(
        kernel,
        in_specs=[SMEM] + [VMEM] * 6,
        out_specs=[VMEM] * 3,
        out_shape=[jax.ShapeDtypeStruct(v, BF) for v in (padded(c), sums, sums)],
        scratch_shapes=[
            edge_sums(c),
            pltpu.VMEM(pair_shape(c), BF),
            pltpu.VMEM(grad_pairs(c), BF),
            pltpu.VMEM((2,) + sums, BF),
        ],
        compiler_params=params(),
        cost_estimate=cost(0, 0),
        name="hidden_back",
    )(ids, gp, w, u, slope, xp, after)


def add_up(parts):
    acc = parts[0].astype(F32)
    for part in parts[1:]:
        acc = acc + part.astype(F32)
    return acc.astype(BF)


def tile_sums(plan, parts, below_last=None, after=()):
    tiles, ranks = plan.tiles, plan.ranks
    rows = parts[0].shape[1]
    extra = [] if below_last is None else [below_last]
    shapes = [rows] * (ranks - 1) + [rows + sum(v.shape[0] for v in extra)]
    inputs = [*parts, *extra, *after]

    def kernel(*refs):
        results = refs[len(inputs) :]
        for r in range(ranks):
            results[r][0:rows] = add_up([ref[r] for ref in refs[:tiles]])
        if extra:
            results[-1][rows:] = refs[tiles][...]

    return pl.pallas_call(
        kernel,
        in_specs=[VMEM] * len(inputs),
        out_specs=[VMEM] * ranks,
        out_shape=[jax.ShapeDtypeStruct((v, plan.c), BF) for v in shapes],
        compiler_params=params(),
        cost_estimate=cost(0, 0),
        name="tile_sums",
    )(*inputs)


def rank_sums(plan, early, late, last):
    piece = plan.piece
    count = len(early)
    inputs = [*early, *late, last]

    def kernel(*refs):
        rows_ref = refs[len(inputs) - 1]
        to = refs[-1]
        to[0:piece] = add_up([ref[...] for ref in refs[:count]] + [rows_ref[0:piece]])
        to[piece:] = add_up([ref[...] for ref in refs[count:-2]] + [rows_ref[piece:]])

    return pl.pallas_call(
        kernel,
        in_specs=[VMEM] * len(inputs),
        out_specs=VMEM,
        out_shape=jax.ShapeDtypeStruct((plan.chunk, plan.c), BF),
        compiler_params=params(),
        cost_estimate=cost(0, 0),
        name="rank_sums",
    )(*inputs)


def inputs_back_kernel(gp_ref, w_ref, u_ref, ws_ref, go_ref, out_hbm, out_ref, v_ref, sem):
    c = w_ref.shape[1]
    stores = []
    for face in range(0, FACES, GROUP):
        faces = slice(face, face + GROUP)
        pair_rows(gp_ref, v_ref, face, GROUP)
        skip = dot_back(by_rows(go_ref, face, GROUP, 0, 0), ws_ref[...])
        skip = skip.reshape(FS, GROUP, FS, ROLL, c)
        for i, grad in enumerate(conv(v_ref, w_ref, u_ref, face, GROUP, back=True)):
            out_ref[faces, i] = grad + skip[i]
        part = pl.ds(face, GROUP)
        copy = pltpu.make_async_copy(out_ref.at[part], out_hbm.at[part], sem.at[face // GROUP])
        copy.start()
        stores.append(copy)
    for store in stores:
        store.wait()


def inputs_back(gp, w, u, ws, go):
    c = w.shape[1]
    return pl.pallas_call(
        inputs_back_kernel,
        in_specs=[VMEM] * 5,
        out_specs=HBM,
        out_shape=field(c, F32),
        scratch_shapes=[
            pltpu.VMEM(field(c).shape, F32),
            pltpu.VMEM(pair_shape(c), BF),
            pltpu.SemaphoreType.DMA((FACES // GROUP,)),
        ],
        compiler_params=params(),
        cost_estimate=cost(0, 0),
        name="inputs_back",
    )(gp, w, u, ws, go)


def adamw(weight, moment, square, grad, rate):
    moment_new = 0.9 * moment + 0.1 * grad
    square_new = 0.999 * square + 0.001 * grad * grad
    fix_one = 1.0 - 0.9**STEP_COUNT
    fix_two = 1.0 - 0.999**STEP_COUNT
    weight_new = weight - rate * (
        moment_new / fix_one / (jnp.sqrt(square_new / fix_two) + 1e-08) + 0.01 * weight
    )
    return (weight_new, moment_new, square_new)


UPDATE_STEPS = 4


def update(plan, ids, grads, sets, far, old=()):
    c, tiles = plan.c, plan.tiles

    def kernel(ids_ref, grads_ref, *refs):
        state = refs[:9]
        new, done_refs = refs[9 + len(old) : 18 + len(old)], refs[18 + len(old) : 27 + len(old)]
        sum_ref, sem = refs[27 + len(old) :]
        core, tile = ids_ref[0], ids_ref[1]
        side = 1 - core if far else core
        at = 0
        stores = []
        for n in range(3):
            piece = plan.skip_piece if n == 2 else plan.piece
            rows = tiles * piece
            for d in range(tiles):
                part = grads_ref[d, at : at + piece].astype(F32)
                if piece % 8:
                    for t in range(tiles):

                        def put(part=part, t=t, piece=piece):
                            sum_ref[t * piece : (t + 1) * piece] = part

                        pl.when(tile ^ d == t)(put)
                else:
                    sum_ref[pl.ds(pl.multiple_of((tile ^ d) * piece, 8), piece)] = part
            at += piece
            rate = (2 * rows * plan.ranks) ** (-0.5)
            step = rows // UPDATE_STEPS if rows % (8 * UPDATE_STEPS) == 0 else rows
            for row in range(0, rows, step):
                here = pl.ds(pl.multiple_of(side * rows + row, 8), step)
                done = adamw(*(state[3 * n + k][here] for k in range(3)), sum_ref[row : row + step], rate)
                for k in range(3 * n, 3 * n + 3):
                    done_refs[k][row : row + step] = done[k - 3 * n]
                    source = done_refs[k].at[pl.ds(row, step)]
                    number = UPDATE_STEPS * k + row // step
                    stores.append(pltpu.make_async_copy(source, new[k].at[here], sem.at[number]))
                    stores[-1].start()
        for store in stores:
            store.wait()

    shapes = [v.shape for v in sets]
    return pl.pallas_call(
        kernel,
        in_specs=[SMEM] + [VMEM] * 10 + [HBM] * len(old),
        out_specs=[HBM] * 9,
        out_shape=[jax.ShapeDtypeStruct(v, F32) for v in shapes],
        scratch_shapes=[
            *(pltpu.VMEM((v[0] // 2, c), F32) for v in shapes),
            pltpu.VMEM((plan.shard // 2, c), F32),
            pltpu.SemaphoreType.DMA((9 * UPDATE_STEPS,)),
        ],
        input_output_aliases={11 + k: k for k in range(len(old))},
        compiler_params=params(),
        cost_estimate=cost(2, 9),
        name="update",
    )(ids, grads, *sets, *old)


def send(v, axis, size, step):
    return lax.ppermute(v, axis, [(i, i ^ step) for i in range(size)])


def total(*parts):
    acc = parts[0].astype(F32)
    for part in parts[1:]:
        acc = acc + part.astype(F32)
    return acc.astype(BF)


def make_body(sizes):
    tiles, ranks = sizes["tile"], sizes["fsdp"]

    def to_core(v):
        return send(v, "core", 2, 1)

    def to_tile(v, d):
        return send(v, "tile", tiles, d)

    def to_rank(v, d):
        return send(v, "fsdp", ranks, d)

    def per_device(
        inputs,
        cotangent,
        lengths,
        face_table,
        w_first,
        w_second,
        w_skip,
        mom_first,
        sq_first,
        mom_second,
        sq_second,
        mom_skip,
        sq_skip,
    ):
        plan = Plan(sizes, inputs.shape[-1])
        x = jnp.transpose(inputs[0], (1, 2, 3, 0, 4))
        cot = jnp.transpose(cotangent[0], (1, 2, 3, 0, 4))
        places = jnp.stack([lax.axis_index(n) for n in ("core", "tile", "fsdp")]).astype(jnp.int32)
        weights = w_first, w_second, w_skip
        parts = (plan.sent[0], sum(plan.sent))
        some, sent = pack(plan, places, weights, plan.sent, plan.split, parts)
        near = [to_rank(some if d in plan.direct else sent, d) for d in range(1, ranks)]
        near = [below(near)]
        near_half, after = [], near[:]
        if plan.split:
            near += [to_tile(near[0], e) for e in range(1, tiles)]
            (half,) = pack(plan, places, weights[1:], plan.halves[1:], False, (sum(plan.halves[1:]),))
            near_half = [to_rank(half, d) for d in plan.direct]
            after.append(half)
        ids = jnp.concatenate([places, lengths, face_table.T.reshape(-1)])
        xp, go, dws, low1, low2, low3 = enter(plan, ids, x, cot, weights, after)
        xp, near, near_half = lax.optimization_barrier((xp, near, near_half))
        far = [to_core(v) for v in near]
        far_half = [to_core(v) for v in near_half]
        hp, slope, w1, u1 = first(plan, ids, xp, low1, near, far)
        hp, far_half = lax.optimization_barrier((hp, far_half))
        output, gp, w2, u2, ws, keep2, away2 = second(
            plan, ids, hp, xp, go, dws, low2, low3, near, far, near_half, far_half
        )
        came2 = to_core(away2)
        parts2 = [total(keep2[d], came2[d]) for d in range(tiles)]
        op, keep1, away1 = hidden_back(plan, ids, gp, w2, u2, slope, xp, parts2[0])
        late = [parts2[0]] + [to_tile(parts2[d], d) for d in range(1, tiles)]
        late, away1 = lax.optimization_barrier((late, away1))
        came1 = to_core(away1)
        late = tile_sums(plan, late)
        parts1 = [total(keep1[d], came1[d]) for d in range(tiles)]
        op, parts1, late = lax.optimization_barrier((op, parts1, late))
        early = [parts1[0]] + [to_tile(parts1[d], d) for d in range(1, tiles)]
        late, late_last = late[:-1], late[-1]
        late = [late[0]] + [to_rank(v, d) for d, v in enumerate(late) if d]
        grad_inputs = inputs_back(op, w1, u1, ws, go)
        early, late, grad_inputs = lax.optimization_barrier((early, late, grad_inputs))
        early = tile_sums(plan, early, late_last, late[1:])
        early = [early[0]] + [to_rank(v, d) for d, v in enumerate(early) if d]
        mine = rank_sums(plan, early[:-1], late, early[-1])
        near = jnp.stack([mine] + [to_tile(mine, d) for d in range(1, tiles)])
        far = to_core(near)
        sets = (
            w_first,
            mom_first,
            sq_first,
            w_second,
            mom_second,
            sq_second,
            w_skip,
            mom_skip,
            sq_skip,
        )
        news = update(plan, ids, near, sets, False)
        news = update(plan, ids, far, sets, True, news)
        output = jnp.transpose(output, (3, 0, 1, 2, 4))[None]
        grad_inputs = jnp.transpose(grad_inputs, (3, 0, 1, 2, 4))[None]
        return (output, grad_inputs, *news)

    return per_device


def solution(mesh):
    pairs = mesh.shape["dp"] // 2
    ranks = mesh.shape["fsdp"]
    fine = Mesh(mesh.devices.reshape(pairs, 2, ranks), ("tile", "core", "fsdp"))
    sizes = {"tile": pairs, "core": 2, "fsdp": ranks}
    every = ("tile", "core", "fsdp")
    fields = P(every, None, None, None, None, None)
    rows = P("fsdp", None)
    return jax.shard_map(
        make_body(sizes),
        mesh=fine,
        in_specs=(fields, fields, P(every), P()) + (rows,) * 9,
        out_specs=(fields, fields) + (rows,) * 9,
        check_vma=False,
    )
```

```python
import functools

import jax
import jax.numpy as jnp
from jax import lax
from jax.experimental import pallas as pl
from jax.experimental.pallas import tpu as pltpu
from jax.sharding import Mesh
from jax.sharding import PartitionSpec as P

STEP_COUNT = 10
BF = jnp.bfloat16
F32 = jnp.float32
FS = 6
ROLL = 8
FACES = 12
GELU_K = 0.7978845608028654
GELU_C = 0.044715
VMEM_LIMIT = 30 * 2**20
GROUP = 2


ANY = pl.BlockSpec(memory_space=pl.ANY)
HBM = pl.BlockSpec(memory_space=pltpu.HBM)
VMEM = pl.BlockSpec(memory_space=pltpu.VMEM)
SMEM = pl.BlockSpec(memory_space=pltpu.SMEM)


def field(c, dtype=BF):
    return jax.ShapeDtypeStruct((FACES, FS, FS, ROLL, c), dtype)


def padded(c):
    return (FACES, FS + 2, FS + 2, ROLL, c)


def inner(ref):
    return ref.at[:, 1 : FS + 1, 1 : FS + 1]


def in_hbm(v):
    return pltpu.with_memory_space_constraint(v, pltpu.HBM)


def params():
    return pltpu.CompilerParams(vmem_limit_bytes=VMEM_LIMIT)


def cost(gflop, mbyte):
    return pl.CostEstimate(flops=int(gflop * 1e9), bytes_accessed=int(mbyte * 1e6), transcendentals=0)


def gelu_both(v):
    a = (GELU_K * GELU_C) * (v * v) + GELU_K
    half = 0.5 * jnp.tanh(v * a) + 0.5
    value = v * half
    return value, half + (value * (1.0 - half)) * (6.0 * a - 4.0 * GELU_K)


def pair_shape(c):
    return (4, FS // 2, FACES, FS + 2, ROLL, c)


def grad_pairs(c):
    return (4, FS // 2, FACES, FS, ROLL, c)


def pair_rows(p_ref, v_ref, face, count):
    for t in range(FS // 2):
        d0, d1, d2, d3 = (p_ref[face : face + count, 2 * t + q] for q in range(4))
        v_ref[0, t, face : face + count] = d0 - d2
        v_ref[1, t, face : face + count] = d1 + d2
        v_ref[2, t, face : face + count] = d2 - d1
        v_ref[3, t, face : face + count] = d1 - d3


def pair_weights(w_ref, u_ref):
    c = w_ref.shape[1]
    for b in range(3):
        g0, g1, g2 = (w_ref[(3 * a + b) * c : (3 * a + b + 1) * c].astype(F32) for a in range(3))
        outside, middle = 0.5 * (g0 + g2), 0.5 * g1
        u_ref[0, b] = (outside + middle).astype(BF)
        u_ref[1, b] = (outside - middle).astype(BF)


def dot_back(v, w):
    return lax.dot_general(v, w, (((1,), (1,)), ((), ())), preferred_element_type=F32)


def conv(v_ref, w_ref, u_ref, face, count, back=False):
    c = w_ref.shape[1]
    products = []
    for k in range(4):
        acc = None
        for b in range(3):
            v = v_ref[k, :, face : face + count, b : b + FS].reshape(-1, c)
            col = 2 - b if back else b
            if k in (0, 3):
                t = 3 * (2 if (k == 3) != back else 0) + col
                g = w_ref[t * c : (t + 1) * c]
            else:
                g = u_ref[k - 1, col]
            part = dot_back(v, g) if back else jnp.dot(v, g, preferred_element_type=F32)
            acc = part if acc is None else acc + part
        products.append(acc.reshape(FS // 2, count, FS, ROLL, c))
    m0, m1, m2, m3 = products
    even, odd = m0 + m1 + m2, m1 - m2 - m3
    return [(odd if i % 2 else even)[i // 2] for i in range(FS)]


def by_rows(ref, face, count, first_row, first_col):
    cols = slice(first_col, first_col + FS)
    rows = [ref[face : face + count, first_row + i, cols] for i in range(FS)]
    return jnp.stack(rows).reshape(-1, ref.shape[-1])


def outer(p, g):
    c = p.shape[-1]
    return lax.dot_general(
        p.reshape(-1, c), g.reshape(-1, c), (((0,), (0,)), ((), ())), preferred_element_type=F32
    )


def zero_corners(p_ref):
    zero = jnp.zeros((FACES, 1, 1, ROLL, p_ref.shape[-1]), p_ref.dtype)
    for i in (0, FS + 1):
        for j in (0, FS + 1):
            p_ref[:, i : i + 1, j : j + 1] = zero


def neighbour(ids_ref, side, face):
    return ids_ref[4 + side * FACES + face]


def fill_halo(ids_ref, p_ref):
    for face in range(FACES):
        p_ref[face, 0, 1 : FS + 1] = p_ref[neighbour(ids_ref, 0, face), FS, 1 : FS + 1]
        p_ref[face, 1 : FS + 1, FS + 1] = p_ref[neighbour(ids_ref, 1, face), 1 : FS + 1, 1]
        p_ref[face, FS + 1, 1 : FS + 1] = p_ref[neighbour(ids_ref, 2, face), 1, 1 : FS + 1]
        p_ref[face, 1 : FS + 1, 0] = p_ref[neighbour(ids_ref, 3, face), 1 : FS + 1, FS]
    zero_corners(p_ref)


def add_edges(e_ref, ids_ref, face, p_ref):
    rows = cols = slice(1, FS + 1)
    edges = (p_ref[face, 1, cols], p_ref[face, rows, FS], p_ref[face, FS, cols], p_ref[face, rows, 1])
    for side, part in enumerate(edges):
        to = neighbour(ids_ref, side, face)
        e_ref[to, side] = e_ref[to, side] + part


def fill_halo_back(e_ref, p_ref):
    for face in range(FACES):
        p_ref[face, FS + 1, 1 : FS + 1] = e_ref[face, 0].astype(p_ref.dtype)
        p_ref[face, 1 : FS + 1, 0] = e_ref[face, 1].astype(p_ref.dtype)
        p_ref[face, 0, 1 : FS + 1] = e_ref[face, 2].astype(p_ref.dtype)
        p_ref[face, 1 : FS + 1, FS + 1] = e_ref[face, 3].astype(p_ref.dtype)
    zero_corners(p_ref)


def edge_sums(c):
    return pltpu.VMEM((FACES, 4, FS, ROLL, c), BF)


class Plan:
    def __init__(self, sizes, channels):
        self.tiles, self.ranks = sizes["tile"], sizes["fsdp"]
        self.c = channels
        self.conv = 9 * channels
        self.shard = self.conv // self.ranks
        self.skip_shard = channels // self.ranks
        self.piece = self.shard // (2 * self.tiles)
        self.skip_piece = self.skip_shard // (2 * self.tiles)
        self.late = self.piece + self.skip_piece
        self.chunk = self.piece + self.late
        self.split = self.piece % 8 == 0 and self.skip_piece % 8 == 0
        self.halves = self.shard // 2, self.shard // 2, self.skip_shard // 2
        self.sent = self.halves
        self.direct = ()
        if self.split:
            self.sent = self.piece, self.piece, self.skip_piece
            self.direct = tuple(d for d in (1, 2) if d < self.ranks - 1)
        self.start = {}
        rows = 0
        for d in range(1, self.ranks):
            self.start[d] = rows
            rows += self.sent[0] if d in self.direct else sum(self.sent)


def place_rows(plan, ids_ref, dst_ref, value, first_row, piece, offset):
    core, tile, rank = ids_ref[0], ids_ref[1], ids_ref[2]
    end = first_row + value.shape[0]
    row = first_row
    while row < end:
        number = row // piece
        stop = min(end, (number + 1) * piece)
        to_tile = number % plan.tiles
        to_core = number // plan.tiles % 2
        to_rank = number // (2 * plan.tiles)
        at = offset + row - number * piece
        dst_ref[
            to_core ^ core,
            to_tile ^ tile,
            to_rank ^ rank,
            at : at + stop - row,
        ] = value[row - first_row : stop - first_row]
        row = stop


def weight_grad(plan, ids_ref, v_ref, g_ref, z_ref, dst_ref):
    c = plan.c
    halves = range(FS // 2)
    cols = slice(1, FS + 1)
    for t in halves:
        y0, y1 = g_ref[:, 2 * t + 1, cols], g_ref[:, 2 * t + 2, cols]
        z_ref[0, t] = y0
        z_ref[1, t] = (y0 + y1) * 0.5
        z_ref[2, t] = (y0 - y1) * 0.5
        z_ref[3, t] = y1
    for b in range(3):
        m0, m1, m2, m3 = (outer(v_ref[k, :, :, b : b + FS], z_ref[k]) for k in range(4))
        both = m1 + m2
        for a, part in enumerate((m0 + both, m1 - m2, both - m3)):
            place_rows(plan, ids_ref, dst_ref, part.astype(BF), (3 * a + b) * c, plan.piece, 0)


def pack(plan, ids, weights, rows, shared, parts):
    c = plan.c
    count = len(weights)

    def kernel(ids_ref, *refs):
        rows_ref, sem = refs[count + len(parts) :]
        loads = []
        at = 0
        for k in range(count):
            hbm = refs[k]
            start = ids_ref[0] * (hbm.shape[0] // 2)
            if shared:
                start = start + ids_ref[1] * rows[k]
            source = hbm.at[pl.ds(pl.multiple_of(start, 8), rows[k])]
            loads.append(pltpu.make_async_copy(source, rows_ref.at[pl.ds(at, rows[k])], sem.at[k]))
            at += rows[k]
        for load in loads:
            load.start()
        for load in loads:
            load.wait()
        for k, part in enumerate(parts):
            refs[count + k][...] = rows_ref[0:part].astype(BF)

    return pl.pallas_call(
        kernel,
        in_specs=[SMEM] + [HBM] * count,
        out_specs=[VMEM] * len(parts),
        out_shape=[jax.ShapeDtypeStruct((v, c), BF) for v in parts],
        scratch_shapes=[pltpu.VMEM((sum(rows), c), F32), pltpu.SemaphoreType.DMA((count,))],
        compiler_params=params(),
        cost_estimate=cost(0, 0),
        name="pack",
    )(ids, *(in_hbm(v) for v in weights))


def below(arrays):
    rows = [v.shape[0] for v in arrays]

    def kernel(*refs):
        at = 0
        for ref, count in zip(refs, rows):
            refs[-1][at : at + count] = ref[...]
            at += count

    return pl.pallas_call(
        kernel,
        in_specs=[VMEM] * len(rows),
        out_specs=VMEM,
        out_shape=jax.ShapeDtypeStruct((sum(rows), arrays[0].shape[1]), BF),
        compiler_params=params(),
        cost_estimate=cost(0, 0),
        name="below",
    )(*arrays)


def join_rows(plan, ids_ref, low_ref, pieces, w_ref, rows):
    rank = ids_ref[2]
    w_ref[pl.ds(pl.multiple_of(rank * rows, 8), rows)] = low_ref[...]
    for ref, index, d, row in pieces:
        start = (rank ^ d) * rows + row
        part = ref[index]
        w_ref[pl.ds(pl.multiple_of(start, 8), part.shape[0])] = part


def received(plan, ids_ref, near_refs, far_refs, weight):
    core, tile = ids_ref[0], ids_ref[1]
    rows = plan.sent[weight]
    pieces = []
    for side, group in ((core, near_refs), (1 - core, far_refs)):
        for e, ref in enumerate(group):
            row = side * plan.halves[weight]
            if plan.split:
                row = row + (tile ^ e) * rows
            for d in range(1, plan.ranks):
                if weight == 0 or d not in plan.direct:
                    at = plan.start[d] + sum(plan.sent[:weight])
                    pieces.append((ref, pl.ds(at, rows), d, row))
    return pieces


def received_directly(plan, ids_ref, near_refs, far_refs, at, weight):
    core = ids_ref[0]
    rows = plan.halves[weight]
    pieces = []
    for side, group in ((core, near_refs), (1 - core, far_refs)):
        for ref, d in zip(group, plan.direct):
            pieces.append((ref, pl.ds(at, rows), d, side * rows))
    return pieces


def enter(plan, ids, x, cot, weights, after):
    c = plan.c

    def kernel(ids_ref, x_hbm, cot_hbm, *refs):
        refs = refs[:3] + refs[3 + len(after) :]
        weights_hbm, xp_ref, go_ref, dw_ref = refs[:3], *refs[3:6]
        low_refs, cot_ref, weight_refs, sem = refs[6:9], refs[9], refs[10:13], refs[13]
        load_x = pltpu.make_async_copy(x_hbm, inner(xp_ref), sem.at[FACES])
        load_x.start()
        loads = []
        for face in range(FACES):
            loads.append(pltpu.make_async_copy(cot_hbm.at[face], cot_ref.at[face], sem.at[face]))
            loads[-1].start()
        low_loads = []
        for k in range(3):
            low_loads.append(
                pltpu.make_async_copy(weights_hbm[k], weight_refs[k], sem.at[FACES + 1 + k])
            )
            low_loads[-1].start()
        live = lax.broadcasted_iota(jnp.int32, (FS, FS, ROLL, c), 2) < ids_ref[3]
        for face in range(FACES):
            loads[face].wait()
            go_ref[face] = jnp.where(live, cot_ref[face].astype(F32), 0.0).astype(BF)
        load_x.wait()
        fill_halo(ids_ref, xp_ref)
        dw_ref[...] = outer(xp_ref[:, 1 : FS + 1, 1 : FS + 1], go_ref[...]).astype(dw_ref.dtype)
        for k in range(3):
            low_loads[k].wait()
            low_refs[k][...] = weight_refs[k][...].astype(BF)

    return pl.pallas_call(
        kernel,
        in_specs=[SMEM] + [HBM] * 5 + [VMEM] * len(after),
        out_specs=[VMEM] * 6,
        out_shape=[
            jax.ShapeDtypeStruct(padded(c), BF),
            field(c),
            jax.ShapeDtypeStruct((c, c), BF),
            *(jax.ShapeDtypeStruct(v.shape, BF) for v in weights),
        ],
        scratch_shapes=[
            pltpu.VMEM(field(c).shape, BF),
            *(pltpu.VMEM(v.shape, F32) for v in weights),
            pltpu.SemaphoreType.DMA((FACES + 4,)),
        ],
        compiler_params=params(),
        cost_estimate=cost(0, 0),
        name="enter",
    )(ids, in_hbm(x), in_hbm(cot), *(in_hbm(v) for v in weights), *after)


def first(plan, ids, xp, low, near, far):
    c = plan.c
    count = len(near)

    def kernel(ids_ref, xp_ref, low_ref, *refs):
        near_refs, far_refs = refs[:count], refs[count : 2 * count]
        hp_ref, slope_ref, w_ref, u_ref, v_ref = refs[2 * count :]
        pieces = received(plan, ids_ref, near_refs, far_refs, 0)
        join_rows(plan, ids_ref, low_ref, pieces, w_ref, plan.shard)
        pair_weights(w_ref, u_ref)
        for face in range(0, FACES, GROUP):
            faces = slice(face, face + GROUP)
            pair_rows(xp_ref, v_ref, face, GROUP)
            for i, pre in enumerate(conv(v_ref, w_ref, u_ref, face, GROUP)):
                hidden, slope = gelu_both(pre)
                hp_ref[faces, i + 1, 1 : FS + 1] = hidden.astype(BF)
                slope_ref[faces, i] = slope.astype(BF)
        fill_halo(ids_ref, hp_ref)

    return pl.pallas_call(
        kernel,
        in_specs=[SMEM] + [VMEM] * (2 + 2 * count),
        out_specs=[VMEM] * 4,
        out_shape=[
            jax.ShapeDtypeStruct(padded(c), BF),
            field(c),
            jax.ShapeDtypeStruct((plan.conv, c), BF),
            jax.ShapeDtypeStruct((2, 3, c, c), BF),
        ],
        scratch_shapes=[pltpu.VMEM(pair_shape(c), BF)],
        compiler_params=params(),
        cost_estimate=cost(0, 0),
        name="first",
    )(ids, xp, low, *near, *far)


def second(plan, ids, hp, xp, go, dws, low, low_skip, near, far, near_half, far_half):
    c = plan.c
    count = len(near)
    halves = len(near_half)

    def kernel(ids_ref, hp_ref, xp_ref, go_ref, dws_ref, low_ref, lows_ref, *refs):
        groups = refs[:count], refs[count : 2 * count]
        refs = refs[2 * count :]
        direct = refs[:halves], refs[halves : 2 * halves]
        refs = refs[2 * halves :]
        out_hbm, gp_ref, w_ref, u_ref, ws_ref, keep_ref, send_ref = refs[:7]
        out_ref, e_ref, dw_ref, v_ref, z_ref, sem_out = refs[7:]
        pieces = received(plan, ids_ref, *groups, 1)
        pieces += received_directly(plan, ids_ref, *direct, 0, 1)
        join_rows(plan, ids_ref, low_ref, pieces, w_ref, plan.shard)
        pieces = received(plan, ids_ref, *groups, 2)
        pieces += received_directly(plan, ids_ref, *direct, plan.halves[1], 2)
        join_rows(plan, ids_ref, lows_ref, pieces, ws_ref, plan.skip_shard)
        e_ref[...] = jnp.zeros_like(e_ref)
        place_rows(plan, ids_ref, dw_ref, dws_ref[...], 0, plan.skip_piece, plan.piece)
        pair_weights(w_ref, u_ref)
        for face in range(0, FACES, GROUP):
            faces = slice(face, face + GROUP)
            pair_rows(hp_ref, v_ref, face, GROUP)
            skip = jnp.dot(
                by_rows(xp_ref, face, GROUP, 1, 1), ws_ref[...], preferred_element_type=F32
            ).reshape(FS, GROUP, FS, ROLL, c)
            for i, pre in enumerate(conv(v_ref, w_ref, u_ref, face, GROUP)):
                value, slope = gelu_both(pre)
                out_ref[faces, i] = (value + skip[i]).astype(BF)
                low_grad = (go_ref[faces, i].astype(F32) * slope).astype(BF)
                gp_ref[faces, i + 1, 1 : FS + 1] = low_grad
            for one in range(face, face + GROUP):
                add_edges(e_ref, ids_ref, one, gp_ref)
        store = pltpu.make_async_copy(out_ref, out_hbm, sem_out)
        store.start()
        weight_grad(plan, ids_ref, v_ref, gp_ref, z_ref, dw_ref)
        keep_ref[...] = dw_ref[0]
        send_ref[...] = dw_ref[1]
        fill_halo_back(e_ref, gp_ref)
        store.wait()

    sums = jax.ShapeDtypeStruct((plan.tiles, plan.ranks, plan.late, c), BF)
    return pl.pallas_call(
        kernel,
        in_specs=[SMEM] + [VMEM] * (6 + 2 * count + 2 * halves),
        out_specs=[HBM] + [VMEM] * 6,
        out_shape=[
            field(c),
            jax.ShapeDtypeStruct(padded(c), BF),
            jax.ShapeDtypeStruct((plan.conv, c), BF),
            jax.ShapeDtypeStruct((2, 3, c, c), BF),
            jax.ShapeDtypeStruct((c, c), BF),
            sums,
            sums,
        ],
        scratch_shapes=[
            pltpu.VMEM(field(c).shape, BF),
            edge_sums(c),
            pltpu.VMEM((2,) + sums.shape, BF),
            pltpu.VMEM(pair_shape(c), BF),
            pltpu.VMEM(grad_pairs(c), BF),
            pltpu.SemaphoreType.DMA,
        ],
        compiler_params=params(),
        cost_estimate=cost(9, 16),
        name="second",
    )(ids, hp, xp, go, dws, low, low_skip, *near, *far, *near_half, *far_half)


def hidden_back(plan, ids, gp, w, u, slope, xp, after):
    c = plan.c

    def kernel(ids_ref, gp_ref, w_ref, u_ref, slope_ref, xp_ref, _, op_ref, keep_ref, send_ref, *refs):
        e_ref, v_ref, z_ref, dw_ref = refs
        e_ref[...] = jnp.zeros_like(e_ref)
        for face in range(0, FACES, GROUP):
            faces = slice(face, face + GROUP)
            pair_rows(gp_ref, v_ref, face, GROUP)
            for i, grad in enumerate(conv(v_ref, w_ref, u_ref, face, GROUP, back=True)):
                low_grad = (grad * slope_ref[faces, i].astype(F32)).astype(BF)
                op_ref[faces, i + 1, 1 : FS + 1] = low_grad
            for one in range(face, face + GROUP):
                add_edges(e_ref, ids_ref, one, op_ref)
        pair_rows(xp_ref, v_ref, 0, FACES)
        weight_grad(plan, ids_ref, v_ref, op_ref, z_ref, dw_ref)
        fill_halo_back(e_ref, op_ref)
        keep_ref[...] = dw_ref[0]
        send_ref[...] = dw_ref[1]

    sums = (plan.tiles, plan.ranks, plan.piece, c)
    return pl.pallas_call(
        kernel,
        in_specs=[SMEM] + [VMEM] * 6,
        out_specs=[VMEM] * 3,
        out_shape=[jax.ShapeDtypeStruct(v, BF) for v in (padded(c), sums, sums)],
        scratch_shapes=[
            edge_sums(c),
            pltpu.VMEM(pair_shape(c), BF),
            pltpu.VMEM(grad_pairs(c), BF),
            pltpu.VMEM((2,) + sums, BF),
        ],
        compiler_params=params(),
        cost_estimate=cost(0, 0),
        name="hidden_back",
    )(ids, gp, w, u, slope, xp, after)


def add_up(parts):
    acc = parts[0].astype(F32)
    for part in parts[1:]:
        acc = acc + part.astype(F32)
    return acc.astype(BF)


def tile_sums(plan, parts, below_last=None, after=()):
    tiles, ranks = plan.tiles, plan.ranks
    rows = parts[0].shape[1]
    extra = [] if below_last is None else [below_last]
    shapes = [rows] * (ranks - 1) + [rows + sum(v.shape[0] for v in extra)]
    inputs = [*parts, *extra, *after]

    def kernel(*refs):
        results = refs[len(inputs) :]
        for r in range(ranks):
            results[r][0:rows] = add_up([ref[r] for ref in refs[:tiles]])
        if extra:
            results[-1][rows:] = refs[tiles][...]

    return pl.pallas_call(
        kernel,
        in_specs=[VMEM] * len(inputs),
        out_specs=[VMEM] * ranks,
        out_shape=[jax.ShapeDtypeStruct((v, plan.c), BF) for v in shapes],
        compiler_params=params(),
        cost_estimate=cost(0, 0),
        name="tile_sums",
    )(*inputs)


def rank_sums(plan, early, late, last):
    piece = plan.piece
    count = len(early)
    inputs = [*early, *late, last]

    def kernel(*refs):
        rows_ref = refs[len(inputs) - 1]
        to = refs[-1]
        to[0:piece] = add_up([ref[...] for ref in refs[:count]] + [rows_ref[0:piece]])
        to[piece:] = add_up([ref[...] for ref in refs[count:-2]] + [rows_ref[piece:]])

    return pl.pallas_call(
        kernel,
        in_specs=[VMEM] * len(inputs),
        out_specs=VMEM,
        out_shape=jax.ShapeDtypeStruct((plan.chunk, plan.c), BF),
        compiler_params=params(),
        cost_estimate=cost(0, 0),
        name="rank_sums",
    )(*inputs)


def inputs_back_kernel(gp_ref, w_ref, u_ref, ws_ref, go_ref, out_hbm, out_ref, v_ref, sem):
    c = w_ref.shape[1]
    stores = []
    for face in range(0, FACES, GROUP):
        faces = slice(face, face + GROUP)
        pair_rows(gp_ref, v_ref, face, GROUP)
        skip = dot_back(by_rows(go_ref, face, GROUP, 0, 0), ws_ref[...])
        skip = skip.reshape(FS, GROUP, FS, ROLL, c)
        for i, grad in enumerate(conv(v_ref, w_ref, u_ref, face, GROUP, back=True)):
            out_ref[faces, i] = grad + skip[i]
        part = pl.ds(face, GROUP)
        copy = pltpu.make_async_copy(out_ref.at[part], out_hbm.at[part], sem.at[face // GROUP])
        copy.start()
        stores.append(copy)
    for store in stores:
        store.wait()


def inputs_back(gp, w, u, ws, go):
    c = w.shape[1]
    return pl.pallas_call(
        inputs_back_kernel,
        in_specs=[VMEM] * 5,
        out_specs=HBM,
        out_shape=field(c, F32),
        scratch_shapes=[
            pltpu.VMEM(field(c).shape, F32),
            pltpu.VMEM(pair_shape(c), BF),
            pltpu.SemaphoreType.DMA((FACES // GROUP,)),
        ],
        compiler_params=params(),
        cost_estimate=cost(0, 0),
        name="inputs_back",
    )(gp, w, u, ws, go)


def adamw(weight, moment, square, grad, rate):
    moment_new = 0.9 * moment + 0.1 * grad
    square_new = 0.999 * square + 0.001 * grad * grad
    fix_one = 1.0 - 0.9**STEP_COUNT
    fix_two = 1.0 - 0.999**STEP_COUNT
    weight_new = weight - rate * (
        moment_new / fix_one / (jnp.sqrt(square_new / fix_two) + 1e-08) + 0.01 * weight
    )
    return (weight_new, moment_new, square_new)


UPDATE_STEPS = 4


def update(plan, ids, grads, sets, far, old=()):
    c, tiles = plan.c, plan.tiles

    def kernel(ids_ref, grads_ref, *refs):
        state = refs[:9]
        new, done_refs = refs[9 + len(old) : 18 + len(old)], refs[18 + len(old) : 27 + len(old)]
        sum_ref, sem = refs[27 + len(old) :]
        core, tile = ids_ref[0], ids_ref[1]
        side = 1 - core if far else core
        at = 0
        stores = []
        for n in range(3):
            piece = plan.skip_piece if n == 2 else plan.piece
            rows = tiles * piece
            for d in range(tiles):
                part = grads_ref[d, at : at + piece].astype(F32)
                if piece % 8:
                    for t in range(tiles):

                        def put(part=part, t=t, piece=piece):
                            sum_ref[t * piece : (t + 1) * piece] = part

                        pl.when(tile ^ d == t)(put)
                else:
                    sum_ref[pl.ds(pl.multiple_of((tile ^ d) * piece, 8), piece)] = part
            at += piece
            rate = (2 * rows * plan.ranks) ** (-0.5)
            step = rows // UPDATE_STEPS if rows % (8 * UPDATE_STEPS) == 0 else rows
            for row in range(0, rows, step):
                here = pl.ds(pl.multiple_of(side * rows + row, 8), step)
                done = adamw(*(state[3 * n + k][here] for k in range(3)), sum_ref[row : row + step], rate)
                for k in range(3 * n, 3 * n + 3):
                    done_refs[k][row : row + step] = done[k - 3 * n]
                    source = done_refs[k].at[pl.ds(row, step)]
                    number = UPDATE_STEPS * k + row // step
                    stores.append(pltpu.make_async_copy(source, new[k].at[here], sem.at[number]))
                    stores[-1].start()
        for store in stores:
            store.wait()

    shapes = [v.shape for v in sets]
    return pl.pallas_call(
        kernel,
        in_specs=[SMEM] + [VMEM] * 10 + [HBM] * len(old),
        out_specs=[HBM] * 9,
        out_shape=[jax.ShapeDtypeStruct(v, F32) for v in shapes],
        scratch_shapes=[
            *(pltpu.VMEM((v[0] // 2, c), F32) for v in shapes),
            pltpu.VMEM((plan.shard // 2, c), F32),
            pltpu.SemaphoreType.DMA((9 * UPDATE_STEPS,)),
        ],
        input_output_aliases={11 + k: k for k in range(len(old))},
        compiler_params=params(),
        cost_estimate=cost(2, 9),
        name="update",
    )(ids, grads, *sets, *old)


def send(v, axis, size, step):
    return lax.ppermute(v, axis, [(i, i ^ step) for i in range(size)])


def total(*parts):
    acc = parts[0].astype(F32)
    for part in parts[1:]:
        acc = acc + part.astype(F32)
    return acc.astype(BF)


def make_body(sizes):
    tiles, ranks = sizes["tile"], sizes["fsdp"]

    def to_core(v):
        return send(v, "core", 2, 1)

    def to_tile(v, d):
        return send(v, "tile", tiles, d)

    def to_rank(v, d):
        return send(v, "fsdp", ranks, d)

    def per_device(
        inputs,
        cotangent,
        lengths,
        face_table,
        w_first,
        w_second,
        w_skip,
        mom_first,
        sq_first,
        mom_second,
        sq_second,
        mom_skip,
        sq_skip,
    ):
        plan = Plan(sizes, inputs.shape[-1])
        x = jnp.transpose(inputs[0], (1, 2, 3, 0, 4))
        cot = jnp.transpose(cotangent[0], (1, 2, 3, 0, 4))
        places = jnp.stack([lax.axis_index(n) for n in ("core", "tile", "fsdp")]).astype(jnp.int32)
        weights = w_first, w_second, w_skip
        parts = (plan.sent[0], sum(plan.sent))
        some, sent = pack(plan, places, weights, plan.sent, plan.split, parts)
        near = [to_rank(some if d in plan.direct else sent, d) for d in range(1, ranks)]
        near = [below(near)]
        near_half, after = [], near[:]
        if plan.split:
            near += [to_tile(near[0], e) for e in range(1, tiles)]
            (half,) = pack(plan, places, weights[1:], plan.halves[1:], False, (sum(plan.halves[1:]),))
            near_half = [to_rank(half, d) for d in plan.direct]
            after.append(half)
        ids = jnp.concatenate([places, lengths, face_table.T.reshape(-1)])
        xp, go, dws, low1, low2, low3 = enter(plan, ids, x, cot, weights, after)
        xp, near, near_half = lax.optimization_barrier((xp, near, near_half))
        far = [to_core(v) for v in near]
        far_half = [to_core(v) for v in near_half]
        hp, slope, w1, u1 = first(plan, ids, xp, low1, near, far)
        hp, far_half = lax.optimization_barrier((hp, far_half))
        output, gp, w2, u2, ws, keep2, away2 = second(
            plan, ids, hp, xp, go, dws, low2, low3, near, far, near_half, far_half
        )
        came2 = to_core(away2)
        parts2 = [total(keep2[d], came2[d]) for d in range(tiles)]
        op, keep1, away1 = hidden_back(plan, ids, gp, w2, u2, slope, xp, parts2[0])
        late = [parts2[0]] + [to_tile(parts2[d], d) for d in range(1, tiles)]
        late, away1 = lax.optimization_barrier((late, away1))
        came1 = to_core(away1)
        late = tile_sums(plan, late)
        parts1 = [total(keep1[d], came1[d]) for d in range(tiles)]
        op, parts1, late = lax.optimization_barrier((op, parts1, late))
        early = [parts1[0]] + [to_tile(parts1[d], d) for d in range(1, tiles)]
        late, late_last = late[:-1], late[-1]
        late = [late[0]] + [to_rank(v, d) for d, v in enumerate(late) if d]
        grad_inputs = inputs_back(op, w1, u1, ws, go)
        early, late, grad_inputs = lax.optimization_barrier((early, late, grad_inputs))
        early = tile_sums(plan, early, late_last, late[1:])
        early = [early[0]] + [to_rank(v, d) for d, v in enumerate(early) if d]
        mine = rank_sums(plan, early[:-1], late, early[-1])
        near = jnp.stack([mine] + [to_tile(mine, d) for d in range(1, tiles)])
        far = to_core(near)
        sets = (
            w_first,
            mom_first,
            sq_first,
            w_second,
            mom_second,
            sq_second,
            w_skip,
            mom_skip,
            sq_skip,
        )
        news = update(plan, ids, near, sets, False)
        news = update(plan, ids, far, sets, True, news)
        output = jnp.transpose(output, (3, 0, 1, 2, 4))[None]
        grad_inputs = jnp.transpose(grad_inputs, (3, 0, 1, 2, 4))[None]
        return (output, grad_inputs, *news)

    return per_device


def solution(mesh):
    pairs = mesh.shape["dp"] // 2
    ranks = mesh.shape["fsdp"]
    fine = Mesh(mesh.devices.reshape(pairs, 2, ranks), ("tile", "core", "fsdp"))
    sizes = {"tile": pairs, "core": 2, "fsdp": ranks}
    every = ("tile", "core", "fsdp")
    fields = P(every, None, None, None, None, None)
    rows = P("fsdp", None)
    return jax.shard_map(
        make_body(sizes),
        mesh=fine,
        in_specs=(fields, fields, P(every), P()) + (rows,) * 9,
        out_specs=(fields, fields) + (rows,) * 9,
        check_vma=False,
    )
```

```python
import functools

import jax
import jax.numpy as jnp
from jax import lax
from jax.experimental import pallas as pl
from jax.experimental.pallas import tpu as pltpu
from jax.sharding import Mesh
from jax.sharding import PartitionSpec as P

STEP_COUNT = 10
BF = jnp.bfloat16
F32 = jnp.float32
FS = 6
ROLL = 8
FACES = 12
GELU_K = 0.7978845608028654
GELU_C = 0.044715
VMEM_LIMIT = 30 * 2**20
GROUP = 2


ANY = pl.BlockSpec(memory_space=pl.ANY)
HBM = pl.BlockSpec(memory_space=pltpu.HBM)
VMEM = pl.BlockSpec(memory_space=pltpu.VMEM)
SMEM = pl.BlockSpec(memory_space=pltpu.SMEM)


def field(c, dtype=BF):
    return jax.ShapeDtypeStruct((FACES, FS, FS, ROLL, c), dtype)


def padded(c):
    return (FACES, FS + 2, FS + 2, ROLL, c)


def inner(ref):
    return ref.at[:, 1 : FS + 1, 1 : FS + 1]


def in_hbm(v):
    return pltpu.with_memory_space_constraint(v, pltpu.HBM)


def params():
    return pltpu.CompilerParams(vmem_limit_bytes=VMEM_LIMIT)


def cost(gflop, mbyte):
    return pl.CostEstimate(flops=int(gflop * 1e9), bytes_accessed=int(mbyte * 1e6), transcendentals=0)


def gelu_both(v):
    a = (GELU_K * GELU_C) * (v * v) + GELU_K
    half = 0.5 * jnp.tanh(v * a) + 0.5
    value = v * half
    return value, half + (value * (1.0 - half)) * (6.0 * a - 4.0 * GELU_K)


def pair_shape(c):
    return (4, FS // 2, FACES, FS + 2, ROLL, c)


def grad_pairs(c):
    return (4, FS // 2, FACES, FS, ROLL, c)


def pair_rows(p_ref, v_ref, face, count):
    for t in range(FS // 2):
        d0, d1, d2, d3 = (p_ref[face : face + count, 2 * t + q] for q in range(4))
        v_ref[0, t, face : face + count] = d0 - d2
        v_ref[1, t, face : face + count] = d1 + d2
        v_ref[2, t, face : face + count] = d2 - d1
        v_ref[3, t, face : face + count] = d1 - d3


def pair_weights(w_ref, u_ref):
    c = w_ref.shape[1]
    for b in range(3):
        g0, g1, g2 = (w_ref[(3 * a + b) * c : (3 * a + b + 1) * c].astype(F32) for a in range(3))
        outside, middle = 0.5 * (g0 + g2), 0.5 * g1
        u_ref[0, b] = (outside + middle).astype(BF)
        u_ref[1, b] = (outside - middle).astype(BF)


def dot_back(v, w):
    return lax.dot_general(v, w, (((1,), (1,)), ((), ())), preferred_element_type=F32)


def conv(v_ref, w_ref, u_ref, face, count, back=False):
    c = w_ref.shape[1]
    products = []
    for k in range(4):
        acc = None
        for b in range(3):
            v = v_ref[k, :, face : face + count, b : b + FS].reshape(-1, c)
            col = 2 - b if back else b
            if k in (0, 3):
                t = 3 * (2 if (k == 3) != back else 0) + col
                g = w_ref[t * c : (t + 1) * c]
            else:
                g = u_ref[k - 1, col]
            part = dot_back(v, g) if back else jnp.dot(v, g, preferred_element_type=F32)
            acc = part if acc is None else acc + part
        products.append(acc.reshape(FS // 2, count, FS, ROLL, c))
    m0, m1, m2, m3 = products
    even, odd = m0 + m1 + m2, m1 - m2 - m3
    return [(odd if i % 2 else even)[i // 2] for i in range(FS)]


def by_rows(ref, face, count, first_row, first_col):
    cols = slice(first_col, first_col + FS)
    rows = [ref[face : face + count, first_row + i, cols] for i in range(FS)]
    return jnp.stack(rows).reshape(-1, ref.shape[-1])


def outer(p, g):
    c = p.shape[-1]
    return lax.dot_general(
        p.reshape(-1, c), g.reshape(-1, c), (((0,), (0,)), ((), ())), preferred_element_type=F32
    )


def zero_corners(p_ref):
    zero = jnp.zeros((FACES, 1, 1, ROLL, p_ref.shape[-1]), p_ref.dtype)
    for i in (0, FS + 1):
        for j in (0, FS + 1):
            p_ref[:, i : i + 1, j : j + 1] = zero


def neighbour(ids_ref, side, face):
    return ids_ref[4 + side * FACES + face]


def fill_halo(ids_ref, p_ref):
    for face in range(FACES):
        p_ref[face, 0, 1 : FS + 1] = p_ref[neighbour(ids_ref, 0, face), FS, 1 : FS + 1]
        p_ref[face, 1 : FS + 1, FS + 1] = p_ref[neighbour(ids_ref, 1, face), 1 : FS + 1, 1]
        p_ref[face, FS + 1, 1 : FS + 1] = p_ref[neighbour(ids_ref, 2, face), 1, 1 : FS + 1]
        p_ref[face, 1 : FS + 1, 0] = p_ref[neighbour(ids_ref, 3, face), 1 : FS + 1, FS]
    zero_corners(p_ref)


def add_edges(e_ref, ids_ref, face, p_ref):
    rows = cols = slice(1, FS + 1)
    edges = (p_ref[face, 1, cols], p_ref[face, rows, FS], p_ref[face, FS, cols], p_ref[face, rows, 1])
    for side, part in enumerate(edges):
        to = neighbour(ids_ref, side, face)
        e_ref[to, side] = e_ref[to, side] + part


def fill_halo_back(e_ref, p_ref):
    for face in range(FACES):
        p_ref[face, FS + 1, 1 : FS + 1] = e_ref[face, 0].astype(p_ref.dtype)
        p_ref[face, 1 : FS + 1, 0] = e_ref[face, 1].astype(p_ref.dtype)
        p_ref[face, 0, 1 : FS + 1] = e_ref[face, 2].astype(p_ref.dtype)
        p_ref[face, 1 : FS + 1, FS + 1] = e_ref[face, 3].astype(p_ref.dtype)
    zero_corners(p_ref)


def edge_sums(c):
    return pltpu.VMEM((FACES, 4, FS, ROLL, c), BF)


class Plan:
    def __init__(self, sizes, channels):
        self.tiles, self.ranks = sizes["tile"], sizes["fsdp"]
        self.c = channels
        self.conv = 9 * channels
        self.shard = self.conv // self.ranks
        self.skip_shard = channels // self.ranks
        self.piece = self.shard // (2 * self.tiles)
        self.skip_piece = self.skip_shard // (2 * self.tiles)
        self.late = self.piece + self.skip_piece
        self.chunk = self.piece + self.late
        self.split = self.piece % 8 == 0 and self.skip_piece % 8 == 0
        self.halves = self.shard // 2, self.shard // 2, self.skip_shard // 2
        self.sent = self.halves
        self.direct = ()
        if self.split:
            self.sent = self.piece, self.piece, self.skip_piece
            self.direct = tuple(d for d in (1, 2) if d < self.ranks - 1)
        self.start = {}
        rows = 0
        for d in range(1, self.ranks):
            self.start[d] = rows
            rows += self.sent[0] if d in self.direct else sum(self.sent)


def place_rows(plan, ids_ref, dst_ref, value, first_row, piece, offset):
    core, tile, rank = ids_ref[0], ids_ref[1], ids_ref[2]
    end = first_row + value.shape[0]
    row = first_row
    while row < end:
        number = row // piece
        stop = min(end, (number + 1) * piece)
        to_tile = number % plan.tiles
        to_core = number // plan.tiles % 2
        to_rank = number // (2 * plan.tiles)
        at = offset + row - number * piece
        dst_ref[
            to_core ^ core,
            to_tile ^ tile,
            to_rank ^ rank,
            at : at + stop - row,
        ] = value[row - first_row : stop - first_row]
        row = stop


def weight_grad(plan, ids_ref, v_ref, g_ref, z_ref, dst_ref):
    c = plan.c
    halves = range(FS // 2)
    cols = slice(1, FS + 1)
    for t in halves:
        y0, y1 = g_ref[:, 2 * t + 1, cols], g_ref[:, 2 * t + 2, cols]
        z_ref[1, t] = (y0 + y1) * 0.5
        z_ref[2, t] = (y0 - y1) * 0.5
    for b in range(3):
        y0, y1 = (jnp.stack([g_ref[:, 2 * t + q, cols] for t in halves]) for q in (1, 2))
        sides = (y0, z_ref[1], z_ref[2], y1)
        m0, m1, m2, m3 = (outer(v_ref[k, :, :, b : b + FS], sides[k]) for k in range(4))
        both = m1 + m2
        for a, part in enumerate((m0 + both, m1 - m2, both - m3)):
            place_rows(plan, ids_ref, dst_ref, part.astype(BF), (3 * a + b) * c, plan.piece, 0)


def pack(plan, ids, weights, rows, shared, parts):
    c = plan.c
    count = len(weights)

    def kernel(ids_ref, *refs):
        rows_ref, sem = refs[count + len(parts) :]
        loads = []
        at = 0
        for k in range(count):
            hbm = refs[k]
            start = ids_ref[0] * (hbm.shape[0] // 2)
            if shared:
                start = start + ids_ref[1] * rows[k]
            source = hbm.at[pl.ds(pl.multiple_of(start, 8), rows[k])]
            loads.append(pltpu.make_async_copy(source, rows_ref.at[pl.ds(at, rows[k])], sem.at[k]))
            at += rows[k]
        for load in loads:
            load.start()
        for load in loads:
            load.wait()
        for k, part in enumerate(parts):
            refs[count + k][...] = rows_ref[0:part].astype(BF)

    return pl.pallas_call(
        kernel,
        in_specs=[SMEM] + [HBM] * count,
        out_specs=[VMEM] * len(parts),
        out_shape=[jax.ShapeDtypeStruct((v, c), BF) for v in parts],
        scratch_shapes=[pltpu.VMEM((sum(rows), c), F32), pltpu.SemaphoreType.DMA((count,))],
        compiler_params=params(),
        cost_estimate=cost(0, 0),
        name="pack",
    )(ids, *(in_hbm(v) for v in weights))


def below(arrays):
    rows = [v.shape[0] for v in arrays]

    def kernel(*refs):
        at = 0
        for ref, count in zip(refs, rows):
            refs[-1][at : at + count] = ref[...]
            at += count

    return pl.pallas_call(
        kernel,
        in_specs=[VMEM] * len(rows),
        out_specs=VMEM,
        out_shape=jax.ShapeDtypeStruct((sum(rows), arrays[0].shape[1]), BF),
        compiler_params=params(),
        cost_estimate=cost(0, 0),
        name="below",
    )(*arrays)


def join_rows(plan, ids_ref, low_ref, pieces, w_ref, rows):
    rank = ids_ref[2]
    w_ref[pl.ds(pl.multiple_of(rank * rows, 8), rows)] = low_ref[...]
    for ref, index, d, row in pieces:
        start = (rank ^ d) * rows + row
        part = ref[index]
        w_ref[pl.ds(pl.multiple_of(start, 8), part.shape[0])] = part


def received(plan, ids_ref, near_refs, far_refs, weight):
    core, tile = ids_ref[0], ids_ref[1]
    rows = plan.sent[weight]
    pieces = []
    for side, group in ((core, near_refs), (1 - core, far_refs)):
        for e, ref in enumerate(group):
            row = side * plan.halves[weight]
            if plan.split:
                row = row + (tile ^ e) * rows
            for d in range(1, plan.ranks):
                if weight == 0 or d not in plan.direct:
                    at = plan.start[d] + sum(plan.sent[:weight])
                    pieces.append((ref, pl.ds(at, rows), d, row))
    return pieces


def received_directly(plan, ids_ref, near_refs, far_refs, at, weight):
    core = ids_ref[0]
    rows = plan.halves[weight]
    pieces = []
    for side, group in ((core, near_refs), (1 - core, far_refs)):
        for ref, d in zip(group, plan.direct):
            pieces.append((ref, pl.ds(at, rows), d, side * rows))
    return pieces


def enter(plan, ids, x, cot, weights, after):
    c = plan.c

    def kernel(ids_ref, x_hbm, cot_hbm, *refs):
        refs = refs[:3] + refs[3 + len(after) :]
        weights_hbm, xp_ref, go_ref, dw_ref = refs[:3], *refs[3:6]
        low_refs, cot_ref, weight_refs, sem = refs[6:9], refs[9], refs[10:13], refs[13]
        load_x = pltpu.make_async_copy(x_hbm, inner(xp_ref), sem.at[FACES])
        load_x.start()
        loads = []
        for face in range(FACES):
            loads.append(pltpu.make_async_copy(cot_hbm.at[face], cot_ref.at[face], sem.at[face]))
            loads[-1].start()
        low_loads = []
        for k in range(3):
            low_loads.append(
                pltpu.make_async_copy(weights_hbm[k], weight_refs[k], sem.at[FACES + 1 + k])
            )
            low_loads[-1].start()
        live = lax.broadcasted_iota(jnp.int32, (FS, FS, ROLL, c), 2) < ids_ref[3]
        for face in range(FACES):
            loads[face].wait()
            go_ref[face] = jnp.where(live, cot_ref[face].astype(F32), 0.0).astype(BF)
        load_x.wait()
        fill_halo(ids_ref, xp_ref)
        dw_ref[...] = outer(xp_ref[:, 1 : FS + 1, 1 : FS + 1], go_ref[...]).astype(dw_ref.dtype)
        for k in range(3):
            low_loads[k].wait()
            low_refs[k][...] = weight_refs[k][...].astype(BF)

    return pl.pallas_call(
        kernel,
        in_specs=[SMEM] + [HBM] * 5 + [VMEM] * len(after),
        out_specs=[VMEM] * 6,
        out_shape=[
            jax.ShapeDtypeStruct(padded(c), BF),
            field(c),
            jax.ShapeDtypeStruct((c, c), BF),
            *(jax.ShapeDtypeStruct(v.shape, BF) for v in weights),
        ],
        scratch_shapes=[
            pltpu.VMEM(field(c).shape, BF),
            *(pltpu.VMEM(v.shape, F32) for v in weights),
            pltpu.SemaphoreType.DMA((FACES + 4,)),
        ],
        compiler_params=params(),
        cost_estimate=cost(0, 0),
        name="enter",
    )(ids, in_hbm(x), in_hbm(cot), *(in_hbm(v) for v in weights), *after)


def first(plan, ids, xp, low, near, far):
    c = plan.c
    count = len(near)

    def kernel(ids_ref, xp_ref, low_ref, *refs):
        near_refs, far_refs = refs[:count], refs[count : 2 * count]
        hp_ref, slope_ref, w_ref, u_ref, v_ref = refs[2 * count :]
        pieces = received(plan, ids_ref, near_refs, far_refs, 0)
        join_rows(plan, ids_ref, low_ref, pieces, w_ref, plan.shard)
        pair_weights(w_ref, u_ref)
        for face in range(0, FACES, GROUP):
            faces = slice(face, face + GROUP)
            pair_rows(xp_ref, v_ref, face, GROUP)
            for i, pre in enumerate(conv(v_ref, w_ref, u_ref, face, GROUP)):
                hidden, slope = gelu_both(pre)
                hp_ref[faces, i + 1, 1 : FS + 1] = hidden.astype(BF)
                slope_ref[faces, i] = slope.astype(BF)
        fill_halo(ids_ref, hp_ref)

    return pl.pallas_call(
        kernel,
        in_specs=[SMEM] + [VMEM] * (2 + 2 * count),
        out_specs=[VMEM] * 4,
        out_shape=[
            jax.ShapeDtypeStruct(padded(c), BF),
            field(c),
            jax.ShapeDtypeStruct((plan.conv, c), BF),
            jax.ShapeDtypeStruct((2, 3, c, c), BF),
        ],
        scratch_shapes=[pltpu.VMEM(pair_shape(c), BF)],
        compiler_params=params(),
        cost_estimate=cost(0, 0),
        name="first",
    )(ids, xp, low, *near, *far)


def second(plan, ids, hp, xp, go, dws, low, low_skip, near, far, near_half, far_half):
    c = plan.c
    count = len(near)
    halves = len(near_half)

    def kernel(ids_ref, hp_ref, xp_ref, go_ref, dws_ref, low_ref, lows_ref, *refs):
        groups = refs[:count], refs[count : 2 * count]
        refs = refs[2 * count :]
        direct = refs[:halves], refs[halves : 2 * halves]
        refs = refs[2 * halves :]
        out_hbm, gp_ref, w_ref, u_ref, ws_ref, keep_ref, send_ref = refs[:7]
        out_ref, e_ref, dw_ref, v_ref, z_ref, sem_out = refs[7:]
        pieces = received(plan, ids_ref, *groups, 1)
        pieces += received_directly(plan, ids_ref, *direct, 0, 1)
        join_rows(plan, ids_ref, low_ref, pieces, w_ref, plan.shard)
        pieces = received(plan, ids_ref, *groups, 2)
        pieces += received_directly(plan, ids_ref, *direct, plan.halves[1], 2)
        join_rows(plan, ids_ref, lows_ref, pieces, ws_ref, plan.skip_shard)
        e_ref[...] = jnp.zeros_like(e_ref)
        place_rows(plan, ids_ref, dw_ref, dws_ref[...], 0, plan.skip_piece, plan.piece)
        pair_weights(w_ref, u_ref)
        for face in range(0, FACES, GROUP):
            faces = slice(face, face + GROUP)
            pair_rows(hp_ref, v_ref, face, GROUP)
            skip = jnp.dot(
                by_rows(xp_ref, face, GROUP, 1, 1), ws_ref[...], preferred_element_type=F32
            ).reshape(FS, GROUP, FS, ROLL, c)
            for i, pre in enumerate(conv(v_ref, w_ref, u_ref, face, GROUP)):
                value, slope = gelu_both(pre)
                out_ref[faces, i] = (value + skip[i]).astype(BF)
                low_grad = (go_ref[faces, i].astype(F32) * slope).astype(BF)
                gp_ref[faces, i + 1, 1 : FS + 1] = low_grad
            for one in range(face, face + GROUP):
                add_edges(e_ref, ids_ref, one, gp_ref)
        store = pltpu.make_async_copy(out_ref, out_hbm, sem_out)
        store.start()
        weight_grad(plan, ids_ref, v_ref, gp_ref, z_ref, dw_ref)
        keep_ref[...] = dw_ref[0]
        send_ref[...] = dw_ref[1]
        fill_halo_back(e_ref, gp_ref)
        store.wait()

    sums = jax.ShapeDtypeStruct((plan.tiles, plan.ranks, plan.late, c), BF)
    return pl.pallas_call(
        kernel,
        in_specs=[SMEM] + [VMEM] * (6 + 2 * count + 2 * halves),
        out_specs=[HBM] + [VMEM] * 6,
        out_shape=[
            field(c),
            jax.ShapeDtypeStruct(padded(c), BF),
            jax.ShapeDtypeStruct((plan.conv, c), BF),
            jax.ShapeDtypeStruct((2, 3, c, c), BF),
            jax.ShapeDtypeStruct((c, c), BF),
            sums,
            sums,
        ],
        scratch_shapes=[
            pltpu.VMEM(field(c).shape, BF),
            edge_sums(c),
            pltpu.VMEM((2,) + sums.shape, BF),
            pltpu.VMEM(pair_shape(c), BF),
            pltpu.VMEM(grad_pairs(c), BF),
            pltpu.SemaphoreType.DMA,
        ],
        compiler_params=params(),
        cost_estimate=cost(9, 16),
        name="second",
    )(ids, hp, xp, go, dws, low, low_skip, *near, *far, *near_half, *far_half)


def hidden_back(plan, ids, gp, w, u, slope, xp, after):
    c = plan.c

    def kernel(ids_ref, gp_ref, w_ref, u_ref, slope_ref, xp_ref, _, op_ref, keep_ref, send_ref, *refs):
        e_ref, v_ref, z_ref, dw_ref = refs
        e_ref[...] = jnp.zeros_like(e_ref)
        for face in range(0, FACES, GROUP):
            faces = slice(face, face + GROUP)
            pair_rows(gp_ref, v_ref, face, GROUP)
            for i, grad in enumerate(conv(v_ref, w_ref, u_ref, face, GROUP, back=True)):
                low_grad = (grad * slope_ref[faces, i].astype(F32)).astype(BF)
                op_ref[faces, i + 1, 1 : FS + 1] = low_grad
            for one in range(face, face + GROUP):
                add_edges(e_ref, ids_ref, one, op_ref)
        pair_rows(xp_ref, v_ref, 0, FACES)
        weight_grad(plan, ids_ref, v_ref, op_ref, z_ref, dw_ref)
        fill_halo_back(e_ref, op_ref)
        keep_ref[...] = dw_ref[0]
        send_ref[...] = dw_ref[1]

    sums = (plan.tiles, plan.ranks, plan.piece, c)
    return pl.pallas_call(
        kernel,
        in_specs=[SMEM] + [VMEM] * 6,
        out_specs=[VMEM] * 3,
        out_shape=[jax.ShapeDtypeStruct(v, BF) for v in (padded(c), sums, sums)],
        scratch_shapes=[
            edge_sums(c),
            pltpu.VMEM(pair_shape(c), BF),
            pltpu.VMEM(grad_pairs(c), BF),
            pltpu.VMEM((2,) + sums, BF),
        ],
        compiler_params=params(),
        cost_estimate=cost(0, 0),
        name="hidden_back",
    )(ids, gp, w, u, slope, xp, after)


def add_up(parts):
    acc = parts[0].astype(F32)
    for part in parts[1:]:
        acc = acc + part.astype(F32)
    return acc.astype(BF)


def tile_sums(plan, parts, below_last=None, after=()):
    tiles, ranks = plan.tiles, plan.ranks
    rows = parts[0].shape[1]
    extra = [] if below_last is None else [below_last]
    shapes = [rows] * (ranks - 1) + [rows + sum(v.shape[0] for v in extra)]
    inputs = [*parts, *extra, *after]

    def kernel(*refs):
        results = refs[len(inputs) :]
        for r in range(ranks):
            results[r][0:rows] = add_up([ref[r] for ref in refs[:tiles]])
        if extra:
            results[-1][rows:] = refs[tiles][...]

    return pl.pallas_call(
        kernel,
        in_specs=[VMEM] * len(inputs),
        out_specs=[VMEM] * ranks,
        out_shape=[jax.ShapeDtypeStruct((v, plan.c), BF) for v in shapes],
        compiler_params=params(),
        cost_estimate=cost(0, 0),
        name="tile_sums",
    )(*inputs)


def rank_sums(plan, early, late, last):
    piece = plan.piece
    count = len(early)
    inputs = [*early, *late, last]

    def kernel(*refs):
        rows_ref = refs[len(inputs) - 1]
        to = refs[-1]
        to[0:piece] = add_up([ref[...] for ref in refs[:count]] + [rows_ref[0:piece]])
        to[piece:] = add_up([ref[...] for ref in refs[count:-2]] + [rows_ref[piece:]])

    return pl.pallas_call(
        kernel,
        in_specs=[VMEM] * len(inputs),
        out_specs=VMEM,
        out_shape=jax.ShapeDtypeStruct((plan.chunk, plan.c), BF),
        compiler_params=params(),
        cost_estimate=cost(0, 0),
        name="rank_sums",
    )(*inputs)


def inputs_back_kernel(gp_ref, w_ref, u_ref, ws_ref, go_ref, out_hbm, out_ref, v_ref, sem):
    c = w_ref.shape[1]
    stores = []
    for face in range(0, FACES, GROUP):
        faces = slice(face, face + GROUP)
        pair_rows(gp_ref, v_ref, face, GROUP)
        skip = dot_back(by_rows(go_ref, face, GROUP, 0, 0), ws_ref[...])
        skip = skip.reshape(FS, GROUP, FS, ROLL, c)
        for i, grad in enumerate(conv(v_ref, w_ref, u_ref, face, GROUP, back=True)):
            out_ref[faces, i] = grad + skip[i]
        part = pl.ds(face, GROUP)
        copy = pltpu.make_async_copy(out_ref.at[part], out_hbm.at[part], sem.at[face // GROUP])
        copy.start()
        stores.append(copy)
    for store in stores:
        store.wait()


def inputs_back(gp, w, u, ws, go):
    c = w.shape[1]
    return pl.pallas_call(
        inputs_back_kernel,
        in_specs=[VMEM] * 5,
        out_specs=HBM,
        out_shape=field(c, F32),
        scratch_shapes=[
            pltpu.VMEM(field(c).shape, F32),
            pltpu.VMEM(pair_shape(c), BF),
            pltpu.SemaphoreType.DMA((FACES // GROUP,)),
        ],
        compiler_params=params(),
        cost_estimate=cost(0, 0),
        name="inputs_back",
    )(gp, w, u, ws, go)


def adamw(weight, moment, square, grad, rate):
    moment_new = 0.9 * moment + 0.1 * grad
    square_new = 0.999 * square + 0.001 * grad * grad
    fix_one = 1.0 - 0.9**STEP_COUNT
    fix_two = 1.0 - 0.999**STEP_COUNT
    weight_new = weight - rate * (
        moment_new / fix_one / (jnp.sqrt(square_new / fix_two) + 1e-08) + 0.01 * weight
    )
    return (weight_new, moment_new, square_new)


UPDATE_STEPS = 4


def update(plan, ids, grads, sets, far, old=()):
    c, tiles = plan.c, plan.tiles

    def kernel(ids_ref, grads_ref, *refs):
        state = refs[:9]
        new, done_refs = refs[9 + len(old) : 18 + len(old)], refs[18 + len(old) : 27 + len(old)]
        sum_ref, sem = refs[27 + len(old) :]
        core, tile = ids_ref[0], ids_ref[1]
        side = 1 - core if far else core
        at = 0
        stores = []
        for n in range(3):
            piece = plan.skip_piece if n == 2 else plan.piece
            rows = tiles * piece
            for d in range(tiles):
                part = grads_ref[d, at : at + piece].astype(F32)
                if piece % 8:
                    for t in range(tiles):

                        def put(part=part, t=t, piece=piece):
                            sum_ref[t * piece : (t + 1) * piece] = part

                        pl.when(tile ^ d == t)(put)
                else:
                    sum_ref[pl.ds(pl.multiple_of((tile ^ d) * piece, 8), piece)] = part
            at += piece
            rate = (2 * rows * plan.ranks) ** (-0.5)
            step = rows // UPDATE_STEPS if rows % (8 * UPDATE_STEPS) == 0 else rows
            for row in range(0, rows, step):
                here = pl.ds(pl.multiple_of(side * rows + row, 8), step)
                done = adamw(*(state[3 * n + k][here] for k in range(3)), sum_ref[row : row + step], rate)
                for k in range(3 * n, 3 * n + 3):
                    done_refs[k][row : row + step] = done[k - 3 * n]
                    source = done_refs[k].at[pl.ds(row, step)]
                    number = UPDATE_STEPS * k + row // step
                    stores.append(pltpu.make_async_copy(source, new[k].at[here], sem.at[number]))
                    stores[-1].start()
        for store in stores:
            store.wait()

    shapes = [v.shape for v in sets]
    return pl.pallas_call(
        kernel,
        in_specs=[SMEM] + [VMEM] * 10 + [HBM] * len(old),
        out_specs=[HBM] * 9,
        out_shape=[jax.ShapeDtypeStruct(v, F32) for v in shapes],
        scratch_shapes=[
            *(pltpu.VMEM((v[0] // 2, c), F32) for v in shapes),
            pltpu.VMEM((plan.shard // 2, c), F32),
            pltpu.SemaphoreType.DMA((9 * UPDATE_STEPS,)),
        ],
        input_output_aliases={11 + k: k for k in range(len(old))},
        compiler_params=params(),
        cost_estimate=cost(2, 9),
        name="update",
    )(ids, grads, *sets, *old)


def send(v, axis, size, step):
    return lax.ppermute(v, axis, [(i, i ^ step) for i in range(size)])


def total(*parts):
    acc = parts[0].astype(F32)
    for part in parts[1:]:
        acc = acc + part.astype(F32)
    return acc.astype(BF)


def make_body(sizes):
    tiles, ranks = sizes["tile"], sizes["fsdp"]

    def to_core(v):
        return send(v, "core", 2, 1)

    def to_tile(v, d):
        return send(v, "tile", tiles, d)

    def to_rank(v, d):
        return send(v, "fsdp", ranks, d)

    def per_device(
        inputs,
        cotangent,
        lengths,
        face_table,
        w_first,
        w_second,
        w_skip,
        mom_first,
        sq_first,
        mom_second,
        sq_second,
        mom_skip,
        sq_skip,
    ):
        plan = Plan(sizes, inputs.shape[-1])
        x = jnp.transpose(inputs[0], (1, 2, 3, 0, 4))
        cot = jnp.transpose(cotangent[0], (1, 2, 3, 0, 4))
        places = jnp.stack([lax.axis_index(n) for n in ("core", "tile", "fsdp")]).astype(jnp.int32)
        weights = w_first, w_second, w_skip
        parts = (plan.sent[0], sum(plan.sent))
        some, sent = pack(plan, places, weights, plan.sent, plan.split, parts)
        near = [to_rank(some if d in plan.direct else sent, d) for d in range(1, ranks)]
        near = [below(near)]
        near_half, after = [], near[:]
        if plan.split:
            near += [to_tile(near[0], e) for e in range(1, tiles)]
            (half,) = pack(plan, places, weights[1:], plan.halves[1:], False, (sum(plan.halves[1:]),))
            near_half = [to_rank(half, d) for d in plan.direct]
            after.append(half)
        ids = jnp.concatenate([places, lengths, face_table.T.reshape(-1)])
        xp, go, dws, low1, low2, low3 = enter(plan, ids, x, cot, weights, after)
        xp, near, near_half = lax.optimization_barrier((xp, near, near_half))
        far = [to_core(v) for v in near]
        far_half = [to_core(v) for v in near_half]
        hp, slope, w1, u1 = first(plan, ids, xp, low1, near, far)
        hp, far_half = lax.optimization_barrier((hp, far_half))
        output, gp, w2, u2, ws, keep2, away2 = second(
            plan, ids, hp, xp, go, dws, low2, low3, near, far, near_half, far_half
        )
        came2 = to_core(away2)
        parts2 = [total(keep2[d], came2[d]) for d in range(tiles)]
        op, keep1, away1 = hidden_back(plan, ids, gp, w2, u2, slope, xp, parts2[0])
        late = [parts2[0]] + [to_tile(parts2[d], d) for d in range(1, tiles)]
        late, away1 = lax.optimization_barrier((late, away1))
        came1 = to_core(away1)
        late = tile_sums(plan, late)
        parts1 = [total(keep1[d], came1[d]) for d in range(tiles)]
        op, parts1, late = lax.optimization_barrier((op, parts1, late))
        early = [parts1[0]] + [to_tile(parts1[d], d) for d in range(1, tiles)]
        late, late_last = late[:-1], late[-1]
        late = [late[0]] + [to_rank(v, d) for d, v in enumerate(late) if d]
        grad_inputs = inputs_back(op, w1, u1, ws, go)
        early, late, grad_inputs = lax.optimization_barrier((early, late, grad_inputs))
        early = tile_sums(plan, early, late_last, late[1:])
        early = [early[0]] + [to_rank(v, d) for d, v in enumerate(early) if d]
        mine = rank_sums(plan, early[:-1], late, early[-1])
        near = jnp.stack([mine] + [to_tile(mine, d) for d in range(1, tiles)])
        far = to_core(near)
        sets = (
            w_first,
            mom_first,
            sq_first,
            w_second,
            mom_second,
            sq_second,
            w_skip,
            mom_skip,
            sq_skip,
        )
        news = update(plan, ids, near, sets, False)
        news = update(plan, ids, far, sets, True, news)
        output = jnp.transpose(output, (3, 0, 1, 2, 4))[None]
        grad_inputs = jnp.transpose(grad_inputs, (3, 0, 1, 2, 4))[None]
        return (output, grad_inputs, *news)

    return per_device


def solution(mesh):
    pairs = mesh.shape["dp"] // 2
    ranks = mesh.shape["fsdp"]
    fine = Mesh(mesh.devices.reshape(pairs, 2, ranks), ("tile", "core", "fsdp"))
    sizes = {"tile": pairs, "core": 2, "fsdp": ranks}
    every = ("tile", "core", "fsdp")
    fields = P(every, None, None, None, None, None)
    rows = P("fsdp", None)
    return jax.shard_map(
        make_body(sizes),
        mesh=fine,
        in_specs=(fields, fields, P(every), P()) + (rows,) * 9,
        out_specs=(fields, fields) + (rows,) * 9,
        check_vma=False,
    )
```
